256 devices in a mesh: shot: 8 (over x_hi, y), box: 32 (over x_lo, z, core).
Axes of the slice: x: 4 (x_hi: 2, x_lo: 2; x = x_hi * 2 + x_lo), y: 4, z: 8, core: 2. Of those that a mesh axis runs over, the one named last changes fastest.
Arguments:
- u_prev: float32 [8, 8, 2048, 256], P('shot', None, 'box'), may hold values from -6 to 6
- u_now: float32 [8, 8, 2048, 256], P('shot', None, 'box'), may hold values from -6 to 6
- born_prev: float32 [8, 8, 2048, 256], P('shot', None, 'box'), may hold values from -6 to 6
- born_now: float32 [8, 8, 2048, 256], P('shot', None, 'box'), may hold values from -6 to 6
- adj_after: float32 [8, 8, 2048, 256], P('shot', None, 'box'), may hold values from -6 to 6
- adj_last: float32 [8, 8, 2048, 256], P('shot', None, 'box'), may hold values from -6 to 6
- velocity: float32 [8, 2048, 256], P('shot', 'box'), may hold values from 0.08 to 0.45
- wavelet: float32 [8, 8, 4], P('shot'), may hold values from -12 to 12
- sources: int32 [8, 8], P('shot'), may hold values from 0 to 524287
- receivers: int32 [8, 1024], P('shot', 'box'), may hold values from 0 to 524095, as said below
- observed: float32 [8, 8, 4, 1024], P('shot', None, None, 'box'), may hold values from -6 to 6
- first_tile: int32 [8], P('shot'), may hold values from 0 to 256
- reflectivity: float32 [40, 32, 2, 256], P(None, 'box'), may hold values from -6 to 6
Outputs:
- migrated: float32 [40, 32, 2, 256], P(None, 'box')
The draws below stay inside these ranges and needn't reach their ends.
Inputs may be any that keep to these rules, and one draw needn't show every extreme that they name: `receivers`: receiver r of every group lies in the grid columns r * 2 to (r + 1) * 2 - 1 of its box, at a depth cell under 256 // 4.
All inputs are finite; a program needn't handle non-finite values.
Results may differ from the reference program's by a relative error of at most 0.00011.
Values sent between devices are 32-bit elements; how exact they have to be, the bound alone decides.
A program may use at most 64 MiB of HBM per device.

```python
import math
import jax
import jax.numpy as jnp
from jax import lax

NS = 8
NZ = 256
TW = 2
STEPS = 4
GROUPS = 8
OWNERS = 32
ROUNDS = 40
NXB = 2048
NREC = 1024
N_BOX = 32


def draw_receivers(key, part):
    key_column, key_depth = jax.random.split(key)
    jitter = jax.random.randint(key_column, (GROUPS, NREC), 0, TW, dtype=jnp.int32)
    depth_cell = jax.random.randint(key_depth, (GROUPS, NREC), 0, NZ // 4, dtype=jnp.int32)
    jitter = jitter.at[:, 0].set(0).at[:, NREC - 1].set(TW - 1)
    depth_cell = depth_cell.at[:, 0].set(0).at[:, NREC - 1].set(NZ // 4 - 1)
    column = jnp.arange(NREC, dtype=jnp.int32)[None, :] * TW + jitter
    return column * NZ + depth_cell


def set_ends(drawn, stream_key, smallest, top_value):
    spot = [jax.random.randint(jax.random.fold_in(stream_key, axis), (), 0, length) for axis, length in enumerate(drawn.shape)]
    longest = drawn.shape.index(max(drawn.shape))
    beside = spot[:longest] + [(spot[longest] + 1) % drawn.shape[longest]] + spot[longest + 1:]
    return drawn.at[tuple(spot)].set(smallest).at[tuple(beside)].set(top_value)


def block_levels(own_key, dims, cuts, least, largest):
    loudness, own = 1.0, jax.random.fold_in(own_key, 6)
    for dim, blocks in cuts:
        draws = jnp.exp(jax.random.uniform(jax.random.fold_in(own, dim), (blocks,), jnp.float32, least / len(cuts), largest / len(cuts)))
        loudness = loudness * jnp.repeat(draws, dims[dim] // blocks).reshape([-1 if axis == dim else 1 for axis in range(len(dims))])
    return loudness


def noise(key, dims, spread, bound, shards=(), kind=jnp.bfloat16):
    array = spread * jax.random.normal(key, dims, jnp.float32)
    if shards:
        array = array * block_levels(key, dims, shards, -0.22, 0.18)
    return jnp.clip(array, -bound, bound).astype(kind)


def setup_inputs(seed: int = 0) -> dict:
    seeds = jax.random.split(jax.random.key(seed), 14)
    u_prev = noise(seeds[0], (GROUPS, NS, NXB, NZ), 1.0, 6.0, ((0, 8), (2, 32)), jnp.float32)
    u_now = noise(seeds[1], (GROUPS, NS, NXB, NZ), 1.0, 6.0, ((0, 8), (2, 32)), jnp.float32)
    born_prev = noise(seeds[2], (GROUPS, NS, NXB, NZ), 1.0, 6.0, ((0, 8), (2, 32)), jnp.float32)
    born_now = noise(seeds[3], (GROUPS, NS, NXB, NZ), 1.0, 6.0, ((0, 8), (2, 32)), jnp.float32)
    adj_after = noise(seeds[4], (GROUPS, NS, NXB, NZ), 1.0, 6.0, ((0, 8), (2, 32)), jnp.float32)
    adj_last = noise(seeds[5], (GROUPS, NS, NXB, NZ), 1.0, 6.0, ((0, 8), (2, 32)), jnp.float32)
    velocity = jnp.clip(jnp.exp(math.log(0.45) - 1.7272209 * jax.random.uniform(seeds[6], (GROUPS, NXB, NZ), jnp.float32) ** block_levels(seeds[6], (GROUPS, NXB, NZ), ((0, 8), (1, 32)), -0.2, 0.2)), 0.08, 0.45)
    wavelet = noise(seeds[7], (GROUPS, NS, STEPS), 3.0, 12.0, ((0, 8),), jnp.float32)
    sources = set_ends(jax.random.randint(seeds[8], (GROUPS, NS), 0, NXB * NZ), jax.random.fold_in(seeds[8], 1), 0, (NXB * NZ) - 1).astype(jnp.int32)
    receivers = draw_receivers(jax.random.fold_in(seeds[13], 71), 0)
    observed = noise(seeds[10], (GROUPS, NS, STEPS, NREC), 1.0, 6.0, ((0, 8), (3, 32)), jnp.float32)
    first_tile = set_ends(jax.random.randint(seeds[11], (GROUPS,), 0, (ROUNDS - N_BOX) * N_BOX + 1), jax.random.fold_in(seeds[11], 1), 0, (ROUNDS - N_BOX) * N_BOX).astype(jnp.int32)
    reflectivity = noise(seeds[12], (ROUNDS, OWNERS, TW, NZ), 1.0, 6.0, ((1, 32),), jnp.float32)
    return {"u_prev": u_prev, "u_now": u_now, "born_prev": born_prev, "born_now": born_now, "adj_after": adj_after, "adj_last": adj_last, "velocity": velocity, "wavelet": wavelet, "sources": sources, "receivers": receivers, "observed": observed, "first_tile": first_tile, "reflectivity": reflectivity}


damping = 1.0

def laplace(wavefield):
    padded = jnp.pad(wavefield, ((0, 0), (1, 1), (1, 1)))
    return padded[:, 2:, 1:-1] + padded[:, :-2, 1:-1] + padded[:, 1:-1, 2:] + padded[:, 1:-1, :-2] - 4.0 * wavefield

def add_sources(wavefield, cells, amount):
    flat = wavefield.reshape(wavefield.shape[0], -1)
    lanes = jnp.arange(wavefield.shape[0], dtype=jnp.int32)
    return flat.at[lanes, cells].add(amount).reshape(wavefield.shape)

def add_receivers(wavefield, cells, amount):
    flat = wavefield.reshape(wavefield.shape[0], -1)
    return flat.at[:, cells].add(amount).reshape(wavefield.shape)

def read_receivers(wavefield, cells):
    flat = wavefield.reshape(wavefield.shape[0], -1)
    return flat[:, cells]

def reference(u_prev, u_now, born_prev, born_now, adj_after, adj_last, velocity, wavelet, sources, receivers, observed, first_tile, reflectivity):
    image_flat = reflectivity.reshape(ROUNDS * OWNERS * TW, NZ)
    gradient = jnp.zeros_like(image_flat)
    illumination = jnp.zeros_like(image_flat)
    for group in range(GROUPS):
        speed = velocity[group]
        first_column = (first_tile[group] * TW).astype(jnp.int32)
        image_box = lax.dynamic_slice_in_dim(image_flat, first_column, NXB, 0)
        older_u, newer_u = (u_prev[group], u_now[group])
        older_b, newer_b = (born_prev[group], born_now[group])
        accelerations = []
        misfits = []
        for moment in range(STEPS):
            next_u = 2.0 * newer_u - older_u + speed * laplace(newer_u)
            next_u = add_sources(next_u, sources[group], wavelet[group, :, moment])
            second_diff = next_u - 2.0 * newer_u + older_u
            next_b = 2.0 * newer_b - older_b + speed * laplace(newer_b) + image_box * second_diff
            accelerations.append(second_diff)
            misfits.append(read_receivers(next_b, receivers[group]) - observed[group, :, moment, :])
            older_u, newer_u = (newer_u, next_u)
            older_b, newer_b = (newer_b, next_b)
        adjoint_old, adjoint_new = (adj_after[group], adj_last[group])
        grad_box = jnp.zeros((NXB, NZ), jnp.float32)
        illum_box = jnp.zeros((NXB, NZ), jnp.float32)
        for moment in reversed(range(STEPS)):
            adjoint_next = 2.0 * adjoint_new - adjoint_old + speed * laplace(adjoint_new)
            adjoint_next = add_receivers(adjoint_next, receivers[group], misfits[moment])
            grad_box = grad_box + lax.optimization_barrier(jnp.sum(adjoint_next * accelerations[moment], axis=0))
            illum_box = illum_box + lax.optimization_barrier(jnp.sum(accelerations[moment] * accelerations[moment], axis=0))
            adjoint_old, adjoint_new = (adjoint_new, adjoint_next)
        old_grad = lax.dynamic_slice_in_dim(gradient, first_column, NXB, 0)
        gradient = lax.dynamic_update_slice_in_dim(gradient, old_grad + grad_box, first_column, 0)
        old_illum = lax.dynamic_slice_in_dim(illumination, first_column, NXB, 0)
        illumination = lax.dynamic_update_slice_in_dim(illumination, old_illum + illum_box, first_column, 0)
    migrated = gradient / jnp.sqrt(illumination + damping)
    return migrated.reshape(ROUNDS, OWNERS, TW, NZ)
```

```python
import functools

import jax
import jax.numpy as jnp
from jax import lax
from jax.experimental import pallas as pl
from jax.experimental.pallas import tpu as pltpu
from jax.sharding import PartitionSpec as P

damping = 1.0
LANES = 128
HALO = 8
BLOCK = 8
F32 = jnp.float32
MESH = pl.DeviceIdType.MESH


def wait_bytes(ref, sem):
    pltpu.make_async_copy(ref, ref, sem).wait()


def column_of(raw, c):
    shots, ext, lanes = raw.shape
    return raw.reshape(shots * ext, lanes)[pl.ds(c, shots, stride=ext), :]


def kernel(
    n_box,
    n_shot,
    first_smem,
    sources_smem,
    wavelet_smem,
    u_prev,
    u_now,
    born_prev,
    born_now,
    adj_after,
    adj_last,
    velocity,
    receivers,
    observed,
    reflectivity,
    out,
    raw_u,
    raw_q,
    raw_b,
    raw_v,
    rec,
    obs,
    refl,
    wave_u,
    accel,
    wave_b,
    wave_q,
    grad_part,
    adj_m,
    speed,
    image,
    mask,
    target,
    tile_out,
    tile_in,
    slab_e,
    slab_l,
    stage_e,
    stage_l,
    back_e,
    back_l,
    aligned_e,
    aligned_l,
    reduce_e,
    reduce_l,
    result,
    load_sem,
    halo_send,
    halo_recv,
    box_send,
    box_recv,
    shot_send,
    shot_recv,
):
    shots, columns, depth = u_now.shape[1:]
    steps = wavelet_smem.shape[2]
    n_rec = receivers.shape[1]
    rounds = reflectivity.shape[0]
    ext = columns + 2 * HALO
    spare = rounds - n_box
    share = rounds // n_shot
    g = lax.axis_index("shot")
    p = lax.axis_index("box")
    last = n_box - 1

    barrier = pltpu.get_barrier_semaphore()

    def greet_box(k, carry):
        pl.semaphore_signal(
            barrier, inc=1, device_id={"box": lax.rem(p + k, n_box)}, device_id_type=MESH
        )
        return carry

    def greet_shot(k, carry):
        pl.semaphore_signal(
            barrier, inc=1, device_id={"shot": lax.rem(g + k, n_shot)}, device_id_type=MESH
        )
        return carry

    lax.fori_loop(1, n_box, greet_box, 0)
    lax.fori_loop(1, n_shot, greet_shot, 0)

    loads = []

    def load(src, dst):
        copy = pltpu.make_async_copy(src, dst, load_sem.at[len(loads)])
        copy.start()
        loads.append(copy)
        return copy

    half = [pl.ds(0, LANES), pl.ds(LANES, LANES)]
    own = pl.ds(HALO, columns)
    load_refl = load(reflectivity.at[:, 0, :, half[0]], refl.at[pl.ds(1, rounds)])
    load_v = [load(velocity.at[0, :, half[h]], raw_v.at[h, own]) for h in range(2)]
    load_u = [
        load(field.at[0, :, :, half[h]], raw_u.at[f, h, :, own])
        for f, field in enumerate((u_prev, u_now))
        for h in range(2)
    ]
    load_r = [load(receivers, rec.at[1]), load(observed.at[0], obs.at[1])]
    load_q = [
        load(field.at[0, :, :, half[h]], raw_q.at[f, h, :, own])
        for f, field in enumerate((adj_after, adj_last))
        for h in range(2)
    ]
    load_b = [
        load(field.at[0, :, :, half[0]], raw_b.at[f, :, own])
        for f, field in enumerate((born_prev, born_now))
    ]

    for edge, place, side in ((0, 0, 0), (last, HALO + columns, 2)):

        @pl.when(p == edge)
        def _():
            strip = pl.ds(place, HALO)
            raw_v[:, strip] = jnp.zeros((2, HALO, LANES), F32)
            raw_b[:, :, strip] = jnp.zeros((2, shots, HALO, LANES), F32)
            for f in range(2):
                raw_u[f, :, :, strip] = jnp.zeros((2, shots, HALO, LANES), F32)
                raw_q[f, :, :, strip] = jnp.zeros((2, shots, HALO, LANES), F32)
            rec[side] = jnp.full((1, n_rec), -1, jnp.int32)
            obs[side] = jnp.zeros((shots, steps, n_rec), F32)

    blank = jnp.zeros((shots, LANES), F32)
    for pad in (0, ext + 1):
        for level in range(2):
            wave_b[level, pad] = blank
            for h in range(2):
                wave_u[level, h, pad] = blank
        for level in range(wave_q.shape[0]):
            for h in range(2):
                wave_q[level, h, pad] = blank
        for level in range(steps):
            adj_m[level, pad] = blank
    for c in (0, 1, ext - 2, ext - 1):
        image[c] = blank
    refl[0] = jnp.zeros((2, LANES), F32)
    refl[rounds + 1] = jnp.zeros((2, LANES), F32)
    back_e[pl.ds(0, spare)] = jnp.zeros((spare,) + back_e.shape[1:], F32)
    back_e[pl.ds(spare + n_box, spare)] = jnp.zeros((spare,) + back_e.shape[1:], F32)
    back_l[pl.ds(0, spare)] = jnp.zeros((spare,) + back_l.shape[1:], F32)
    back_l[pl.ds(spare + n_box, spare)] = jnp.zeros((spare,) + back_l.shape[1:], F32)

    first = first_smem[0]
    rotation = lax.rem(first, n_box)
    first_round = lax.div(first, n_box) + (p < rotation).astype(jnp.int32)
    lead = lax.rem(p - first + 3 + 64 * n_box, n_box)
    source_round = lax.div(first - 3 + lead - p + 64 * n_box, n_box) - 64

    load_refl.wait()
    tile_out[:, 0] = refl[pl.ds(source_round + 1, n_box)]
    tile_out[:, 1] = refl[pl.ds(source_round + 2, n_box)]
    tile_in[p] = tile_out[p]

    pl.semaphore_wait(barrier, n_box - 1 + n_shot - 1)

    def box_exchange(staged, landing, place, sem):
        def send(k, carry):
            target_device = lax.rem(p + k, n_box)
            pltpu.make_async_remote_copy(
                src_ref=staged.at[target_device],
                dst_ref=landing.at[place],
                send_sem=box_send.at[sem],
                recv_sem=box_recv.at[sem],
                device_id={"box": target_device},
                device_id_type=MESH,
            ).start()
            return carry

        lax.fori_loop(1, n_box, send, 0)

    def box_sent(staged, sem):
        wait_bytes(staged.at[pl.ds(0, n_box - 1)], box_send.at[sem])

    def box_arrived(landing, sem):
        wait_bytes(landing.at[pl.ds(0, n_box - 1)], box_recv.at[sem])

    box_exchange(tile_out, tile_in, p, 0)

    left_edge, right_edge = pl.ds(0, HALO), pl.ds(columns - HALO, HALO)
    left_halo, right_halo = pl.ds(0, HALO), pl.ds(HALO + columns, HALO)

    def halo_pieces(edge, halo, side):
        yield 0, [
            (field.at[0, :, edge, half[h]], raw_u.at[f, h, :, halo])
            for f, field in enumerate((u_prev, u_now))
            for h in range(2)
        ]
        yield 1, [(velocity.at[0, edge, half[h]], raw_v.at[h, halo]) for h in range(2)]
        yield 2, [
            (field.at[0, :, edge, half[h]], raw_q.at[f, h, :, halo])
            for f, field in enumerate((adj_after, adj_last))
            for h in range(2)
        ]
        yield 3, [
            (field.at[0, :, edge, half[0]], raw_b.at[f, :, halo])
            for f, field in enumerate((born_prev, born_now))
        ]
        yield 4, [(receivers, rec.at[side])]
        yield 5, [(observed.at[0], obs.at[side])]

    def halo_refs(group, edge_side):
        halo = (left_halo, right_halo)[edge_side]
        side = (0, 2)[edge_side]
        return (
            raw_u.at[:, :, :, halo],
            raw_v.at[:, halo],
            raw_q.at[:, :, :, halo],
            raw_b.at[:, :, halo],
            rec.at[side],
            obs.at[side],
        )[group]

    def send_halo(direction):
        edge, halo, side = (
            (left_edge, right_halo, 2),
            (right_edge, left_halo, 0),
        )[direction]
        neighbour = (p - 1, p + 1)[direction]
        for group, pieces in halo_pieces(edge, halo, side):
            for src, dst in pieces:
                pltpu.make_async_remote_copy(
                    src_ref=src,
                    dst_ref=dst,
                    send_sem=halo_send.at[direction, group],
                    recv_sem=halo_recv.at[direction, group],
                    device_id={"box": neighbour},
                    device_id_type=MESH,
                ).start()

    @pl.when(p > 0)
    def _():
        send_halo(0)

    @pl.when(p < last)
    def _():
        send_halo(1)

    def halo_arrived(group):
        @pl.when(p < last)
        def _():
            wait_bytes(halo_refs(group, 1), halo_recv.at[0, group])

        @pl.when(p > 0)
        def _():
            wait_bytes(halo_refs(group, 0), halo_recv.at[1, group])

    def halo_sent(group):
        @pl.when(p > 0)
        def _():
            wait_bytes(halo_refs(group, 1), halo_send.at[0, group])

        @pl.when(p < last)
        def _():
            wait_bytes(halo_refs(group, 0), halo_send.at[1, group])

    lane = lax.broadcasted_iota(jnp.int32, (shots, LANES), 1)
    at_top = lane == 0
    at_bottom = lane == LANES - 1
    shot_row = lax.broadcasted_iota(jnp.int32, (shots, LANES), 0)
    first_cell = (p * columns - HALO) * depth

    def by_columns(raw, working):
        def move(c, carry):
            working[c + 1] = column_of(raw, c)
            return carry

        lax.fori_loop(0, ext, move, 0, unroll=16)

    source_cell = jnp.zeros((shots, LANES), jnp.int32)
    pulses = [jnp.zeros((shots, LANES), F32) for _ in range(steps)]
    for s in range(shots):
        source_cell = jnp.where(shot_row == s, sources_smem[0, s], source_cell)
        for t in range(steps):
            pulses[t] = jnp.where(shot_row == s, wavelet_smem[0, s, t], pulses[t])
    source_cell = source_cell - first_cell - lane

    for copy in load_u + load_v:
        copy.wait()
    halo_arrived(0)
    halo_arrived(1)
    for h in range(2):
        by_columns(raw_u.at[0, h], wave_u.at[1, h])
        by_columns(raw_u.at[1, h], wave_u.at[0, h])

        def widen(c, carry):
            speed[h, c] = jnp.broadcast_to(raw_v[h, pl.ds(c, 1), :], (shots, LANES))
            return carry

        lax.fori_loop(0, ext, widen, 0, unroll=16)

    def blocks(body, count=ext // BLOCK, offset=0):
        def step(i, carry):
            body(offset + i * BLOCK, i)
            return carry

        lax.fori_loop(0, count, step, 0, unroll=2)

    def turn(x, by):
        return pltpu.roll(x, by, axis=2)

    def lap_both(wave, level, c):
        n = [wave[level, h, pl.ds(c + 1, BLOCK)] for h in range(2)]
        down = [turn(n[h], 1) for h in range(2)]
        up = [turn(n[h], LANES - 1) for h in range(2)]
        shallow = [jnp.where(at_top, 0.0, down[0]), jnp.where(at_top, down[0], down[1])]
        deep = [jnp.where(at_bottom, up[1], up[0]), jnp.where(at_bottom, 0.0, up[1])]
        laps = [
            (wave[level, h, pl.ds(c, BLOCK)] + wave[level, h, pl.ds(c + 2, BLOCK)])
            + (shallow[h] + deep[h])
            - 4.0 * n[h]
            for h in range(2)
        ]
        return n, laps

    def lap_top(wave, level, c):
        n = wave[level, pl.ds(c + 1, BLOCK)]
        shallow = jnp.where(at_top, 0.0, turn(n, 1))
        deep = jnp.where(at_bottom, 0.0, turn(n, LANES - 1))
        lap = (wave[level, pl.ds(c, BLOCK)] + wave[level, pl.ds(c + 2, BLOCK)]) + (
            shallow + deep
        )
        return n, lap - 4.0 * n

    cell_step = lax.broadcasted_iota(jnp.int32, (BLOCK, shots, LANES), 0) * depth

    for t in range(steps):
        now, old = t % 2, 1 - t % 2

        def advance(c, i):
            n, laps = lap_both(wave_u, now, c)
            for h in range(2):
                offset = (source_cell - (c * depth + h * LANES))[None]
                a = speed[h, pl.ds(c, BLOCK)] * laps[h] + jnp.where(
                    offset == cell_step, pulses[t][None], 0.0
                )
                accel[t, h, pl.ds(c, BLOCK)] = a
                if t < steps - 1:
                    wave_u[old, h, pl.ds(c + 1, BLOCK)] = (
                        (n[h] + n[h]) - wave_u[old, h, pl.ds(c + 1, BLOCK)]
                    ) + a

        blocks(advance)

    for copy in load_q:
        copy.wait()
    halo_arrived(2)
    for h in range(2):
        by_columns(raw_q.at[0, h], wave_q.at[0, h])
        by_columns(raw_q.at[1, h], wave_q.at[1, h])
    for k in range(steps):

        def retreat(c, i):
            n, laps = lap_both(wave_q, k + 1, c)
            for h in range(2):
                wave_q[k + 2, h, pl.ds(c + 1, BLOCK)] = (
                    (n[h] + n[h]) - wave_q[k, h, pl.ds(c + 1, BLOCK)]
                ) + speed[h, pl.ds(c, BLOCK)] * laps[h]

        blocks(retreat)

    def store_rows(slab, kind, i, block):
        for r in range(BLOCK):
            row = jnp.sum(block[r], axis=0, keepdims=True)
            j = i * (BLOCK // 2) + r // 2
            slab[j, kind, pl.ds(r % 2, 1), :] = row
            slab[j + n_box, kind, pl.ds(r % 2, 1), :] = row

    def correlate(c, i):
        a = [[accel[t, h, pl.ds(c, BLOCK)] for h in range(2)] for t in range(steps)]
        q = [
            [wave_q[steps + 1 - t, h, pl.ds(c + 1, BLOCK)] for h in range(2)]
            for t in range(steps)
        ]
        for h in range(2):
            store_rows(slab_e, h, i, sum(a[t][h] * a[t][h] for t in range(steps)))
        store_rows(slab_e, 2, i, sum(q[t][1] * a[t][1] for t in range(steps)))
        grad_part[pl.ds(i * BLOCK, BLOCK)] = sum(q[t][0] * a[t][0] for t in range(steps))

    blocks(correlate, columns // BLOCK, HALO)

    turned = lax.rem(n_box - rotation, n_box)
    stage_e[...] = slab_e[pl.ds(turned, n_box)]
    back_e[spare + p] = stage_e[p]
    box_exchange(stage_e, back_e, spare + p, 1)

    for copy in load_r + load_b:
        copy.wait()
    halo_arrived(4)
    halo_arrived(5)
    halo_arrived(3)
    by_columns(raw_b.at[0], wave_b.at[1])
    by_columns(raw_b.at[1], wave_b.at[0])
    beside = HALO // 2
    heard = (
        [(0, n_rec - beside + r) for r in range(beside)]
        + [(1, r) for r in range(n_rec)]
        + [(2, r) for r in range(beside)]
    )
    cells = [rec[side] for side in range(3)]
    data = [[obs[side, :, t, :] for t in range(steps)] for side in range(3)]
    for slot, (side, r) in enumerate(heard):
        cell = jnp.broadcast_to(cells[side][:, r : r + 1], (shots, LANES)) - first_cell - lane
        amounts = [
            jnp.broadcast_to(data[side][t][:, r : r + 1], (shots, LANES))
            for t in range(steps)
        ]
        for w in range(2):
            c = 2 * slot + w
            hit = cell == c * depth
            mask[c] = jnp.where(hit, 1.0, 0.0)
            for t in range(steps):
                target[t, c] = jnp.where(hit, amounts[t], 0.0)

    box_arrived(tile_in, 0)
    for j in range(n_box + 6):
        owner = lax.rem(rotation + j - 3 + n_box, n_box)
        tile = tile_in[owner, j // n_box]
        for w in range(2):
            image[HALO - 6 + 2 * j + w] = jnp.broadcast_to(tile[w : w + 1], (shots, LANES))

    for t in range(steps):
        now, old = t % 2, 1 - t % 2

        def scatter_wave(c, i):
            n, lap = lap_top(wave_b, now, c)
            b = (
                ((n + n) - wave_b[old, pl.ds(c + 1, BLOCK)])
                + speed[0, pl.ds(c, BLOCK)] * lap
                + image[pl.ds(c, BLOCK)] * accel[t, 0, pl.ds(c, BLOCK)]
            )
            if t < steps - 1:
                wave_b[old, pl.ds(c + 1, BLOCK)] = b
            adj_m[t, pl.ds(c + 1, BLOCK)] = (
                mask[pl.ds(c, BLOCK)] * b - target[t, pl.ds(c, BLOCK)]
            )

        blocks(scatter_wave)

    for t in reversed(range(steps - 1)):

        def residual(c, i):
            n, lap = lap_top(adj_m, t + 1, c)
            q = (n + n) + speed[0, pl.ds(c, BLOCK)] * lap + adj_m[t, pl.ds(c + 1, BLOCK)]
            if t + 2 < steps:
                q = q - adj_m[t + 2, pl.ds(c + 1, BLOCK)]
            adj_m[t, pl.ds(c + 1, BLOCK)] = q

        blocks(residual)

    def correlate_late(c, i):
        total = grad_part[pl.ds(i * BLOCK, BLOCK)] + sum(
            adj_m[t, pl.ds(c + 1, BLOCK)] * accel[t, 0, pl.ds(c, BLOCK)]
            for t in range(steps)
        )
        store_rows(slab_l, 0, i, total)

    blocks(correlate_late, columns // BLOCK, HALO)
    stage_l[...] = slab_l[pl.ds(turned, n_box)]
    back_l[spare + p] = stage_l[p]
    box_exchange(stage_l, back_l, spare + p, 2)

    def shot_exchange(src_of, landing, sem):
        def send(k, carry):
            s = lax.rem(g + k, n_shot)
            pltpu.make_async_remote_copy(
                src_ref=src_of(s),
                dst_ref=landing,
                send_sem=shot_send.at[sem],
                recv_sem=shot_recv.at[sem],
                device_id={"shot": s},
                device_id_type=MESH,
            ).start()
            return carry

        lax.fori_loop(1, n_shot, send, 0)

    mine = pl.ds(g * share, share)
    others = pl.ds(0, (n_shot - 1) * share)

    def scatter_rounds(back, aligned, landing, box_sem, sem):
        box_arrived(back, box_sem)
        aligned[...] = back[pl.ds(spare - first_round, rounds)]
        landing[g] = aligned[mine]
        shot_exchange(lambda s: aligned.at[pl.ds(s * share, share)], landing.at[g], sem)

    scatter_rounds(back_e, aligned_e, reduce_e, 1, 0)
    scatter_rounds(back_l, aligned_l, reduce_l, 2, 1)
    wait_bytes(reduce_e.at[pl.ds(0, n_shot - 1)], shot_recv.at[0])
    sums = reduce_e[0]
    for s in range(1, n_shot):
        sums = sums + reduce_e[s]
    scale = [jnp.sqrt(sums[:, h] + damping) for h in range(2)]
    result[mine, 0, :, half[1]] = sums[:, 2] / scale[1]
    wait_bytes(reduce_l.at[pl.ds(0, n_shot - 1)], shot_recv.at[1])
    sums = reduce_l[0, :, 0]
    for s in range(1, n_shot):
        sums = sums + reduce_l[s, :, 0]
    result[mine, 0, :, half[0]] = sums / scale[0]
    shot_exchange(lambda s: result.at[mine], result.at[mine], 2)
    wait_bytes(result.at[others], shot_recv.at[2])
    pltpu.sync_copy(result, out)

    for group in range(6):
        halo_sent(group)
    box_sent(tile_out, 0)
    box_sent(stage_e, 1)
    box_sent(stage_l, 2)
    wait_bytes(aligned_e.at[others], shot_send.at[0])
    wait_bytes(aligned_l.at[others], shot_send.at[1])
    wait_bytes(result.at[others], shot_send.at[2])


def on_device(
    n_box,
    n_shot,
    u_prev,
    u_now,
    born_prev,
    born_now,
    adj_after,
    adj_last,
    velocity,
    wavelet,
    sources,
    receivers,
    observed,
    first_tile,
    reflectivity,
):
    shots, columns, depth = u_now.shape[1:]
    steps = wavelet.shape[2]
    n_rec = receivers.shape[1]
    rounds = reflectivity.shape[0]
    ext = columns + 2 * HALO
    spare = rounds - n_box
    share = rounds // n_shot

    def vmem(*dims):
        return pltpu.VMEM(dims, F32)

    plane = (shots, LANES)
    tile = (2, LANES)
    scratch = [
        vmem(2, 2, shots, ext, LANES),
        vmem(2, 2, shots, ext, LANES),
        vmem(2, shots, ext, LANES),
        vmem(2, ext, LANES),
        pltpu.VMEM((3, 1, n_rec), jnp.int32),
        vmem(3, shots, steps, n_rec),
        vmem(rounds + 2, *tile),
        vmem(2, 2, ext + 2, *plane),
        vmem(steps, 2, ext, *plane),
        vmem(2, ext + 2, *plane),
        vmem(steps + 2, 2, ext + 2, *plane),
        vmem(columns, *plane),
        vmem(steps, ext + 2, *plane),
        vmem(2, ext, *plane),
        vmem(ext, *plane),
        vmem(ext, *plane),
        vmem(steps, ext, *plane),
        vmem(n_box, 2, *tile),
        vmem(n_box, 2, *tile),
        vmem(2 * n_box, 3, *tile),
        vmem(2 * n_box, 1, *tile),
        vmem(n_box, 3, *tile),
        vmem(n_box, 1, *tile),
        vmem(n_box + 2 * spare, 3, *tile),
        vmem(n_box + 2 * spare, 1, *tile),
        vmem(rounds, 3, *tile),
        vmem(rounds, 1, *tile),
        vmem(n_shot, share, 3, *tile),
        vmem(n_shot, share, 1, *tile),
        vmem(rounds, 1, 2, depth),
        pltpu.SemaphoreType.DMA((17,)),
        pltpu.SemaphoreType.DMA((2, 6)),
        pltpu.SemaphoreType.DMA((2, 6)),
        pltpu.SemaphoreType.DMA((3,)),
        pltpu.SemaphoreType.DMA((3,)),
        pltpu.SemaphoreType.DMA((3,)),
        pltpu.SemaphoreType.DMA((3,)),
    ]
    smem = pl.BlockSpec(memory_space=pltpu.SMEM)
    anywhere = pl.BlockSpec(memory_space=pl.ANY)
    return pl.pallas_call(
        functools.partial(kernel, n_box, n_shot),
        out_shape=jax.ShapeDtypeStruct(reflectivity.shape, F32),
        in_specs=[smem] * 3 + [anywhere] * 10,
        out_specs=anywhere,
        scratch_shapes=scratch,
        compiler_params=pltpu.CompilerParams(
            collective_id=0, has_side_effects=True, vmem_limit_bytes=48 * 1024 * 1024
        ),
    )(
        first_tile,
        sources,
        wavelet,
        u_prev,
        u_now,
        born_prev,
        born_now,
        adj_after,
        adj_last,
        velocity,
        receivers,
        observed,
        reflectivity,
    )


def solution(mesh):
    return jax.shard_map(
        functools.partial(on_device, mesh.shape["box"], mesh.shape["shot"]),
        mesh=mesh,
        in_specs=(
            P("shot", None, "box", None),
            P("shot", None, "box", None),
            P("shot", None, "box", None),
            P("shot", None, "box", None),
            P("shot", None, "box", None),
            P("shot", None, "box", None),
            P("shot", "box", None),
            P("shot", None, None),
            P("shot", None),
            P("shot", "box"),
            P("shot", None, None, "box"),
            P("shot"),
            P(None, "box", None, None),
        ),
        out_specs=P(None, "box", None, None),
        check_vma=False,
    )
```

```python
import functools

import jax
import jax.numpy as jnp
from jax import lax
from jax.experimental import pallas as pl
from jax.experimental.pallas import tpu as pltpu
from jax.sharding import PartitionSpec as P

damping = 1.0
LANES = 128
HALO = 8
BLOCK = 8
F32 = jnp.float32
MESH = pl.DeviceIdType.MESH


def wait_bytes(ref, sem):
    pltpu.make_async_copy(ref, ref, sem).wait()


def column_of(raw, c):
    shots, ext, lanes = raw.shape
    return raw.reshape(shots * ext, lanes)[pl.ds(c, shots, stride=ext), :]


def kernel(
    n_box,
    n_shot,
    first_tile,
    sources,
    wavelet,
    u_prev,
    u_now,
    born_prev,
    born_now,
    adj_after,
    adj_last,
    velocity,
    receivers,
    observed,
    reflectivity,
    out,
    sources_smem,
    wavelet_smem,
    raw_u,
    raw_q,
    raw_b,
    raw_v,
    rec,
    obs,
    refl,
    wave_u,
    accel,
    wave_b,
    wave_q,
    grad_part,
    adj_m,
    speed,
    image,
    mask,
    target,
    tile_out,
    tile_in,
    slab_e,
    slab_l,
    stage_e,
    stage_l,
    back_e,
    back_l,
    aligned_e,
    aligned_l,
    reduce_e,
    reduce_l,
    result,
    load_sem,
    halo_send,
    halo_recv,
    box_send,
    box_recv,
    shot_send,
    shot_recv,
):
    shots, columns, depth = u_now.shape[1:]
    steps = wavelet_smem.shape[1]
    n_rec = receivers.shape[1]
    rounds = reflectivity.shape[0]
    ext = columns + 2 * HALO
    spare = rounds - n_box
    share = rounds // n_shot
    g = lax.axis_index("shot")
    p = lax.axis_index("box")
    last = n_box - 1

    barrier = pltpu.get_barrier_semaphore()

    def greet_box(k, carry):
        pl.semaphore_signal(
            barrier, inc=1, device_id={"box": lax.rem(p + k, n_box)}, device_id_type=MESH
        )
        return carry

    def greet_shot(k, carry):
        pl.semaphore_signal(
            barrier, inc=1, device_id={"shot": lax.rem(g + k, n_shot)}, device_id_type=MESH
        )
        return carry

    lax.fori_loop(1, n_box, greet_box, 0)
    lax.fori_loop(1, n_shot, greet_shot, 0)

    loads = []

    def load(src, dst):
        copy = pltpu.make_async_copy(src, dst, load_sem.at[len(loads)])
        copy.start()
        loads.append(copy)
        return copy

    half = [pl.ds(0, LANES), pl.ds(LANES, LANES)]
    own = pl.ds(HALO, columns)
    load_refl = load(reflectivity.at[:, 0, :, half[0]], refl.at[pl.ds(1, rounds)])
    load_v = [load(velocity.at[0, :, half[h]], raw_v.at[h, own]) for h in range(2)]
    load_u = [
        load(field.at[0, :, :, half[h]], raw_u.at[f, h, :, own])
        for f, field in enumerate((u_prev, u_now))
        for h in range(2)
    ]
    load_s = [load(sources, sources_smem), load(wavelet, wavelet_smem)]
    load_r = [load(receivers, rec.at[1]), load(observed.at[0], obs.at[1])]
    load_q = [
        load(field.at[0, :, :, half[h]], raw_q.at[f, h, :, own])
        for f, field in enumerate((adj_after, adj_last))
        for h in range(2)
    ]
    load_b = [
        load(field.at[0, :, :, half[0]], raw_b.at[f, :, own])
        for f, field in enumerate((born_prev, born_now))
    ]

    for edge, place, side in ((0, 0, 0), (last, HALO + columns, 2)):

        @pl.when(p == edge)
        def _():
            strip = pl.ds(place, HALO)
            raw_v[:, strip] = jnp.zeros((2, HALO, LANES), F32)
            raw_b[:, :, strip] = jnp.zeros((2, shots, HALO, LANES), F32)
            for f in range(2):
                raw_u[f, :, :, strip] = jnp.zeros((2, shots, HALO, LANES), F32)
                raw_q[f, :, :, strip] = jnp.zeros((2, shots, HALO, LANES), F32)
            rec[side] = jnp.full((1, n_rec), -1, jnp.int32)
            obs[side] = jnp.zeros((shots, steps, n_rec), F32)

    blank = jnp.zeros((shots, LANES), F32)
    for pad in (0, ext + 1):
        for level in range(2):
            wave_b[level, pad] = blank
            for h in range(2):
                wave_u[level, h, pad] = blank
        for level in range(wave_q.shape[0]):
            for h in range(2):
                wave_q[level, h, pad] = blank
        for level in range(steps):
            adj_m[level, pad] = blank
    for c in (0, 1, ext - 2, ext - 1):
        image[c] = blank
    refl[0] = jnp.zeros((2, LANES), F32)
    refl[rounds + 1] = jnp.zeros((2, LANES), F32)
    back_e[pl.ds(0, spare)] = jnp.zeros((spare,) + back_e.shape[1:], F32)
    back_e[pl.ds(spare + n_box, spare)] = jnp.zeros((spare,) + back_e.shape[1:], F32)
    back_l[pl.ds(0, spare)] = jnp.zeros((spare,) + back_l.shape[1:], F32)
    back_l[pl.ds(spare + n_box, spare)] = jnp.zeros((spare,) + back_l.shape[1:], F32)

    first = first_tile[0]
    rotation = lax.rem(first, n_box)
    first_round = lax.div(first, n_box) + (p < rotation).astype(jnp.int32)
    lead = lax.rem(p - first + 3 + 64 * n_box, n_box)
    source_round = lax.div(first - 3 + lead - p + 64 * n_box, n_box) - 64

    load_refl.wait()
    tile_out[:, 0] = refl[pl.ds(source_round + 1, n_box)]
    tile_out[:, 1] = refl[pl.ds(source_round + 2, n_box)]
    tile_in[p] = tile_out[p]

    pl.semaphore_wait(barrier, n_box - 1 + n_shot - 1)

    def box_exchange(staged, landing, place, sem):
        def send(k, carry):
            target_device = lax.rem(p + k, n_box)
            pltpu.make_async_remote_copy(
                src_ref=staged.at[target_device],
                dst_ref=landing.at[place],
                send_sem=box_send.at[sem],
                recv_sem=box_recv.at[sem],
                device_id={"box": target_device},
                device_id_type=MESH,
            ).start()
            return carry

        lax.fori_loop(1, n_box, send, 0)

    def box_sent(staged, sem):
        wait_bytes(staged.at[pl.ds(0, n_box - 1)], box_send.at[sem])

    def box_arrived(landing, sem):
        wait_bytes(landing.at[pl.ds(0, n_box - 1)], box_recv.at[sem])

    box_exchange(tile_out, tile_in, p, 0)

    left_edge, right_edge = pl.ds(0, HALO), pl.ds(columns - HALO, HALO)
    left_halo, right_halo = pl.ds(0, HALO), pl.ds(HALO + columns, HALO)

    def halo_pieces(edge, halo, side):
        yield 0, [
            (field.at[0, :, edge, half[h]], raw_u.at[f, h, :, halo])
            for f, field in enumerate((u_prev, u_now))
            for h in range(2)
        ]
        yield 1, [(velocity.at[0, edge, half[h]], raw_v.at[h, halo]) for h in range(2)]
        yield 2, [
            (field.at[0, :, edge, half[h]], raw_q.at[f, h, :, halo])
            for f, field in enumerate((adj_after, adj_last))
            for h in range(2)
        ]
        yield 3, [
            (field.at[0, :, edge, half[0]], raw_b.at[f, :, halo])
            for f, field in enumerate((born_prev, born_now))
        ]
        yield 4, [(receivers, rec.at[side])]
        yield 5, [(observed.at[0], obs.at[side])]

    def halo_refs(group, edge_side):
        halo = (left_halo, right_halo)[edge_side]
        side = (0, 2)[edge_side]
        return (
            raw_u.at[:, :, :, halo],
            raw_v.at[:, halo],
            raw_q.at[:, :, :, halo],
            raw_b.at[:, :, halo],
            rec.at[side],
            obs.at[side],
        )[group]

    def send_halo(direction):
        edge, halo, side = (
            (left_edge, right_halo, 2),
            (right_edge, left_halo, 0),
        )[direction]
        neighbour = (p - 1, p + 1)[direction]
        for group, pieces in halo_pieces(edge, halo, side):
            for src, dst in pieces:
                pltpu.make_async_remote_copy(
                    src_ref=src,
                    dst_ref=dst,
                    send_sem=halo_send.at[direction, group],
                    recv_sem=halo_recv.at[direction, group],
                    device_id={"box": neighbour},
                    device_id_type=MESH,
                ).start()

    @pl.when(p > 0)
    def _():
        send_halo(0)

    @pl.when(p < last)
    def _():
        send_halo(1)

    def halo_arrived(group):
        @pl.when(p < last)
        def _():
            wait_bytes(halo_refs(group, 1), halo_recv.at[0, group])

        @pl.when(p > 0)
        def _():
            wait_bytes(halo_refs(group, 0), halo_recv.at[1, group])

    def halo_sent(group):
        @pl.when(p > 0)
        def _():
            wait_bytes(halo_refs(group, 1), halo_send.at[0, group])

        @pl.when(p < last)
        def _():
            wait_bytes(halo_refs(group, 0), halo_send.at[1, group])

    lane = lax.broadcasted_iota(jnp.int32, (shots, LANES), 1)
    at_top = lane == 0
    at_bottom = lane == LANES - 1
    shot_row = lax.broadcasted_iota(jnp.int32, (shots, LANES), 0)
    first_cell = (p * columns - HALO) * depth

    def by_columns(raw, working):
        def move(c, carry):
            working[c + 1] = column_of(raw, c)
            return carry

        lax.fori_loop(0, ext, move, 0, unroll=16)

    for copy in load_s:
        copy.wait()
    source_cell = jnp.zeros((shots, LANES), jnp.int32)
    pulses = [jnp.zeros((shots, LANES), F32) for _ in range(steps)]
    for s in range(shots):
        source_cell = jnp.where(shot_row == s, sources_smem[0, s], source_cell)
        for t in range(steps):
            pulses[t] = jnp.where(shot_row == s, wavelet_smem[0, t, s], pulses[t])
    source_cell = source_cell - first_cell - lane

    for copy in load_u + load_v:
        copy.wait()
    halo_arrived(0)
    halo_arrived(1)
    for h in range(2):
        by_columns(raw_u.at[0, h], wave_u.at[1, h])
        by_columns(raw_u.at[1, h], wave_u.at[0, h])

        def widen(c, carry):
            speed[h, c] = jnp.broadcast_to(raw_v[h, pl.ds(c, 1), :], (shots, LANES))
            return carry

        lax.fori_loop(0, ext, widen, 0, unroll=16)

    def blocks(body, count=ext // BLOCK, offset=0):
        def step(i, carry):
            body(offset + i * BLOCK, i)
            return carry

        lax.fori_loop(0, count, step, 0, unroll=2)

    def turn(x, by):
        return pltpu.roll(x, by, axis=2)

    def lap_both(wave, level, c):
        n = [wave[level, h, pl.ds(c + 1, BLOCK)] for h in range(2)]
        down = [turn(n[h], 1) for h in range(2)]
        up = [turn(n[h], LANES - 1) for h in range(2)]
        shallow = [jnp.where(at_top, 0.0, down[0]), jnp.where(at_top, down[0], down[1])]
        deep = [jnp.where(at_bottom, up[1], up[0]), jnp.where(at_bottom, 0.0, up[1])]
        laps = [
            (wave[level, h, pl.ds(c, BLOCK)] + wave[level, h, pl.ds(c + 2, BLOCK)])
            + (shallow[h] + deep[h])
            - 4.0 * n[h]
            for h in range(2)
        ]
        return n, laps

    def lap_top(wave, level, c):
        n = wave[level, pl.ds(c + 1, BLOCK)]
        shallow = jnp.where(at_top, 0.0, turn(n, 1))
        deep = jnp.where(at_bottom, 0.0, turn(n, LANES - 1))
        lap = (wave[level, pl.ds(c, BLOCK)] + wave[level, pl.ds(c + 2, BLOCK)]) + (
            shallow + deep
        )
        return n, lap - 4.0 * n

    cell_step = lax.broadcasted_iota(jnp.int32, (BLOCK, shots, LANES), 0) * depth

    for t in range(steps):
        now, old = t % 2, 1 - t % 2

        def advance(c, i):
            n, laps = lap_both(wave_u, now, c)
            for h in range(2):
                offset = (source_cell - (c * depth + h * LANES))[None]
                a = speed[h, pl.ds(c, BLOCK)] * laps[h] + jnp.where(
                    offset == cell_step, pulses[t][None], 0.0
                )
                accel[t, h, pl.ds(c, BLOCK)] = a
                if t < steps - 1:
                    wave_u[old, h, pl.ds(c + 1, BLOCK)] = (
                        (n[h] + n[h]) - wave_u[old, h, pl.ds(c + 1, BLOCK)]
                    ) + a

        blocks(advance)

    for copy in load_q:
        copy.wait()
    halo_arrived(2)
    for h in range(2):
        by_columns(raw_q.at[0, h], wave_q.at[0, h])
        by_columns(raw_q.at[1, h], wave_q.at[1, h])
    for k in range(steps):

        def retreat(c, i):
            n, laps = lap_both(wave_q, k + 1, c)
            for h in range(2):
                wave_q[k + 2, h, pl.ds(c + 1, BLOCK)] = (
                    (n[h] + n[h]) - wave_q[k, h, pl.ds(c + 1, BLOCK)]
                ) + speed[h, pl.ds(c, BLOCK)] * laps[h]

        blocks(retreat)

    def store_rows(slab, kind, i, block):
        for r in range(BLOCK):
            row = jnp.sum(block[r], axis=0, keepdims=True)
            j = i * (BLOCK // 2) + r // 2
            slab[j, kind, pl.ds(r % 2, 1), :] = row
            slab[j + n_box, kind, pl.ds(r % 2, 1), :] = row

    def correlate(c, i):
        a = [[accel[t, h, pl.ds(c, BLOCK)] for h in range(2)] for t in range(steps)]
        q = [
            [wave_q[steps + 1 - t, h, pl.ds(c + 1, BLOCK)] for h in range(2)]
            for t in range(steps)
        ]
        for h in range(2):
            store_rows(slab_e, h, i, sum(a[t][h] * a[t][h] for t in range(steps)))
        store_rows(slab_e, 2, i, sum(q[t][1] * a[t][1] for t in range(steps)))
        grad_part[pl.ds(i * BLOCK, BLOCK)] = sum(q[t][0] * a[t][0] for t in range(steps))

    blocks(correlate, columns // BLOCK, HALO)

    turned = lax.rem(n_box - rotation, n_box)
    stage_e[...] = slab_e[pl.ds(turned, n_box)]
    back_e[spare + p] = stage_e[p]
    box_exchange(stage_e, back_e, spare + p, 1)

    for copy in load_r + load_b:
        copy.wait()
    halo_arrived(4)
    halo_arrived(5)
    halo_arrived(3)
    by_columns(raw_b.at[0], wave_b.at[1])
    by_columns(raw_b.at[1], wave_b.at[0])
    beside = HALO // 2
    heard = (
        [(0, n_rec - beside + r) for r in range(beside)]
        + [(1, r) for r in range(n_rec)]
        + [(2, r) for r in range(beside)]
    )
    cells = [rec[side] for side in range(3)]
    data = [[obs[side, :, t, :] for t in range(steps)] for side in range(3)]
    for slot, (side, r) in enumerate(heard):
        cell = jnp.broadcast_to(cells[side][:, r : r + 1], (shots, LANES)) - first_cell - lane
        amounts = [
            jnp.broadcast_to(data[side][t][:, r : r + 1], (shots, LANES))
            for t in range(steps)
        ]
        for w in range(2):
            c = 2 * slot + w
            hit = cell == c * depth
            mask[c] = jnp.where(hit, 1.0, 0.0)
            for t in range(steps):
                target[t, c] = jnp.where(hit, amounts[t], 0.0)

    box_arrived(tile_in, 0)
    for j in range(n_box + 6):
        owner = lax.rem(rotation + j - 3 + n_box, n_box)
        tile = tile_in[owner, j // n_box]
        for w in range(2):
            image[HALO - 6 + 2 * j + w] = jnp.broadcast_to(tile[w : w + 1], (shots, LANES))

    for t in range(steps):
        now, old = t % 2, 1 - t % 2

        def scatter_wave(c, i):
            n, lap = lap_top(wave_b, now, c)
            b = (
                ((n + n) - wave_b[old, pl.ds(c + 1, BLOCK)])
                + speed[0, pl.ds(c, BLOCK)] * lap
                + image[pl.ds(c, BLOCK)] * accel[t, 0, pl.ds(c, BLOCK)]
            )
            if t < steps - 1:
                wave_b[old, pl.ds(c + 1, BLOCK)] = b
            adj_m[t, pl.ds(c + 1, BLOCK)] = (
                mask[pl.ds(c, BLOCK)] * b - target[t, pl.ds(c, BLOCK)]
            )

        blocks(scatter_wave)

    for t in reversed(range(steps - 1)):

        def residual(c, i):
            n, lap = lap_top(adj_m, t + 1, c)
            q = (n + n) + speed[0, pl.ds(c, BLOCK)] * lap + adj_m[t, pl.ds(c + 1, BLOCK)]
            if t + 2 < steps:
                q = q - adj_m[t + 2, pl.ds(c + 1, BLOCK)]
            adj_m[t, pl.ds(c + 1, BLOCK)] = q

        blocks(residual)

    def correlate_late(c, i):
        total = grad_part[pl.ds(i * BLOCK, BLOCK)] + sum(
            adj_m[t, pl.ds(c + 1, BLOCK)] * accel[t, 0, pl.ds(c, BLOCK)]
            for t in range(steps)
        )
        store_rows(slab_l, 0, i, total)

    blocks(correlate_late, columns // BLOCK, HALO)
    stage_l[...] = slab_l[pl.ds(turned, n_box)]
    back_l[spare + p] = stage_l[p]
    box_exchange(stage_l, back_l, spare + p, 2)

    def shot_exchange(src_of, landing, sem):
        def send(k, carry):
            s = lax.rem(g + k, n_shot)
            pltpu.make_async_remote_copy(
                src_ref=src_of(s),
                dst_ref=landing,
                send_sem=shot_send.at[sem],
                recv_sem=shot_recv.at[sem],
                device_id={"shot": s},
                device_id_type=MESH,
            ).start()
            return carry

        lax.fori_loop(1, n_shot, send, 0)

    mine = pl.ds(g * share, share)
    others = pl.ds(0, (n_shot - 1) * share)

    def scatter_rounds(back, aligned, landing, box_sem, sem):
        box_arrived(back, box_sem)
        aligned[...] = back[pl.ds(spare - first_round, rounds)]
        landing[g] = aligned[mine]
        shot_exchange(lambda s: aligned.at[pl.ds(s * share, share)], landing.at[g], sem)

    scatter_rounds(back_e, aligned_e, reduce_e, 1, 0)
    scatter_rounds(back_l, aligned_l, reduce_l, 2, 1)
    wait_bytes(reduce_e.at[pl.ds(0, n_shot - 1)], shot_recv.at[0])
    sums = reduce_e[0]
    for s in range(1, n_shot):
        sums = sums + reduce_e[s]
    scale = [jnp.sqrt(sums[:, h] + damping) for h in range(2)]
    result[mine, 0, :, half[1]] = sums[:, 2] / scale[1]
    wait_bytes(reduce_l.at[pl.ds(0, n_shot - 1)], shot_recv.at[1])
    sums = reduce_l[0, :, 0]
    for s in range(1, n_shot):
        sums = sums + reduce_l[s, :, 0]
    result[mine, 0, :, half[0]] = sums / scale[0]
    shot_exchange(lambda s: result.at[mine], result.at[mine], 2)
    wait_bytes(result.at[others], shot_recv.at[2])
    pltpu.sync_copy(result, out)

    for group in range(6):
        halo_sent(group)
    box_sent(tile_out, 0)
    box_sent(stage_e, 1)
    box_sent(stage_l, 2)
    wait_bytes(aligned_e.at[others], shot_send.at[0])
    wait_bytes(aligned_l.at[others], shot_send.at[1])
    wait_bytes(result.at[others], shot_send.at[2])


def on_device(
    n_box,
    n_shot,
    u_prev,
    u_now,
    born_prev,
    born_now,
    adj_after,
    adj_last,
    velocity,
    wavelet,
    sources,
    receivers,
    observed,
    first_tile,
    reflectivity,
):
    shots, columns, depth = u_now.shape[1:]
    steps = wavelet.shape[2]
    n_rec = receivers.shape[1]
    rounds = reflectivity.shape[0]
    ext = columns + 2 * HALO
    spare = rounds - n_box
    share = rounds // n_shot

    def vmem(*dims):
        return pltpu.VMEM(dims, F32)

    plane = (shots, LANES)
    tile = (2, LANES)
    scratch = [
        pltpu.SMEM(sources.shape, jnp.int32),
        pltpu.SMEM((1, steps, shots), F32),
        vmem(2, 2, shots, ext, LANES),
        vmem(2, 2, shots, ext, LANES),
        vmem(2, shots, ext, LANES),
        vmem(2, ext, LANES),
        pltpu.VMEM((3, 1, n_rec), jnp.int32),
        vmem(3, shots, steps, n_rec),
        vmem(rounds + 2, *tile),
        vmem(2, 2, ext + 2, *plane),
        vmem(steps, 2, ext, *plane),
        vmem(2, ext + 2, *plane),
        vmem(steps + 2, 2, ext + 2, *plane),
        vmem(columns, *plane),
        vmem(steps, ext + 2, *plane),
        vmem(2, ext, *plane),
        vmem(ext, *plane),
        vmem(ext, *plane),
        vmem(steps, ext, *plane),
        vmem(n_box, 2, *tile),
        vmem(n_box, 2, *tile),
        vmem(2 * n_box, 3, *tile),
        vmem(2 * n_box, 1, *tile),
        vmem(n_box, 3, *tile),
        vmem(n_box, 1, *tile),
        vmem(n_box + 2 * spare, 3, *tile),
        vmem(n_box + 2 * spare, 1, *tile),
        vmem(rounds, 3, *tile),
        vmem(rounds, 1, *tile),
        vmem(n_shot, share, 3, *tile),
        vmem(n_shot, share, 1, *tile),
        vmem(rounds, 1, 2, depth),
        pltpu.SemaphoreType.DMA((19,)),
        pltpu.SemaphoreType.DMA((2, 6)),
        pltpu.SemaphoreType.DMA((2, 6)),
        pltpu.SemaphoreType.DMA((3,)),
        pltpu.SemaphoreType.DMA((3,)),
        pltpu.SemaphoreType.DMA((3,)),
        pltpu.SemaphoreType.DMA((3,)),
    ]
    hbm = pl.BlockSpec(memory_space=pltpu.HBM)
    return pl.pallas_call(
        functools.partial(kernel, n_box, n_shot),
        out_shape=jax.ShapeDtypeStruct(reflectivity.shape, F32),
        in_specs=[pl.BlockSpec(memory_space=pltpu.SMEM)] + [hbm] * 12,
        out_specs=hbm,
        scratch_shapes=scratch,
        compiler_params=pltpu.CompilerParams(
            collective_id=0, has_side_effects=True, vmem_limit_bytes=67043328
        ),
    )(
        first_tile,
        sources,
        jnp.transpose(wavelet, (0, 2, 1)),
        u_prev,
        u_now,
        born_prev,
        born_now,
        adj_after,
        adj_last,
        velocity,
        receivers,
        observed,
        reflectivity,
    )


def solution(mesh):
    return jax.shard_map(
        functools.partial(on_device, mesh.shape["box"], mesh.shape["shot"]),
        mesh=mesh,
        in_specs=(
            P("shot", None, "box", None),
            P("shot", None, "box", None),
            P("shot", None, "box", None),
            P("shot", None, "box", None),
            P("shot", None, "box", None),
            P("shot", None, "box", None),
            P("shot", "box", None),
            P("shot", None, None),
            P("shot", None),
            P("shot", "box"),
            P("shot", None, None, "box"),
            P("shot"),
            P(None, "box", None, None),
        ),
        out_specs=P(None, "box", None, None),
        check_vma=False,
    )
```

```python
import functools

import jax
import jax.numpy as jnp
from jax import lax
from jax.experimental import pallas as pl
from jax.experimental.pallas import tpu as pltpu
from jax.sharding import PartitionSpec as P

damping = 1.0
LANES = 128
HALO = 8
BLOCK = 8
F32 = jnp.float32
MESH = pl.DeviceIdType.MESH


def wait_bytes(ref, sem):
    pltpu.make_async_copy(ref, ref, sem).wait()


def column_of(raw, c):
    shots, ext, lanes = raw.shape
    return raw.reshape(shots * ext, lanes)[pl.ds(c, shots, stride=ext), :]


def kernel(
    n_box,
    n_shot,
    first_tile,
    sources,
    wavelet,
    u_prev,
    u_now,
    born_prev,
    born_now,
    adj_after,
    adj_last,
    velocity,
    receivers,
    observed,
    reflectivity,
    out,
    sources_smem,
    wavelet_smem,
    raw_u,
    raw_q,
    raw_b,
    raw_v,
    rec,
    obs,
    refl,
    wave_u,
    accel,
    wave_b,
    wave_q,
    grad_part,
    adj_m,
    speed,
    image,
    mask,
    target,
    by_step,
    adj_r,
    tile_out,
    tile_in,
    slab_i,
    slab_d,
    slab_s,
    stage_i,
    stage_d,
    stage_s,
    back_i,
    back_d,
    back_s,
    aligned_i,
    aligned_d,
    aligned_s,
    reduce_i,
    gather_d,
    gather_s,
    scale,
    load_sem,
    halo_send,
    halo_recv,
    box_send,
    box_recv,
    shot_send,
    shot_recv,
):
    shots, columns, depth = u_now.shape[1:]
    steps = wavelet_smem.shape[1]
    n_rec = receivers.shape[1]
    rounds = reflectivity.shape[0]
    ext = columns + 2 * HALO
    spare = rounds - n_box
    share = rounds // n_shot
    g = lax.axis_index("shot")
    p = lax.axis_index("box")
    last = n_box - 1

    barrier = pltpu.get_barrier_semaphore()

    def greet_box(k, carry):
        pl.semaphore_signal(
            barrier, inc=1, device_id={"box": lax.rem(p + k, n_box)}, device_id_type=MESH
        )
        return carry

    def greet_shot(k, carry):
        pl.semaphore_signal(
            barrier, inc=1, device_id={"shot": lax.rem(g + k, n_shot)}, device_id_type=MESH
        )
        return carry

    lax.fori_loop(1, n_box, greet_box, 0)
    lax.fori_loop(1, n_shot, greet_shot, 0)

    loads = []

    def load(src, dst):
        copy = pltpu.make_async_copy(src, dst, load_sem.at[len(loads)])
        copy.start()
        loads.append(copy)
        return copy

    half = [pl.ds(0, LANES), pl.ds(LANES, LANES)]
    own = pl.ds(HALO, columns)
    load_refl = load(reflectivity.at[:, 0, :, half[0]], refl.at[pl.ds(1, rounds)])
    load_v = [load(velocity.at[0, :, half[h]], raw_v.at[h, own]) for h in range(2)]
    load_u = [
        load(field.at[0, :, :, half[h]], raw_u.at[f, h, :, own])
        for f, field in enumerate((u_prev, u_now))
        for h in range(2)
    ]
    load_s = [load(sources, sources_smem), load(wavelet, wavelet_smem)]
    load_r = [load(receivers, rec.at[1]), load(observed.at[0], obs.at[1])]
    load_q = [
        load(field.at[0, :, :, half[h]], raw_q.at[f, h, :, own])
        for f, field in enumerate((adj_after, adj_last))
        for h in range(2)
    ]
    load_b = [
        load(field.at[0, :, :, half[0]], raw_b.at[f, :, own])
        for f, field in enumerate((born_prev, born_now))
    ]

    for edge, place, side in ((0, 0, 0), (last, HALO + columns, 2)):

        @pl.when(p == edge)
        def _():
            strip = pl.ds(place, HALO)
            raw_v[:, strip] = jnp.zeros((2, HALO, LANES), F32)
            raw_b[:, :, strip] = jnp.zeros((2, shots, HALO, LANES), F32)
            for f in range(2):
                raw_u[f, :, :, strip] = jnp.zeros((2, shots, HALO, LANES), F32)
                raw_q[f, :, :, strip] = jnp.zeros((2, shots, HALO, LANES), F32)
            rec[side] = jnp.full((1, n_rec), -1, jnp.int32)
            obs[side] = jnp.zeros((shots, steps, n_rec), F32)

    refl[0] = jnp.zeros((2, LANES), F32)
    refl[rounds + 1] = jnp.zeros((2, LANES), F32)

    first = first_tile[0]
    rotation = lax.rem(first, n_box)
    first_round = lax.div(first, n_box) + (p < rotation).astype(jnp.int32)
    lead = lax.rem(p - first + 3 + 64 * n_box, n_box)
    source_round = lax.div(first - 3 + lead - p + 64 * n_box, n_box) - 64

    load_refl.wait()
    tile_out[:, 0] = refl[pl.ds(source_round + 1, n_box)]
    tile_out[:, 1] = refl[pl.ds(source_round + 2, n_box)]
    tile_in[p] = tile_out[p]

    pl.semaphore_wait(barrier, n_box - 1 + n_shot - 1)

    def box_exchange(staged, landing, place, sem):
        def send(k, carry):
            target_device = lax.rem(p + k, n_box)
            pltpu.make_async_remote_copy(
                src_ref=staged.at[target_device],
                dst_ref=landing.at[place],
                send_sem=box_send.at[sem],
                recv_sem=box_recv.at[sem],
                device_id={"box": target_device},
                device_id_type=MESH,
            ).start()
            return carry

        lax.fori_loop(1, n_box, send, 0)

    def box_sent(staged, sem):
        wait_bytes(staged.at[pl.ds(0, n_box - 1)], box_send.at[sem])

    def box_arrived(landing, sem):
        wait_bytes(landing.at[pl.ds(0, n_box - 1)], box_recv.at[sem])

    left_edge, right_edge = pl.ds(0, HALO), pl.ds(columns - HALO, HALO)
    left_halo, right_halo = pl.ds(0, HALO), pl.ds(HALO + columns, HALO)

    def halo_pieces(edge, halo, side):
        yield 0, [
            (field.at[0, :, edge, half[h]], raw_u.at[f, h, :, halo])
            for f, field in enumerate((u_prev, u_now))
            for h in range(2)
        ]
        yield 1, [(velocity.at[0, edge, half[h]], raw_v.at[h, halo]) for h in range(2)]
        yield 2, [
            (field.at[0, :, edge, half[h]], raw_q.at[f, h, :, halo])
            for f, field in enumerate((adj_after, adj_last))
            for h in range(2)
        ]
        yield 3, [
            (field.at[0, :, edge, half[0]], raw_b.at[f, :, halo])
            for f, field in enumerate((born_prev, born_now))
        ]
        yield 4, [(receivers, rec.at[side])]
        yield 5, [(observed.at[0], obs.at[side])]

    def halo_refs(group, edge_side):
        halo = (left_halo, right_halo)[edge_side]
        side = (0, 2)[edge_side]
        return (
            raw_u.at[:, :, :, halo],
            raw_v.at[:, halo],
            raw_q.at[:, :, :, halo],
            raw_b.at[:, :, halo],
            rec.at[side],
            obs.at[side],
        )[group]

    def send_halo(direction, groups):
        edge, halo, side = (
            (left_edge, right_halo, 2),
            (right_edge, left_halo, 0),
        )[direction]
        neighbour = (p - 1, p + 1)[direction]
        for group, pieces in halo_pieces(edge, halo, side):
            if group not in groups:
                continue
            for src, dst in pieces:
                pltpu.make_async_remote_copy(
                    src_ref=src,
                    dst_ref=dst,
                    send_sem=halo_send.at[direction, group],
                    recv_sem=halo_recv.at[direction, group],
                    device_id={"box": neighbour},
                    device_id_type=MESH,
                ).start()

    def send_halos(groups):
        @pl.when(p > 0)
        def _():
            send_halo(0, groups)

        @pl.when(p < last)
        def _():
            send_halo(1, groups)

    send_halos((0, 1))
    box_exchange(tile_out, tile_in, p, 0)
    send_halos((2, 3, 4, 5))

    blank = jnp.zeros((shots, LANES), F32)
    for pad in (0, ext + 1):
        for level in range(2):
            wave_b[level, pad] = blank
        for level in range(steps):
            adj_m[level, pad] = blank
    for c in (0, 1, ext - 2, ext - 1):
        image[c] = blank
    for back in (back_i, back_d, back_s):
        for place in (0, spare + n_box):
            back[pl.ds(place, spare)] = jnp.zeros((spare,) + back.shape[1:], F32)

    def halo_arrived(group):
        @pl.when(p < last)
        def _():
            wait_bytes(halo_refs(group, 1), halo_recv.at[0, group])

        @pl.when(p > 0)
        def _():
            wait_bytes(halo_refs(group, 0), halo_recv.at[1, group])

    def halo_sent(group):
        @pl.when(p > 0)
        def _():
            wait_bytes(halo_refs(group, 1), halo_send.at[0, group])

        @pl.when(p < last)
        def _():
            wait_bytes(halo_refs(group, 0), halo_send.at[1, group])

    lane = lax.broadcasted_iota(jnp.int32, (shots, LANES), 1)
    at_top = lane == 0
    at_bottom = lane == LANES - 1
    shot_row = lax.broadcasted_iota(jnp.int32, (shots, LANES), 0)
    first_cell = (p * columns - HALO) * depth

    def by_columns(raw, working, start, count):
        def move(c, carry):
            working[start + c + 1] = column_of(raw, start + c)
            return carry

        lax.fori_loop(0, count, move, 0, unroll=min(count, 16))

    def widen(start, count):
        for h in range(2):

            def spread(c, carry):
                speed[h, start + c] = jnp.broadcast_to(
                    raw_v[h, pl.ds(start + c, 1), :], (shots, LANES)
                )
                return carry

            lax.fori_loop(0, count, spread, 0, unroll=min(count, 16))

    for copy in load_s:
        copy.wait()
    source_cell = jnp.zeros((shots, LANES), jnp.int32)
    pulses = [jnp.zeros((shots, LANES), F32) for _ in range(steps)]
    for s in range(shots):
        source_cell = jnp.where(shot_row == s, sources_smem[0, s], source_cell)
        for t in range(steps):
            pulses[t] = jnp.where(shot_row == s, wavelet_smem[0, t, s], pulses[t])
    source_cell = source_cell - first_cell - lane

    def blocks(body, start, stop, unroll):
        count = -(-(stop - start) // BLOCK)

        def step(i, carry):
            body(jnp.minimum(start + i * BLOCK, stop - BLOCK), i)
            return carry

        lax.fori_loop(0, count, step, 0, unroll=unroll if count % unroll == 0 else 1)

    def turn(x, by):
        return pltpu.roll(x, by, axis=2)

    def around(wave, c):
        wide = wave[pl.ds(c, BLOCK + 2)]
        return wide[1 : BLOCK + 1], wide[:BLOCK] + wide[2:]

    def lap_both(wave, level, c):
        pairs = [around(wave.at[level, h], c) for h in range(2)]
        n = [pair[0] for pair in pairs]
        down = [turn(n[h], 1) for h in range(2)]
        up = [turn(n[h], LANES - 1) for h in range(2)]
        shallow = [jnp.where(at_top, 0.0, down[0]), jnp.where(at_top, down[0], down[1])]
        deep = [jnp.where(at_bottom, up[1], up[0]), jnp.where(at_bottom, 0.0, up[1])]
        laps = [pairs[h][1] + (shallow[h] + deep[h]) - 4.0 * n[h] for h in range(2)]
        return n, laps

    def lap_top(wave, level, c, closed):
        n, sides = around(wave.at[level], c)
        shallow = jnp.where(at_top, 0.0, turn(n, 1))
        deep = turn(n, LANES - 1)
        if closed:
            deep = jnp.where(at_bottom, 0.0, deep)
        return n, sides + (shallow + deep) - 4.0 * n

    def store_rows(slab, kind, i, block):
        for r in range(BLOCK):
            row = jnp.sum(block[r], axis=0, keepdims=True)
            j = i * (BLOCK // 2) + r // 2
            slab[j, kind, pl.ds(r % 2, 1), :] = row
            slab[j + n_box, kind, pl.ds(r % 2, 1), :] = row

    turned = lax.rem(n_box - rotation, n_box)

    def to_owners(slab, staged, back, sem):
        staged[...] = slab[pl.ds(turned, n_box)]
        back[spare + p] = staged[p]
        box_exchange(staged, back, spare + p, sem)

    def from_boxes(back, aligned, sem):
        box_arrived(back, sem)
        aligned[...] = back[pl.ds(spare - first_round, rounds)]

    def shot_exchange(src_of, landing, sem):
        def send(k, carry):
            s = lax.rem(g + k, n_shot)
            pltpu.make_async_remote_copy(
                src_ref=src_of(s),
                dst_ref=landing,
                send_sem=shot_send.at[sem],
                recv_sem=shot_recv.at[sem],
                device_id={"shot": s},
                device_id_type=MESH,
            ).start()
            return carry

        lax.fori_loop(1, n_shot, send, 0)

    def to_all(aligned, gathered, sem):
        shot_exchange(lambda s: aligned, gathered.at[g], sem)
        gathered[g] = aligned[...]

    mine = pl.ds(g * share, share)
    others = pl.ds(0, (n_shot - 1) * share)
    cell_step = lax.broadcasted_iota(jnp.int32, (BLOCK, shots, LANES), 0) * depth

    def advance(t, c):
        n, laps = lap_both(wave_u, t + 1, c)
        for h in range(2):
            offset = (source_cell - (c * depth + h * LANES))[None]
            a = speed[h, pl.ds(c, BLOCK)] * laps[h] + jnp.where(
                offset == cell_step, pulses[t][None], 0.0
            )
            accel[t, h, pl.ds(c, BLOCK)] = a
            if t < steps - 1:
                wave_u[t + 2, h, pl.ds(c + 1, BLOCK)] = (
                    (n[h] + n[h]) - wave_u[t, h, pl.ds(c + 1, BLOCK)]
                ) + a

    for copy in load_u + load_v:
        copy.wait()
    widen(HALO, columns)
    for h in range(2):
        for level in range(2):
            by_columns(raw_u.at[level, h], wave_u.at[level, h], HALO, columns)
    for t in range(steps):
        blocks(lambda c, i: advance(t, c), HALO + 1 + t, HALO + columns - 1 - t, 2)
    halo_arrived(0)
    halo_arrived(1)
    for start in (0, HALO + columns):
        widen(start, HALO)
        for h in range(2):
            for level in range(2):
                by_columns(raw_u.at[level, h], wave_u.at[level, h], start, HALO)
    for t in range(steps):
        advance(t, 1 + t)
        advance(t, HALO + columns - 1 - t)

    def brighten(c, i):
        for h in range(2):
            a = [accel[t, h, pl.ds(c, BLOCK)] for t in range(steps)]
            store_rows(slab_i, h, i, sum(x * x for x in a))

    blocks(brighten, HALO, HALO + columns, 2)
    to_owners(slab_i, stage_i, back_i, 1)

    for copy in load_q:
        copy.wait()
    halo_arrived(2)
    for h in range(2):
        for level in range(2):
            by_columns(raw_q.at[level, h], wave_q.at[level, h], 0, ext)

    def retreat(k, c):
        n, laps = lap_both(wave_q, k + 1, c)
        for h in range(2):
            wave_q[k + 2, h, pl.ds(c + 1, BLOCK)] = (
                (n[h] + n[h]) - wave_q[k, h, pl.ds(c + 1, BLOCK)]
            ) + speed[h, pl.ds(c, BLOCK)] * laps[h]

    for k in range(steps):
        blocks(lambda c, i: retreat(k, c), HALO - 3 + k, HALO + columns + 3 - k, 3)

    def correlate(c, i):
        products = [
            sum(
                wave_q[steps + 1 - t, h, pl.ds(c + 1, BLOCK)] * accel[t, h, pl.ds(c, BLOCK)]
                for t in range(steps)
            )
            for h in range(2)
        ]
        store_rows(slab_d, 0, i, products[1])
        grad_part[pl.ds(i * BLOCK, BLOCK)] = products[0]

    blocks(correlate, HALO, HALO + columns, 2)
    to_owners(slab_d, stage_d, back_d, 2)

    for copy in load_r + load_b:
        copy.wait()
    halo_arrived(4)
    halo_arrived(5)
    halo_arrived(3)
    by_columns(raw_b.at[0], wave_b.at[0], 0, ext)
    by_columns(raw_b.at[1], wave_b.at[1], 0, ext)
    beside = HALO // 2
    heard = (
        [(0, n_rec - beside + r) for r in range(beside)]
        + [(1, r) for r in range(n_rec)]
        + [(2, r) for r in range(beside)]
    )
    for side in range(3):
        for t in range(steps):
            by_step[side, t] = obs[side, :, t, :]
    cells = [jnp.broadcast_to(rec[side], (shots, n_rec)) for side in range(3)]
    data = [[by_step[side, t] for t in range(steps)] for side in range(3)]
    for slot, (side, r) in enumerate(heard):
        cell = jnp.broadcast_to(cells[side][:, r : r + 1], (shots, LANES)) - first_cell - lane
        for t in range(steps):
            target[t, slot] = jnp.broadcast_to(data[side][t][:, r : r + 1], (shots, LANES))
        for w in range(2):
            c = 2 * slot + w
            mask[c] = jnp.where(cell == c * depth, 1.0, 0.0)

    box_arrived(tile_in, 0)
    for j in range(n_box + 6):
        owner = lax.rem(rotation + j - 3 + n_box, n_box)
        tile = tile_in[owner, j // n_box]
        for w in range(2):
            image[HALO - 6 + 2 * j + w] = jnp.broadcast_to(tile[w : w + 1], (shots, LANES))

    def scatter_wave(t, c):
        n, lap = lap_top(wave_b, t + 1, c, False)
        b = (
            ((n + n) - wave_b[t, pl.ds(c + 1, BLOCK)])
            + speed[0, pl.ds(c, BLOCK)] * lap
            + image[pl.ds(c, BLOCK)] * accel[t, 0, pl.ds(c, BLOCK)]
        )
        if t < steps - 1:
            wave_b[t + 2, pl.ds(c + 1, BLOCK)] = b
        recorded = target[t, pl.ds(c // 2, BLOCK // 2)]
        recorded = jnp.broadcast_to(
            recorded[:, None], (BLOCK // 2, 2, shots, LANES)
        ).reshape(BLOCK, shots, LANES)
        adj_m[t, pl.ds(c + 1, BLOCK)] = mask[pl.ds(c, BLOCK)] * (b - recorded)

    for t in range(steps):
        inset = 0 if t < 2 else HALO // 2
        count = (ext - 2 * inset) // BLOCK
        for i in range(count):
            scatter_wave(t, inset + i * BLOCK)

    from_boxes(back_i, aligned_i, 1)
    reduce_i[g] = aligned_i[mine]
    shot_exchange(lambda s: aligned_i.at[pl.ds(s * share, share)], reduce_i.at[g], 0)

    def misfit_wave(t):
        return adj_m.at[t] if t == steps - 1 else adj_r.at[t]

    def residual(t, c):
        n, sides = around(misfit_wave(t + 1), c)
        shallow = jnp.where(at_top, 0.0, turn(n, 1))
        deep = jnp.where(at_bottom, 0.0, turn(n, LANES - 1))
        lap = sides + (shallow + deep) - 4.0 * n
        q = (n + n) + speed[0, pl.ds(c, BLOCK)] * lap + adj_m[t, pl.ds(c + 1, BLOCK)]
        if t + 2 < steps:
            q = q - misfit_wave(t + 2)[pl.ds(c + 1, BLOCK)]
        adj_r[t, pl.ds(c + 1, BLOCK)] = q

    for t in reversed(range(steps - 1)):
        start, stop = HALO - t, HALO + columns + t
        count = -(-(stop - start) // BLOCK)
        for i in range(count):
            residual(t, min(start + i * BLOCK, stop - BLOCK))

    def correlate_late(c, i):
        total = grad_part[pl.ds(i * BLOCK, BLOCK)] + sum(
            misfit_wave(t)[pl.ds(c + 1, BLOCK)] * accel[t, 0, pl.ds(c, BLOCK)]
            for t in range(steps)
        )
        store_rows(slab_s, 0, i, total)

    for i in range(columns // BLOCK):
        correlate_late(HALO + i * BLOCK, i)
    to_owners(slab_s, stage_s, back_s, 3)

    from_boxes(back_d, aligned_d, 2)
    to_all(aligned_d, gather_d, 1)

    wait_bytes(reduce_i.at[pl.ds(0, n_shot - 1)], shot_recv.at[0])
    light = reduce_i[0]
    for s in range(1, n_shot):
        light = light + reduce_i[s]
    scale[mine] = jnp.sqrt(light + damping)
    shot_exchange(lambda s: scale.at[mine], scale.at[mine], 2)

    from_boxes(back_s, aligned_s, 3)
    to_all(aligned_s, gather_s, 3)

    def total_of(gathered, sem):
        wait_bytes(gathered.at[pl.ds(0, n_shot - 1)], shot_recv.at[sem])
        total = gathered[0, :, 0]
        for s in range(1, n_shot):
            total = total + gathered[s, :, 0]
        return total

    deep_total = total_of(gather_d, 1)
    wait_bytes(scale.at[others], shot_recv.at[2])
    out[:, 0, :, half[1]] = deep_total / scale[:, 1]
    out[:, 0, :, half[0]] = total_of(gather_s, 3) / scale[:, 0]

    for group in range(6):
        halo_sent(group)
    box_sent(tile_out, 0)
    box_sent(stage_i, 1)
    box_sent(stage_d, 2)
    box_sent(stage_s, 3)
    wait_bytes(aligned_i.at[others], shot_send.at[0])
    wait_bytes(gather_d.at[pl.ds(0, n_shot - 1)], shot_send.at[1])
    wait_bytes(scale.at[others], shot_send.at[2])
    wait_bytes(gather_s.at[pl.ds(0, n_shot - 1)], shot_send.at[3])


def on_device(
    n_box,
    n_shot,
    u_prev,
    u_now,
    born_prev,
    born_now,
    adj_after,
    adj_last,
    velocity,
    wavelet,
    sources,
    receivers,
    observed,
    first_tile,
    reflectivity,
):
    shots, columns, depth = u_now.shape[1:]
    steps = wavelet.shape[2]
    n_rec = receivers.shape[1]
    rounds = reflectivity.shape[0]
    ext = columns + 2 * HALO
    spare = rounds - n_box
    share = rounds // n_shot

    def vmem(*dims):
        return pltpu.VMEM(dims, F32)

    plane = (shots, LANES)
    tile = (2, LANES)
    scratch = [
        pltpu.SMEM(sources.shape, jnp.int32),
        pltpu.SMEM((1, steps, shots), F32),
        vmem(2, 2, shots, ext, LANES),
        vmem(2, 2, shots, ext, LANES),
        vmem(2, shots, ext, LANES),
        vmem(2, ext, LANES),
        pltpu.VMEM((3, 1, n_rec), jnp.int32),
        vmem(3, shots, steps, n_rec),
        vmem(rounds + 2, *tile),
        vmem(steps + 1, 2, ext + 2, *plane),
        vmem(steps, 2, ext, *plane),
        vmem(steps + 1, ext + 2, *plane),
        vmem(steps + 2, 2, ext + 2, *plane),
        vmem(columns, *plane),
        vmem(steps, ext + 2, *plane),
        vmem(2, ext, *plane),
        vmem(ext, *plane),
        vmem(ext, *plane),
        vmem(steps, ext // 2, *plane),
        vmem(3, steps, shots, n_rec),
        vmem(steps - 1, ext + 2, *plane),
        vmem(n_box, 2, *tile),
        vmem(n_box, 2, *tile),
        vmem(2 * n_box, 2, *tile),
        vmem(2 * n_box, 1, *tile),
        vmem(2 * n_box, 1, *tile),
        vmem(n_box, 2, *tile),
        vmem(n_box, 1, *tile),
        vmem(n_box, 1, *tile),
        vmem(n_box + 2 * spare, 2, *tile),
        vmem(n_box + 2 * spare, 1, *tile),
        vmem(n_box + 2 * spare, 1, *tile),
        vmem(rounds, 2, *tile),
        vmem(rounds, 1, *tile),
        vmem(rounds, 1, *tile),
        vmem(n_shot, share, 2, *tile),
        vmem(n_shot, rounds, 1, *tile),
        vmem(n_shot, rounds, 1, *tile),
        vmem(rounds, 2, *tile),
        pltpu.SemaphoreType.DMA((19,)),
        pltpu.SemaphoreType.DMA((2, 6)),
        pltpu.SemaphoreType.DMA((2, 6)),
        pltpu.SemaphoreType.DMA((4,)),
        pltpu.SemaphoreType.DMA((4,)),
        pltpu.SemaphoreType.DMA((4,)),
        pltpu.SemaphoreType.DMA((4,)),
    ]
    hbm = pl.BlockSpec(memory_space=pltpu.HBM)
    return pl.pallas_call(
        functools.partial(kernel, n_box, n_shot),
        out_shape=jax.ShapeDtypeStruct(reflectivity.shape, F32),
        in_specs=[pl.BlockSpec(memory_space=pltpu.SMEM)] + [hbm] * 12,
        out_specs=pl.BlockSpec(memory_space=pltpu.VMEM),
        scratch_shapes=scratch,
        compiler_params=pltpu.CompilerParams(
            collective_id=0, has_side_effects=True, vmem_limit_bytes=60 * 1024 * 1024
        ),
    )(
        first_tile,
        sources,
        jnp.transpose(wavelet, (0, 2, 1)),
        u_prev,
        u_now,
        born_prev,
        born_now,
        adj_after,
        adj_last,
        velocity,
        receivers,
        observed,
        reflectivity,
    )


def solution(mesh):
    return jax.shard_map(
        functools.partial(on_device, mesh.shape["box"], mesh.shape["shot"]),
        mesh=mesh,
        in_specs=(
            P("shot", None, "box", None),
            P("shot", None, "box", None),
            P("shot", None, "box", None),
            P("shot", None, "box", None),
            P("shot", None, "box", None),
            P("shot", None, "box", None),
            P("shot", "box", None),
            P("shot", None, None),
            P("shot", None),
            P("shot", "box"),
            P("shot", None, None, "box"),
            P("shot"),
            P(None, "box", None, None),
        ),
        out_specs=P(None, "box", None, None),
        check_vma=False,
    )
```

```python
import functools

import jax
import jax.numpy as jnp
from jax import lax
from jax.experimental import pallas as pl
from jax.experimental.pallas import tpu as pltpu
from jax.sharding import PartitionSpec as P

damping = 1.0
LANES = 128
HALO = 8
BLOCK = 8
F32 = jnp.float32
MESH = pl.DeviceIdType.MESH


def wait_bytes(ref, sem):
    pltpu.make_async_copy(ref, ref, sem).wait()


def column_of(raw, c):
    shots, ext, lanes = raw.shape
    return raw.reshape(shots * ext, lanes)[pl.ds(c, shots, stride=ext), :]


def kernel(
    n_box,
    n_shot,
    first_tile,
    sources,
    wavelet,
    u_prev,
    u_now,
    born_prev,
    born_now,
    adj_after,
    adj_last,
    velocity,
    receivers,
    observed,
    reflectivity,
    out,
    sources_smem,
    wavelet_smem,
    raw_u,
    raw_q,
    raw_b,
    raw_v,
    rec,
    obs,
    refl,
    wave_u,
    accel,
    wave_b,
    wave_q,
    grad_part,
    adj_m,
    speed,
    image,
    mask,
    target,
    by_step,
    adj_r,
    tile_out,
    tile_in,
    slab_i,
    slab_d,
    slab_s,
    stage_i,
    stage_d,
    stage_s,
    back_i,
    back_d,
    back_s,
    aligned_i,
    aligned_d,
    aligned_s,
    reduce_i,
    reduce_d,
    gather_s,
    finished,
    load_sem,
    halo_send,
    halo_recv,
    box_send,
    box_recv,
    shot_send,
    shot_recv,
):
    shots, columns, depth = u_now.shape[1:]
    steps = wavelet_smem.shape[1]
    n_rec = receivers.shape[1]
    rounds = reflectivity.shape[0]
    ext = columns + 2 * HALO
    spare = rounds - n_box
    share = rounds // n_shot
    g = lax.axis_index("shot")
    p = lax.axis_index("box")
    last = n_box - 1

    barrier = pltpu.get_barrier_semaphore()

    def greet_box(k, carry):
        pl.semaphore_signal(
            barrier, inc=1, device_id={"box": lax.rem(p + k, n_box)}, device_id_type=MESH
        )
        return carry

    def greet_shot(k, carry):
        pl.semaphore_signal(
            barrier, inc=1, device_id={"shot": lax.rem(g + k, n_shot)}, device_id_type=MESH
        )
        return carry

    lax.fori_loop(1, n_box, greet_box, 0)
    lax.fori_loop(1, n_shot, greet_shot, 0)

    loads = []

    def load(src, dst):
        copy = pltpu.make_async_copy(src, dst, load_sem.at[len(loads)])
        copy.start()
        loads.append(copy)
        return copy

    half = [pl.ds(0, LANES), pl.ds(LANES, LANES)]
    own = pl.ds(HALO, columns)
    load_refl = load(reflectivity.at[:, 0, :, half[0]], refl.at[pl.ds(1, rounds)])
    load_v = [load(velocity.at[0, :, half[h]], raw_v.at[h, own]) for h in range(2)]
    load_u = [
        load(field.at[0, :, :, half[h]], raw_u.at[f, h, :, own])
        for f, field in enumerate((u_prev, u_now))
        for h in range(2)
    ]
    load_s = [load(sources, sources_smem), load(wavelet, wavelet_smem)]
    load_r = [load(receivers, rec.at[1]), load(observed.at[0], obs.at[1])]
    load_q = [
        load(field.at[0, :, :, half[h]], raw_q.at[f, h, :, own])
        for f, field in enumerate((adj_after, adj_last))
        for h in range(2)
    ]
    load_b = [
        load(field.at[0, :, :, half[0]], raw_b.at[f, :, own])
        for f, field in enumerate((born_prev, born_now))
    ]

    for edge, place, side in ((0, 0, 0), (last, HALO + columns, 2)):

        @pl.when(p == edge)
        def _():
            strip = pl.ds(place, HALO)
            raw_v[:, strip] = jnp.zeros((2, HALO, LANES), F32)
            raw_b[:, :, strip] = jnp.zeros((2, shots, HALO, LANES), F32)
            for f in range(2):
                raw_u[f, :, :, strip] = jnp.zeros((2, shots, HALO, LANES), F32)
                raw_q[f, :, :, strip] = jnp.zeros((2, shots, HALO, LANES), F32)
            rec[side] = jnp.full((1, n_rec), -1, jnp.int32)
            obs[side] = jnp.zeros((shots, steps, n_rec), F32)

    refl[0] = jnp.zeros((2, LANES), F32)
    refl[rounds + 1] = jnp.zeros((2, LANES), F32)

    first = first_tile[0]
    rotation = lax.rem(first, n_box)
    first_round = lax.div(first, n_box) + (p < rotation).astype(jnp.int32)
    lead = lax.rem(p - first + 3 + 64 * n_box, n_box)
    source_round = lax.div(first - 3 + lead - p + 64 * n_box, n_box) - 64

    load_refl.wait()
    tile_out[:, 0] = refl[pl.ds(source_round + 1, n_box)]
    tile_out[:, 1] = refl[pl.ds(source_round + 2, n_box)]
    tile_in[p] = tile_out[p]

    pl.semaphore_wait(barrier, n_box - 1 + n_shot - 1)

    def box_exchange(staged, landing, place, sem):
        def send(k, carry):
            target_device = lax.rem(p + k, n_box)
            pltpu.make_async_remote_copy(
                src_ref=staged.at[target_device],
                dst_ref=landing.at[place],
                send_sem=box_send.at[sem],
                recv_sem=box_recv.at[sem],
                device_id={"box": target_device},
                device_id_type=MESH,
            ).start()
            return carry

        lax.fori_loop(1, n_box, send, 0)

    def box_sent(staged, sem):
        wait_bytes(staged.at[pl.ds(0, n_box - 1)], box_send.at[sem])

    def box_arrived(landing, sem):
        wait_bytes(landing.at[pl.ds(0, n_box - 1)], box_recv.at[sem])

    left_edge, right_edge = pl.ds(0, HALO), pl.ds(columns - HALO, HALO)
    left_halo, right_halo = pl.ds(0, HALO), pl.ds(HALO + columns, HALO)

    def halo_pieces(edge, halo, side):
        yield 0, [
            (field.at[0, :, edge, half[h]], raw_u.at[f, h, :, halo])
            for f, field in enumerate((u_prev, u_now))
            for h in range(2)
        ]
        yield 1, [(velocity.at[0, edge, half[h]], raw_v.at[h, halo]) for h in range(2)]
        yield 2, [
            (field.at[0, :, edge, half[h]], raw_q.at[f, h, :, halo])
            for f, field in enumerate((adj_after, adj_last))
            for h in range(2)
        ]
        yield 3, [
            (field.at[0, :, edge, half[0]], raw_b.at[f, :, halo])
            for f, field in enumerate((born_prev, born_now))
        ]
        yield 4, [(receivers, rec.at[side])]
        yield 5, [(observed.at[0], obs.at[side])]

    def halo_refs(group, edge_side):
        halo = (left_halo, right_halo)[edge_side]
        side = (0, 2)[edge_side]
        return (
            raw_u.at[:, :, :, halo],
            raw_v.at[:, halo],
            raw_q.at[:, :, :, halo],
            raw_b.at[:, :, halo],
            rec.at[side],
            obs.at[side],
        )[group]

    def send_halo(direction, groups):
        edge, halo, side = (
            (left_edge, right_halo, 2),
            (right_edge, left_halo, 0),
        )[direction]
        neighbour = (p - 1, p + 1)[direction]
        for group, pieces in halo_pieces(edge, halo, side):
            if group not in groups:
                continue
            for src, dst in pieces:
                pltpu.make_async_remote_copy(
                    src_ref=src,
                    dst_ref=dst,
                    send_sem=halo_send.at[direction, group],
                    recv_sem=halo_recv.at[direction, group],
                    device_id={"box": neighbour},
                    device_id_type=MESH,
                ).start()

    def send_halos(groups):
        @pl.when(p > 0)
        def _():
            send_halo(0, groups)

        @pl.when(p < last)
        def _():
            send_halo(1, groups)

    send_halos((0, 1))
    box_exchange(tile_out, tile_in, p, 0)
    send_halos((2, 3, 4, 5))

    blank = jnp.zeros((shots, LANES), F32)
    for pad in (0, ext + 1):
        for level in range(2):
            wave_b[level, pad] = blank
        for level in range(steps):
            adj_m[level, pad] = blank
    for c in (0, 1, ext - 2, ext - 1):
        image[c] = blank
    for back in (back_i, back_d, back_s):
        for place in (0, spare + n_box):
            back[pl.ds(place, spare)] = jnp.zeros((spare,) + back.shape[1:], F32)

    def halo_arrived(group):
        @pl.when(p < last)
        def _():
            wait_bytes(halo_refs(group, 1), halo_recv.at[0, group])

        @pl.when(p > 0)
        def _():
            wait_bytes(halo_refs(group, 0), halo_recv.at[1, group])

    def halo_sent(group):
        @pl.when(p > 0)
        def _():
            wait_bytes(halo_refs(group, 1), halo_send.at[0, group])

        @pl.when(p < last)
        def _():
            wait_bytes(halo_refs(group, 0), halo_send.at[1, group])

    lane = lax.broadcasted_iota(jnp.int32, (shots, LANES), 1)
    at_top = lane == 0
    at_bottom = lane == LANES - 1
    shot_row = lax.broadcasted_iota(jnp.int32, (shots, LANES), 0)
    first_cell = (p * columns - HALO) * depth

    def by_columns(raw, working, start, count):
        def move(c, carry):
            working[start + c + 1] = column_of(raw, start + c)
            return carry

        lax.fori_loop(0, count, move, 0, unroll=min(count, 16))

    def widen(start, count):
        for h in range(2):

            def spread(c, carry):
                speed[h, start + c] = jnp.broadcast_to(
                    raw_v[h, pl.ds(start + c, 1), :], (shots, LANES)
                )
                return carry

            lax.fori_loop(0, count, spread, 0, unroll=min(count, 16))

    for copy in load_s:
        copy.wait()
    source_cell = jnp.zeros((shots, LANES), jnp.int32)
    pulses = [jnp.zeros((shots, LANES), F32) for _ in range(steps)]
    for s in range(shots):
        source_cell = jnp.where(shot_row == s, sources_smem[0, s], source_cell)
        for t in range(steps):
            pulses[t] = jnp.where(shot_row == s, wavelet_smem[0, t, s], pulses[t])
    source_cell = source_cell - first_cell - lane

    def blocks(body, start, stop, unroll):
        count = -(-(stop - start) // BLOCK)

        def step(i, carry):
            body(jnp.minimum(start + i * BLOCK, stop - BLOCK), i)
            return carry

        lax.fori_loop(0, count, step, 0, unroll=unroll if count % unroll == 0 else 1)

    def turn(x, by):
        return pltpu.roll(x, by, axis=2)

    def around(wave, c):
        wide = wave[pl.ds(c, BLOCK + 2)]
        return wide[1 : BLOCK + 1], wide[:BLOCK] + wide[2:]

    def lap_both(wave, level, c):
        pairs = [around(wave.at[level, h], c) for h in range(2)]
        n = [pair[0] for pair in pairs]
        down = [turn(n[h], 1) for h in range(2)]
        up = [turn(n[h], LANES - 1) for h in range(2)]
        shallow = [jnp.where(at_top, 0.0, down[0]), jnp.where(at_top, down[0], down[1])]
        deep = [jnp.where(at_bottom, up[1], up[0]), jnp.where(at_bottom, 0.0, up[1])]
        laps = [pairs[h][1] + (shallow[h] + deep[h]) - 4.0 * n[h] for h in range(2)]
        return n, laps

    def lap_top(wave, level, c, closed):
        n, sides = around(wave.at[level], c)
        shallow = jnp.where(at_top, 0.0, turn(n, 1))
        deep = turn(n, LANES - 1)
        if closed:
            deep = jnp.where(at_bottom, 0.0, deep)
        return n, sides + (shallow + deep) - 4.0 * n

    def store_rows(slab, kind, i, block):
        for r in range(BLOCK):
            row = jnp.sum(block[r], axis=0, keepdims=True)
            j = i * (BLOCK // 2) + r // 2
            slab[j, kind, pl.ds(r % 2, 1), :] = row
            slab[j + n_box, kind, pl.ds(r % 2, 1), :] = row

    turned = lax.rem(n_box - rotation, n_box)

    def to_owners(slab, staged, back, sem):
        staged[...] = slab[pl.ds(turned, n_box)]
        back[spare + p] = staged[p]
        box_exchange(staged, back, spare + p, sem)

    def from_boxes(back, aligned, sem):
        box_arrived(back, sem)
        aligned[...] = back[pl.ds(spare - first_round, rounds)]

    def shot_exchange(src_of, landing, sem):
        def send(k, carry):
            s = lax.rem(g + k, n_shot)
            pltpu.make_async_remote_copy(
                src_ref=src_of(s),
                dst_ref=landing,
                send_sem=shot_send.at[sem],
                recv_sem=shot_recv.at[sem],
                device_id={"shot": s},
                device_id_type=MESH,
            ).start()
            return carry

        lax.fori_loop(1, n_shot, send, 0)

    def to_all(aligned, gathered, sem):
        shot_exchange(lambda s: aligned, gathered.at[g], sem)
        gathered[g] = aligned[...]

    mine = pl.ds(g * share, share)
    others = pl.ds(0, (n_shot - 1) * share)
    cell_step = lax.broadcasted_iota(jnp.int32, (BLOCK, shots, LANES), 0) * depth

    def advance(t, c):
        n, laps = lap_both(wave_u, t + 1, c)
        for h in range(2):
            offset = (source_cell - (c * depth + h * LANES))[None]
            a = speed[h, pl.ds(c, BLOCK)] * laps[h] + jnp.where(
                offset == cell_step, pulses[t][None], 0.0
            )
            accel[t, h, pl.ds(c, BLOCK)] = a
            if t < steps - 1:
                wave_u[t + 2, h, pl.ds(c + 1, BLOCK)] = (
                    (n[h] + n[h]) - wave_u[t, h, pl.ds(c + 1, BLOCK)]
                ) + a

    for copy in load_u + load_v:
        copy.wait()
    widen(HALO, columns)
    for h in range(2):
        for level in range(2):
            by_columns(raw_u.at[level, h], wave_u.at[level, h], HALO, columns)
    for t in range(steps):
        blocks(lambda c, i: advance(t, c), HALO + 1 + t, HALO + columns - 1 - t, 2)
    halo_arrived(0)
    halo_arrived(1)
    for start in (0, HALO + columns):
        widen(start, HALO)
        for h in range(2):
            for level in range(2):
                by_columns(raw_u.at[level, h], wave_u.at[level, h], start, HALO)
    for t in range(steps):
        advance(t, 1 + t)
        advance(t, HALO + columns - 1 - t)

    def brighten(c, i):
        for h in range(2):
            a = [accel[t, h, pl.ds(c, BLOCK)] for t in range(steps)]
            store_rows(slab_i, h, i, sum(x * x for x in a))

    blocks(brighten, HALO, HALO + columns, 2)
    to_owners(slab_i, stage_i, back_i, 1)

    for copy in load_q:
        copy.wait()
    halo_arrived(2)
    for h in range(2):
        for level in range(2):
            by_columns(raw_q.at[level, h], wave_q.at[level, h], 0, ext)

    def retreat(k, c):
        n, laps = lap_both(wave_q, k + 1, c)
        for h in range(2):
            wave_q[k + 2, h, pl.ds(c + 1, BLOCK)] = (
                (n[h] + n[h]) - wave_q[k, h, pl.ds(c + 1, BLOCK)]
            ) + speed[h, pl.ds(c, BLOCK)] * laps[h]

    for k in range(steps):
        blocks(lambda c, i: retreat(k, c), HALO - 3 + k, HALO + columns + 3 - k, 3)

    def correlate(c, i):
        products = [
            sum(
                wave_q[steps + 1 - t, h, pl.ds(c + 1, BLOCK)] * accel[t, h, pl.ds(c, BLOCK)]
                for t in range(steps)
            )
            for h in range(2)
        ]
        store_rows(slab_d, 0, i, products[1])
        grad_part[pl.ds(i * BLOCK, BLOCK)] = products[0]

    blocks(correlate, HALO, HALO + columns, 2)
    to_owners(slab_d, stage_d, back_d, 2)

    for copy in load_r + load_b:
        copy.wait()
    halo_arrived(4)
    halo_arrived(5)
    halo_arrived(3)
    by_columns(raw_b.at[0], wave_b.at[0], 0, ext)
    by_columns(raw_b.at[1], wave_b.at[1], 0, ext)
    beside = HALO // 2
    heard = (
        [(0, n_rec - beside + r) for r in range(beside)]
        + [(1, r) for r in range(n_rec)]
        + [(2, r) for r in range(beside)]
    )
    for side in range(3):
        for t in range(steps):
            by_step[side, t] = obs[side, :, t, :]
    cells = [jnp.broadcast_to(rec[side], (shots, n_rec)) for side in range(3)]
    data = [[by_step[side, t] for t in range(steps)] for side in range(3)]
    for slot, (side, r) in enumerate(heard):
        cell = jnp.broadcast_to(cells[side][:, r : r + 1], (shots, LANES)) - first_cell - lane
        for t in range(steps):
            target[t, slot] = jnp.broadcast_to(data[side][t][:, r : r + 1], (shots, LANES))
        for w in range(2):
            c = 2 * slot + w
            mask[c] = jnp.where(cell == c * depth, 1.0, 0.0)

    box_arrived(tile_in, 0)
    for j in range(n_box + 6):
        owner = lax.rem(rotation + j - 3 + n_box, n_box)
        tile = tile_in[owner, j // n_box]
        for w in range(2):
            image[HALO - 6 + 2 * j + w] = jnp.broadcast_to(tile[w : w + 1], (shots, LANES))

    def scatter_wave(t, c):
        n, lap = lap_top(wave_b, t + 1, c, False)
        b = (
            ((n + n) - wave_b[t, pl.ds(c + 1, BLOCK)])
            + speed[0, pl.ds(c, BLOCK)] * lap
            + image[pl.ds(c, BLOCK)] * accel[t, 0, pl.ds(c, BLOCK)]
        )
        if t < steps - 1:
            wave_b[t + 2, pl.ds(c + 1, BLOCK)] = b
        recorded = target[t, pl.ds(c // 2, BLOCK // 2)]
        recorded = jnp.broadcast_to(
            recorded[:, None], (BLOCK // 2, 2, shots, LANES)
        ).reshape(BLOCK, shots, LANES)
        adj_m[t, pl.ds(c + 1, BLOCK)] = mask[pl.ds(c, BLOCK)] * (b - recorded)

    for t in range(steps):
        inset = 0 if t < 2 else HALO // 2
        count = (ext - 2 * inset) // BLOCK
        for i in range(count):
            scatter_wave(t, inset + i * BLOCK)

    from_boxes(back_i, aligned_i, 1)
    reduce_i[g] = aligned_i[mine]
    shot_exchange(lambda s: aligned_i.at[pl.ds(s * share, share)], reduce_i.at[g], 0)

    def misfit_wave(t):
        return adj_m.at[t] if t == steps - 1 else adj_r.at[t]

    def residual(t, c):
        n, sides = around(misfit_wave(t + 1), c)
        shallow = jnp.where(at_top, 0.0, turn(n, 1))
        deep = jnp.where(at_bottom, 0.0, turn(n, LANES - 1))
        lap = sides + (shallow + deep) - 4.0 * n
        q = (n + n) + speed[0, pl.ds(c, BLOCK)] * lap + adj_m[t, pl.ds(c + 1, BLOCK)]
        if t + 2 < steps:
            q = q - misfit_wave(t + 2)[pl.ds(c + 1, BLOCK)]
        adj_r[t, pl.ds(c + 1, BLOCK)] = q

    for t in reversed(range(steps - 1)):
        start, stop = HALO - t, HALO + columns + t
        count = -(-(stop - start) // BLOCK)
        for i in range(count):
            residual(t, min(start + i * BLOCK, stop - BLOCK))

    def correlate_late(c, i):
        total = grad_part[pl.ds(i * BLOCK, BLOCK)] + sum(
            misfit_wave(t)[pl.ds(c + 1, BLOCK)] * accel[t, 0, pl.ds(c, BLOCK)]
            for t in range(steps)
        )
        store_rows(slab_s, 0, i, total)

    for i in range(columns // BLOCK):
        correlate_late(HALO + i * BLOCK, i)
    to_owners(slab_s, stage_s, back_s, 3)

    from_boxes(back_d, aligned_d, 2)
    reduce_d[g] = aligned_d[mine]
    shot_exchange(lambda s: aligned_d.at[pl.ds(s * share, share)], reduce_d.at[g], 1)

    def total_of(gathered, sem):
        wait_bytes(gathered.at[pl.ds(0, n_shot - 1)], shot_recv.at[sem])
        total = gathered[0]
        for s in range(1, n_shot):
            total = total + gathered[s]
        return total

    light = jnp.sqrt(total_of(reduce_i, 0) + damping)

    from_boxes(back_s, aligned_s, 3)
    to_all(aligned_s, gather_s, 3)

    finished[mine, 1] = total_of(reduce_d, 1)[:, 0] / light[:, 1]
    finished[mine, 0] = light[:, 0]
    shot_exchange(lambda s: finished.at[mine], finished.at[mine], 2)

    shallow_total = total_of(gather_s, 3)[:, 0]
    wait_bytes(finished.at[others], shot_recv.at[2])
    out[:, 0, :, half[1]] = finished[:, 1]
    out[:, 0, :, half[0]] = shallow_total / finished[:, 0]

    for group in range(6):
        halo_sent(group)
    box_sent(tile_out, 0)
    box_sent(stage_i, 1)
    box_sent(stage_d, 2)
    box_sent(stage_s, 3)
    wait_bytes(aligned_i.at[others], shot_send.at[0])
    wait_bytes(aligned_d.at[others], shot_send.at[1])
    wait_bytes(finished.at[others], shot_send.at[2])
    wait_bytes(gather_s.at[pl.ds(0, n_shot - 1)], shot_send.at[3])


def on_device(
    n_box,
    n_shot,
    u_prev,
    u_now,
    born_prev,
    born_now,
    adj_after,
    adj_last,
    velocity,
    wavelet,
    sources,
    receivers,
    observed,
    first_tile,
    reflectivity,
):
    shots, columns, depth = u_now.shape[1:]
    steps = wavelet.shape[2]
    n_rec = receivers.shape[1]
    rounds = reflectivity.shape[0]
    ext = columns + 2 * HALO
    spare = rounds - n_box
    share = rounds // n_shot

    def vmem(*dims):
        return pltpu.VMEM(dims, F32)

    plane = (shots, LANES)
    tile = (2, LANES)
    scratch = [
        pltpu.SMEM(sources.shape, jnp.int32),
        pltpu.SMEM((1, steps, shots), F32),
        vmem(2, 2, shots, ext, LANES),
        vmem(2, 2, shots, ext, LANES),
        vmem(2, shots, ext, LANES),
        vmem(2, ext, LANES),
        pltpu.VMEM((3, 1, n_rec), jnp.int32),
        vmem(3, shots, steps, n_rec),
        vmem(rounds + 2, *tile),
        vmem(steps + 1, 2, ext + 2, *plane),
        vmem(steps, 2, ext, *plane),
        vmem(steps + 1, ext + 2, *plane),
        vmem(steps + 2, 2, ext + 2, *plane),
        vmem(columns, *plane),
        vmem(steps, ext + 2, *plane),
        vmem(2, ext, *plane),
        vmem(ext, *plane),
        vmem(ext, *plane),
        vmem(steps, ext // 2, *plane),
        vmem(3, steps, shots, n_rec),
        vmem(steps - 1, ext + 2, *plane),
        vmem(n_box, 2, *tile),
        vmem(n_box, 2, *tile),
        vmem(2 * n_box, 2, *tile),
        vmem(2 * n_box, 1, *tile),
        vmem(2 * n_box, 1, *tile),
        vmem(n_box, 2, *tile),
        vmem(n_box, 1, *tile),
        vmem(n_box, 1, *tile),
        vmem(n_box + 2 * spare, 2, *tile),
        vmem(n_box + 2 * spare, 1, *tile),
        vmem(n_box + 2 * spare, 1, *tile),
        vmem(rounds, 2, *tile),
        vmem(rounds, 1, *tile),
        vmem(rounds, 1, *tile),
        vmem(n_shot, share, 2, *tile),
        vmem(n_shot, share, 1, *tile),
        vmem(n_shot, rounds, 1, *tile),
        vmem(rounds, 2, *tile),
        pltpu.SemaphoreType.DMA((19,)),
        pltpu.SemaphoreType.DMA((2, 6)),
        pltpu.SemaphoreType.DMA((2, 6)),
        pltpu.SemaphoreType.DMA((4,)),
        pltpu.SemaphoreType.DMA((4,)),
        pltpu.SemaphoreType.DMA((4,)),
        pltpu.SemaphoreType.DMA((4,)),
    ]
    hbm = pl.BlockSpec(memory_space=pltpu.HBM)
    return pl.pallas_call(
        functools.partial(kernel, n_box, n_shot),
        out_shape=jax.ShapeDtypeStruct(reflectivity.shape, F32),
        in_specs=[pl.BlockSpec(memory_space=pltpu.SMEM)] + [hbm] * 12,
        out_specs=pl.BlockSpec(memory_space=pltpu.VMEM),
        scratch_shapes=scratch,
        compiler_params=pltpu.CompilerParams(
            collective_id=0, has_side_effects=True, vmem_limit_bytes=60 * 1024 * 1024
        ),
    )(
        first_tile,
        sources,
        jnp.transpose(wavelet, (0, 2, 1)),
        u_prev,
        u_now,
        born_prev,
        born_now,
        adj_after,
        adj_last,
        velocity,
        receivers,
        observed,
        reflectivity,
    )


def solution(mesh):
    return jax.shard_map(
        functools.partial(on_device, mesh.shape["box"], mesh.shape["shot"]),
        mesh=mesh,
        in_specs=(
            P("shot", None, "box", None),
            P("shot", None, "box", None),
            P("shot", None, "box", None),
            P("shot", None, "box", None),
            P("shot", None, "box", None),
            P("shot", None, "box", None),
            P("shot", "box", None),
            P("shot", None, None),
            P("shot", None),
            P("shot", "box"),
            P("shot", None, None, "box"),
            P("shot"),
            P(None, "box", None, None),
        ),
        out_specs=P(None, "box", None, None),
        check_vma=False,
    )
```

```python
import functools

import jax
import jax.numpy as jnp
from jax import lax
from jax.experimental import pallas as pl
from jax.experimental.pallas import tpu as pltpu
from jax.sharding import PartitionSpec as P

damping = 1.0
LANES = 128
HALO = 8
BLOCK = 8
F32 = jnp.float32
MESH = pl.DeviceIdType.MESH


def wait_bytes(ref, sem):
    pltpu.make_async_copy(ref, ref, sem).wait()


def column_of(raw, c):
    shots, ext, lanes = raw.shape
    return raw.reshape(shots * ext, lanes)[pl.ds(c, shots, stride=ext), :]


def kernel(
    n_box,
    n_shot,
    first_tile,
    sources,
    wavelet,
    u_prev,
    u_now,
    born_prev,
    born_now,
    adj_after,
    adj_last,
    velocity,
    receivers,
    observed,
    reflectivity,
    out,
    sources_smem,
    wavelet_smem,
    raw_u,
    raw_q,
    raw_b,
    raw_v,
    rec,
    obs,
    refl,
    wave_u,
    accel,
    wave_b,
    wave_q,
    grad_part,
    adj_m,
    speed,
    image,
    mask,
    target,
    by_step,
    adj_r,
    tile_out,
    tile_in,
    slab_i,
    slab_d,
    slab_s,
    stage_i,
    stage_d,
    stage_s,
    back_i,
    back_d,
    back_s,
    aligned_i,
    aligned_d,
    aligned_s,
    reduce_i,
    gather_d,
    gather_s,
    scale,
    load_sem,
    halo_send,
    halo_recv,
    box_send,
    box_recv,
    shot_send,
    shot_recv,
):
    shots, columns, depth = u_now.shape[1:]
    steps = wavelet_smem.shape[1]
    n_rec = receivers.shape[1]
    rounds = reflectivity.shape[0]
    ext = columns + 2 * HALO
    spare = rounds - n_box
    share = rounds // n_shot
    g = lax.axis_index("shot")
    p = lax.axis_index("box")
    last = n_box - 1

    barrier = pltpu.get_barrier_semaphore()

    def greet_box(k, carry):
        pl.semaphore_signal(
            barrier, inc=1, device_id={"box": lax.rem(p + k, n_box)}, device_id_type=MESH
        )
        return carry

    def greet_shot(k, carry):
        pl.semaphore_signal(
            barrier, inc=1, device_id={"shot": lax.rem(g + k, n_shot)}, device_id_type=MESH
        )
        return carry

    lax.fori_loop(1, n_box, greet_box, 0)
    lax.fori_loop(1, n_shot, greet_shot, 0)

    loads = []

    def load(src, dst):
        copy = pltpu.make_async_copy(src, dst, load_sem.at[len(loads)])
        copy.start()
        loads.append(copy)
        return copy

    half = [pl.ds(0, LANES), pl.ds(LANES, LANES)]
    own = pl.ds(HALO, columns)
    load_refl = load(reflectivity.at[:, 0, :, half[0]], refl.at[pl.ds(1, rounds)])
    load_v = [load(velocity.at[0, :, half[h]], raw_v.at[h, own]) for h in range(2)]
    load_u = [
        load(field.at[0, :, :, half[h]], raw_u.at[f, h, :, own])
        for f, field in enumerate((u_prev, u_now))
        for h in range(2)
    ]
    load_s = [load(sources, sources_smem), load(wavelet, wavelet_smem)]
    load_r = [load(receivers, rec.at[1]), load(observed.at[0], obs.at[1])]
    load_q = [
        load(field.at[0, :, :, half[h]], raw_q.at[f, h, :, own])
        for f, field in enumerate((adj_after, adj_last))
        for h in range(2)
    ]
    load_b = [
        load(field.at[0, :, :, half[0]], raw_b.at[f, :, own])
        for f, field in enumerate((born_prev, born_now))
    ]

    for edge, place, side in ((0, 0, 0), (last, HALO + columns, 2)):

        @pl.when(p == edge)
        def _():
            strip = pl.ds(place, HALO)
            raw_v[:, strip] = jnp.zeros((2, HALO, LANES), F32)
            raw_b[:, :, strip] = jnp.zeros((2, shots, HALO, LANES), F32)
            for f in range(2):
                raw_u[f, :, :, strip] = jnp.zeros((2, shots, HALO, LANES), F32)
                raw_q[f, :, :, strip] = jnp.zeros((2, shots, HALO, LANES), F32)
            rec[side] = jnp.full((1, n_rec), -1, jnp.int32)
            obs[side] = jnp.zeros((shots, steps, n_rec), F32)

    refl[0] = jnp.zeros((2, LANES), F32)
    refl[rounds + 1] = jnp.zeros((2, LANES), F32)

    first = first_tile[0]
    rotation = lax.rem(first, n_box)
    first_round = lax.div(first, n_box) + (p < rotation).astype(jnp.int32)
    lead = lax.rem(p - first + 3 + 64 * n_box, n_box)
    source_round = lax.div(first - 3 + lead - p + 64 * n_box, n_box) - 64

    load_refl.wait()
    tile_out[:, 0] = refl[pl.ds(source_round + 1, n_box)]
    tile_out[:, 1] = refl[pl.ds(source_round + 2, n_box)]
    tile_in[p] = tile_out[p]

    pl.semaphore_wait(barrier, n_box - 1 + n_shot - 1)

    def box_exchange(staged, landing, place, sem):
        def send(k, carry):
            target_device = lax.rem(p + k, n_box)
            pltpu.make_async_remote_copy(
                src_ref=staged.at[target_device],
                dst_ref=landing.at[place],
                send_sem=box_send.at[sem],
                recv_sem=box_recv.at[sem],
                device_id={"box": target_device},
                device_id_type=MESH,
            ).start()
            return carry

        lax.fori_loop(1, n_box, send, 0)

    def box_sent(staged, sem):
        wait_bytes(staged.at[pl.ds(0, n_box - 1)], box_send.at[sem])

    def box_arrived(landing, sem):
        wait_bytes(landing.at[pl.ds(0, n_box - 1)], box_recv.at[sem])

    left_edge, right_edge = pl.ds(0, HALO), pl.ds(columns - HALO, HALO)
    left_halo, right_halo = pl.ds(0, HALO), pl.ds(HALO + columns, HALO)

    def halo_pieces(edge, halo, side):
        yield 0, [
            (field.at[0, :, edge, half[h]], raw_u.at[f, h, :, halo])
            for f, field in enumerate((u_prev, u_now))
            for h in range(2)
        ]
        yield 1, [(velocity.at[0, edge, half[h]], raw_v.at[h, halo]) for h in range(2)]
        yield 2, [
            (field.at[0, :, edge, half[h]], raw_q.at[f, h, :, halo])
            for f, field in enumerate((adj_after, adj_last))
            for h in range(2)
        ]
        yield 3, [
            (field.at[0, :, edge, half[0]], raw_b.at[f, :, halo])
            for f, field in enumerate((born_prev, born_now))
        ]
        yield 4, [(receivers, rec.at[side])]
        yield 5, [(observed.at[0], obs.at[side])]

    def halo_refs(group, edge_side):
        halo = (left_halo, right_halo)[edge_side]
        side = (0, 2)[edge_side]
        return (
            raw_u.at[:, :, :, halo],
            raw_v.at[:, halo],
            raw_q.at[:, :, :, halo],
            raw_b.at[:, :, halo],
            rec.at[side],
            obs.at[side],
        )[group]

    def send_halo(direction, groups):
        edge, halo, side = (
            (left_edge, right_halo, 2),
            (right_edge, left_halo, 0),
        )[direction]
        neighbour = (p - 1, p + 1)[direction]
        for group, pieces in halo_pieces(edge, halo, side):
            if group not in groups:
                continue
            for src, dst in pieces:
                pltpu.make_async_remote_copy(
                    src_ref=src,
                    dst_ref=dst,
                    send_sem=halo_send.at[direction, group],
                    recv_sem=halo_recv.at[direction, group],
                    device_id={"box": neighbour},
                    device_id_type=MESH,
                ).start()

    def send_halos(groups):
        @pl.when(p > 0)
        def _():
            send_halo(0, groups)

        @pl.when(p < last)
        def _():
            send_halo(1, groups)

    send_halos((0, 1))
    box_exchange(tile_out, tile_in, p, 0)
    send_halos((2, 3, 4, 5))

    blank = jnp.zeros((shots, LANES), F32)
    for pad in (0, ext + 1):
        for level in range(2):
            wave_b[level, pad] = blank
        for level in range(steps):
            adj_m[level, pad] = blank
    for c in (0, 1, ext - 2, ext - 1):
        image[c] = blank
    for back in (back_i, back_d, back_s):
        for place in (0, spare + n_box):
            back[pl.ds(place, spare)] = jnp.zeros((spare,) + back.shape[1:], F32)

    def halo_arrived(group):
        @pl.when(p < last)
        def _():
            wait_bytes(halo_refs(group, 1), halo_recv.at[0, group])

        @pl.when(p > 0)
        def _():
            wait_bytes(halo_refs(group, 0), halo_recv.at[1, group])

    def halo_sent(group):
        @pl.when(p > 0)
        def _():
            wait_bytes(halo_refs(group, 1), halo_send.at[0, group])

        @pl.when(p < last)
        def _():
            wait_bytes(halo_refs(group, 0), halo_send.at[1, group])

    lane = lax.broadcasted_iota(jnp.int32, (shots, LANES), 1)
    at_top = lane == 0
    at_bottom = lane == LANES - 1
    shot_row = lax.broadcasted_iota(jnp.int32, (shots, LANES), 0)
    first_cell = (p * columns - HALO) * depth

    def by_columns(raw, working, start, count):
        def move(c, carry):
            working[start + c + 1] = column_of(raw, start + c)
            return carry

        lax.fori_loop(0, count, move, 0, unroll=min(count, 16))

    def widen(start, count):
        for h in range(2):

            def spread(c, carry):
                speed[h, start + c] = jnp.broadcast_to(
                    raw_v[h, pl.ds(start + c, 1), :], (shots, LANES)
                )
                return carry

            lax.fori_loop(0, count, spread, 0, unroll=min(count, 16))

    for copy in load_s:
        copy.wait()
    source_cell = jnp.zeros((shots, LANES), jnp.int32)
    pulses = [jnp.zeros((shots, LANES), F32) for _ in range(steps)]
    for s in range(shots):
        source_cell = jnp.where(shot_row == s, sources_smem[0, s], source_cell)
        for t in range(steps):
            pulses[t] = jnp.where(shot_row == s, wavelet_smem[0, t, s], pulses[t])
    source_cell = source_cell - first_cell - lane

    def blocks(body, start, stop, unroll):
        count = -(-(stop - start) // BLOCK)

        def step(i, carry):
            body(jnp.minimum(start + i * BLOCK, stop - BLOCK), i)
            return carry

        lax.fori_loop(0, count, step, 0, unroll=unroll if count % unroll == 0 else 1)

    def turn(x, by):
        return pltpu.roll(x, by, axis=2)

    def around(wave, c):
        wide = wave[pl.ds(c, BLOCK + 2)]
        return wide[1 : BLOCK + 1], wide[:BLOCK] + wide[2:]

    def lap_both(wave, level, c):
        pairs = [around(wave.at[level, h], c) for h in range(2)]
        n = [pair[0] for pair in pairs]
        down = [turn(n[h], 1) for h in range(2)]
        up = [turn(n[h], LANES - 1) for h in range(2)]
        shallow = [jnp.where(at_top, 0.0, down[0]), jnp.where(at_top, down[0], down[1])]
        deep = [jnp.where(at_bottom, up[1], up[0]), jnp.where(at_bottom, 0.0, up[1])]
        laps = [pairs[h][1] + (shallow[h] + deep[h]) - 4.0 * n[h] for h in range(2)]
        return n, laps

    def lap_top(wave, level, c, closed):
        n, sides = around(wave.at[level], c)
        shallow = jnp.where(at_top, 0.0, turn(n, 1))
        deep = turn(n, LANES - 1)
        if closed:
            deep = jnp.where(at_bottom, 0.0, deep)
        return n, sides + (shallow + deep) - 4.0 * n

    def store_rows(slab, kind, i, block):
        for r in range(BLOCK):
            row = jnp.sum(block[r], axis=0, keepdims=True)
            j = i * (BLOCK // 2) + r // 2
            slab[j, kind, pl.ds(r % 2, 1), :] = row
            slab[j + n_box, kind, pl.ds(r % 2, 1), :] = row

    turned = lax.rem(n_box - rotation, n_box)

    def to_owners(slab, staged, back, sem):
        staged[...] = slab[pl.ds(turned, n_box)]
        back[spare + p] = staged[p]
        box_exchange(staged, back, spare + p, sem)

    def from_boxes(back, aligned, sem):
        box_arrived(back, sem)
        aligned[...] = back[pl.ds(spare - first_round, rounds)]

    def shot_exchange(src_of, landing, sem):
        def send(k, carry):
            s = lax.rem(g + k, n_shot)
            pltpu.make_async_remote_copy(
                src_ref=src_of(s),
                dst_ref=landing,
                send_sem=shot_send.at[sem],
                recv_sem=shot_recv.at[sem],
                device_id={"shot": s},
                device_id_type=MESH,
            ).start()
            return carry

        lax.fori_loop(1, n_shot, send, 0)

    def to_all(aligned, gathered, sem):
        shot_exchange(lambda s: aligned, gathered.at[g], sem)
        gathered[g] = aligned[...]

    mine = pl.ds(g * share, share)
    others = pl.ds(0, (n_shot - 1) * share)
    cell_step = lax.broadcasted_iota(jnp.int32, (BLOCK, shots, LANES), 0) * depth

    def advance(t, c):
        n, laps = lap_both(wave_u, t + 1, c)
        for h in range(2):
            offset = (source_cell - (c * depth + h * LANES))[None]
            a = speed[h, pl.ds(c, BLOCK)] * laps[h] + jnp.where(
                offset == cell_step, pulses[t][None], 0.0
            )
            accel[t, h, pl.ds(c, BLOCK)] = a
            if t < steps - 1:
                wave_u[t + 2, h, pl.ds(c + 1, BLOCK)] = (
                    (n[h] + n[h]) - wave_u[t, h, pl.ds(c + 1, BLOCK)]
                ) + a

    for copy in load_u + load_v:
        copy.wait()
    widen(HALO, columns)
    for h in range(2):
        for level in range(2):
            by_columns(raw_u.at[level, h], wave_u.at[level, h], HALO, columns)
    for t in range(steps):
        blocks(lambda c, i: advance(t, c), HALO + 1 + t, HALO + columns - 1 - t, 2)
    halo_arrived(0)
    halo_arrived(1)
    for start in (0, HALO + columns):
        widen(start, HALO)
        for h in range(2):
            for level in range(2):
                by_columns(raw_u.at[level, h], wave_u.at[level, h], start, HALO)
    for t in range(steps):
        advance(t, 1 + t)
        advance(t, HALO + columns - 1 - t)

    def brighten(c, i):
        for h in range(2):
            a = [accel[t, h, pl.ds(c, BLOCK)] for t in range(steps)]
            store_rows(slab_i, h, i, sum(x * x for x in a))

    blocks(brighten, HALO, HALO + columns, 2)
    to_owners(slab_i, stage_i, back_i, 1)

    for copy in load_q:
        copy.wait()
    halo_arrived(2)
    for h in range(2):
        for level in range(2):
            by_columns(raw_q.at[level, h], wave_q.at[level, h], 0, ext)

    def retreat(k, c):
        n, laps = lap_both(wave_q, k + 1, c)
        for h in range(2):
            wave_q[k + 2, h, pl.ds(c + 1, BLOCK)] = (
                (n[h] + n[h]) - wave_q[k, h, pl.ds(c + 1, BLOCK)]
            ) + speed[h, pl.ds(c, BLOCK)] * laps[h]

    for k in range(steps):
        blocks(lambda c, i: retreat(k, c), HALO - 3 + k, HALO + columns + 3 - k, 3)

    def correlate(c, i):
        products = [
            sum(
                wave_q[steps + 1 - t, h, pl.ds(c + 1, BLOCK)] * accel[t, h, pl.ds(c, BLOCK)]
                for t in range(steps)
            )
            for h in range(2)
        ]
        store_rows(slab_d, 0, i, products[1])
        grad_part[pl.ds(i * BLOCK, BLOCK)] = products[0]

    blocks(correlate, HALO, HALO + columns, 2)
    to_owners(slab_d, stage_d, back_d, 2)

    for copy in load_r + load_b:
        copy.wait()
    halo_arrived(4)
    halo_arrived(5)
    halo_arrived(3)
    by_columns(raw_b.at[0], wave_b.at[0], 0, ext)
    by_columns(raw_b.at[1], wave_b.at[1], 0, ext)
    beside = HALO // 2
    heard = (
        [(0, n_rec - beside + r) for r in range(beside)]
        + [(1, r) for r in range(n_rec)]
        + [(2, r) for r in range(beside)]
    )
    for side in range(3):
        for t in range(steps):
            by_step[side, t] = obs[side, :, t, :]
    cells = [jnp.broadcast_to(rec[side], (shots, n_rec)) for side in range(3)]
    data = [[by_step[side, t] for t in range(steps)] for side in range(3)]
    for slot, (side, r) in enumerate(heard):
        cell = jnp.broadcast_to(cells[side][:, r : r + 1], (shots, LANES)) - first_cell - lane
        for t in range(steps):
            target[t, slot] = jnp.broadcast_to(data[side][t][:, r : r + 1], (shots, LANES))
        for w in range(2):
            c = 2 * slot + w
            mask[c] = jnp.where(cell == c * depth, 1.0, 0.0)

    box_arrived(tile_in, 0)
    for j in range(n_box + 6):
        owner = lax.rem(rotation + j - 3 + n_box, n_box)
        tile = tile_in[owner, j // n_box]
        for w in range(2):
            image[HALO - 6 + 2 * j + w] = jnp.broadcast_to(tile[w : w + 1], (shots, LANES))

    def scatter_wave(t, c):
        n, lap = lap_top(wave_b, t + 1, c, False)
        b = (
            ((n + n) - wave_b[t, pl.ds(c + 1, BLOCK)])
            + speed[0, pl.ds(c, BLOCK)] * lap
            + image[pl.ds(c, BLOCK)] * accel[t, 0, pl.ds(c, BLOCK)]
        )
        if t < steps - 1:
            wave_b[t + 2, pl.ds(c + 1, BLOCK)] = b
        recorded = target[t, pl.ds(c // 2, BLOCK // 2)]
        recorded = jnp.broadcast_to(
            recorded[:, None], (BLOCK // 2, 2, shots, LANES)
        ).reshape(BLOCK, shots, LANES)
        adj_m[t, pl.ds(c + 1, BLOCK)] = mask[pl.ds(c, BLOCK)] * (b - recorded)

    for t in range(steps):
        inset = 0 if t < 2 else HALO // 2
        count = (ext - 2 * inset) // BLOCK
        for i in range(count):
            scatter_wave(t, inset + i * BLOCK)

    from_boxes(back_i, aligned_i, 1)
    reduce_i[g] = aligned_i[mine]
    shot_exchange(lambda s: aligned_i.at[pl.ds(s * share, share)], reduce_i.at[g], 0)

    def misfit_wave(t):
        return adj_m.at[t] if t == steps - 1 else adj_r.at[t]

    def residual(t, c):
        n, sides = around(misfit_wave(t + 1), c)
        shallow = jnp.where(at_top, 0.0, turn(n, 1))
        deep = jnp.where(at_bottom, 0.0, turn(n, LANES - 1))
        lap = sides + (shallow + deep) - 4.0 * n
        q = (n + n) + speed[0, pl.ds(c, BLOCK)] * lap + adj_m[t, pl.ds(c + 1, BLOCK)]
        if t + 2 < steps:
            q = q - misfit_wave(t + 2)[pl.ds(c + 1, BLOCK)]
        adj_r[t, pl.ds(c + 1, BLOCK)] = q

    for t in reversed(range(steps - 1)):
        start, stop = HALO - t, HALO + columns + t
        count = -(-(stop - start) // BLOCK)
        for i in range(count):
            residual(t, min(start + i * BLOCK, stop - BLOCK))

    def correlate_late(c, i):
        total = grad_part[pl.ds(i * BLOCK, BLOCK)] + sum(
            misfit_wave(t)[pl.ds(c + 1, BLOCK)] * accel[t, 0, pl.ds(c, BLOCK)]
            for t in range(steps)
        )
        store_rows(slab_s, 0, i, total)

    for i in range(columns // BLOCK):
        correlate_late(HALO + i * BLOCK, i)
    to_owners(slab_s, stage_s, back_s, 3)

    from_boxes(back_d, aligned_d, 2)
    to_all(aligned_d, gather_d, 1)

    wait_bytes(reduce_i.at[pl.ds(0, n_shot - 1)], shot_recv.at[0])
    light = reduce_i[0]
    for s in range(1, n_shot):
        light = light + reduce_i[s]
    scale[mine] = jnp.sqrt(light + damping)
    shot_exchange(lambda s: scale.at[mine], scale.at[mine], 2)

    from_boxes(back_s, aligned_s, 3)
    to_all(aligned_s, gather_s, 3)

    def total_of(gathered, sem):
        wait_bytes(gathered.at[pl.ds(0, n_shot - 1)], shot_recv.at[sem])
        total = gathered[0, :, 0]
        for s in range(1, n_shot):
            total = total + gathered[s, :, 0]
        return total

    deep_total = total_of(gather_d, 1)
    wait_bytes(scale.at[others], shot_recv.at[2])
    out[:, 0, :, half[1]] = deep_total / scale[:, 1]
    out[:, 0, :, half[0]] = total_of(gather_s, 3) / scale[:, 0]

    for group in range(6):
        halo_sent(group)
    box_sent(tile_out, 0)
    box_sent(stage_i, 1)
    box_sent(stage_d, 2)
    box_sent(stage_s, 3)
    wait_bytes(aligned_i.at[others], shot_send.at[0])
    wait_bytes(gather_d.at[pl.ds(0, n_shot - 1)], shot_send.at[1])
    wait_bytes(scale.at[others], shot_send.at[2])
    wait_bytes(gather_s.at[pl.ds(0, n_shot - 1)], shot_send.at[3])


def on_device(
    n_box,
    n_shot,
    u_prev,
    u_now,
    born_prev,
    born_now,
    adj_after,
    adj_last,
    velocity,
    wavelet,
    sources,
    receivers,
    observed,
    first_tile,
    reflectivity,
):
    shots, columns, depth = u_now.shape[1:]
    steps = wavelet.shape[2]
    n_rec = receivers.shape[1]
    rounds = reflectivity.shape[0]
    ext = columns + 2 * HALO
    spare = rounds - n_box
    share = rounds // n_shot

    def vmem(*dims):
        return pltpu.VMEM(dims, F32)

    pitch = ext + HALO
    plane = (shots, LANES)
    tile = (2, LANES)
    scratch = [
        pltpu.SMEM(sources.shape, jnp.int32),
        pltpu.SMEM((1, steps, shots), F32),
        vmem(2, 2, shots, pitch, LANES),
        vmem(2, 2, shots, pitch, LANES),
        vmem(2, shots, pitch, LANES),
        vmem(2, ext, LANES),
        pltpu.VMEM((3, 1, n_rec), jnp.int32),
        vmem(3, shots, steps, n_rec),
        vmem(rounds + 2, *tile),
        vmem(steps + 1, 2, ext + 2, *plane),
        vmem(steps, 2, ext, *plane),
        vmem(steps + 1, ext + 2, *plane),
        vmem(steps + 2, 2, ext + 2, *plane),
        vmem(columns, *plane),
        vmem(steps, ext + 2, *plane),
        vmem(2, ext, *plane),
        vmem(ext, *plane),
        vmem(ext, *plane),
        vmem(steps, ext // 2, *plane),
        vmem(3, steps, shots, n_rec),
        vmem(steps - 1, ext + 2, *plane),
        vmem(n_box, 2, *tile),
        vmem(n_box, 2, *tile),
        vmem(2 * n_box, 2, *tile),
        vmem(2 * n_box, 1, *tile),
        vmem(2 * n_box, 1, *tile),
        vmem(n_box, 2, *tile),
        vmem(n_box, 1, *tile),
        vmem(n_box, 1, *tile),
        vmem(n_box + 2 * spare, 2, *tile),
        vmem(n_box + 2 * spare, 1, *tile),
        vmem(n_box + 2 * spare, 1, *tile),
        vmem(rounds, 2, *tile),
        vmem(rounds, 1, *tile),
        vmem(rounds, 1, *tile),
        vmem(n_shot, share, 2, *tile),
        vmem(n_shot, rounds, 1, *tile),
        vmem(n_shot, rounds, 1, *tile),
        vmem(rounds, 2, *tile),
        pltpu.SemaphoreType.DMA((19,)),
        pltpu.SemaphoreType.DMA((2, 6)),
        pltpu.SemaphoreType.DMA((2, 6)),
        pltpu.SemaphoreType.DMA((4,)),
        pltpu.SemaphoreType.DMA((4,)),
        pltpu.SemaphoreType.DMA((4,)),
        pltpu.SemaphoreType.DMA((4,)),
    ]
    hbm = pl.BlockSpec(memory_space=pltpu.HBM)
    return pl.pallas_call(
        functools.partial(kernel, n_box, n_shot),
        out_shape=jax.ShapeDtypeStruct(reflectivity.shape, F32),
        in_specs=[pl.BlockSpec(memory_space=pltpu.SMEM)] + [hbm] * 12,
        out_specs=pl.BlockSpec(memory_space=pltpu.VMEM),
        scratch_shapes=scratch,
        compiler_params=pltpu.CompilerParams(
            collective_id=0, has_side_effects=True, vmem_limit_bytes=60 * 1024 * 1024
        ),
    )(
        first_tile,
        sources,
        jnp.transpose(wavelet, (0, 2, 1)),
        u_prev,
        u_now,
        born_prev,
        born_now,
        adj_after,
        adj_last,
        velocity,
        receivers,
        observed,
        reflectivity,
    )


def solution(mesh):
    return jax.shard_map(
        functools.partial(on_device, mesh.shape["box"], mesh.shape["shot"]),
        mesh=mesh,
        in_specs=(
            P("shot", None, "box", None),
            P("shot", None, "box", None),
            P("shot", None, "box", None),
            P("shot", None, "box", None),
            P("shot", None, "box", None),
            P("shot", None, "box", None),
            P("shot", "box", None),
            P("shot", None, None),
            P("shot", None),
            P("shot", "box"),
            P("shot", None, None, "box"),
            P("shot"),
            P(None, "box", None, None),
        ),
        out_specs=P(None, "box", None, None),
        check_vma=False,
    )
```

```python
import functools

import jax
import jax.numpy as jnp
from jax import lax
from jax.experimental import pallas as pl
from jax.experimental.pallas import tpu as pltpu
from jax.sharding import PartitionSpec as P

damping = 1.0
LANES = 128
HALO = 8
BLOCK = 8
F32 = jnp.float32
MESH = pl.DeviceIdType.MESH


def wait_bytes(ref, sem):
    pltpu.make_async_copy(ref, ref, sem).wait()


def column_of(raw, c):
    shots, ext, lanes = raw.shape
    return raw.reshape(shots * ext, lanes)[pl.ds(c, shots, stride=ext), :]


def kernel(
    n_box,
    n_shot,
    first_tile,
    sources,
    wavelet,
    u_prev,
    u_now,
    born_prev,
    born_now,
    adj_after,
    adj_last,
    velocity,
    receivers,
    observed,
    reflectivity,
    out,
    sources_smem,
    wavelet_smem,
    raw_u,
    raw_q,
    raw_b,
    raw_v,
    rec,
    obs,
    refl,
    wave_u,
    accel,
    wave_b,
    wave_q,
    grad_part,
    adj_m,
    speed,
    image,
    mask,
    target,
    by_step,
    adj_r,
    tile_out,
    tile_in,
    slab_i,
    slab_d,
    slab_s,
    stage_i,
    stage_d,
    stage_s,
    back_i,
    back_d,
    back_s,
    aligned_i,
    reduce_i,
    gather_d,
    gather_s,
    scale,
    start_out,
    start_in,
    start_smem,
    load_sem,
    halo_send,
    halo_recv,
    box_send,
    box_recv,
    shot_send,
    shot_recv,
):
    shots, columns, depth = u_now.shape[1:]
    steps = wavelet_smem.shape[1]
    n_rec = receivers.shape[1]
    rounds = reflectivity.shape[0]
    ext = columns + 2 * HALO
    spare = rounds - n_box
    share = rounds // n_shot
    g = lax.axis_index("shot")
    p = lax.axis_index("box")
    last = n_box - 1

    barrier = pltpu.get_barrier_semaphore()

    def greet_box(k, carry):
        pl.semaphore_signal(
            barrier, inc=1, device_id={"box": lax.rem(p + k, n_box)}, device_id_type=MESH
        )
        return carry

    def greet_shot(k, carry):
        pl.semaphore_signal(
            barrier, inc=1, device_id={"shot": lax.rem(g + k, n_shot)}, device_id_type=MESH
        )
        return carry

    lax.fori_loop(1, n_box, greet_box, 0)
    lax.fori_loop(1, n_shot, greet_shot, 0)

    loads = []

    def load(src, dst):
        copy = pltpu.make_async_copy(src, dst, load_sem.at[len(loads)])
        copy.start()
        loads.append(copy)
        return copy

    half = [pl.ds(0, LANES), pl.ds(LANES, LANES)]
    own = pl.ds(HALO, columns)
    load_refl = load(reflectivity.at[:, 0, :, half[0]], refl.at[pl.ds(1, rounds)])
    load_v = [load(velocity.at[0, :, half[h]], raw_v.at[h, own]) for h in range(2)]
    load_u = [
        load(field.at[0, :, :, half[h]], raw_u.at[f, h, :, own])
        for f, field in enumerate((u_prev, u_now))
        for h in range(2)
    ]
    load_s = [load(sources, sources_smem), load(wavelet, wavelet_smem)]
    load_r = [load(receivers, rec.at[1]), load(observed.at[0], obs.at[1])]
    load_q = [
        load(field.at[0, :, :, half[h]], raw_q.at[f, h, :, own])
        for f, field in enumerate((adj_after, adj_last))
        for h in range(2)
    ]
    load_b = [
        load(field.at[0, :, :, half[0]], raw_b.at[f, :, own])
        for f, field in enumerate((born_prev, born_now))
    ]

    for edge, place, side in ((0, 0, 0), (last, HALO + columns, 2)):

        @pl.when(p == edge)
        def _():
            strip = pl.ds(place, HALO)
            raw_v[:, strip] = jnp.zeros((2, HALO, LANES), F32)
            raw_b[:, :, strip] = jnp.zeros((2, shots, HALO, LANES), F32)
            for f in range(2):
                raw_u[f, :, :, strip] = jnp.zeros((2, shots, HALO, LANES), F32)
                raw_q[f, :, :, strip] = jnp.zeros((2, shots, HALO, LANES), F32)
            rec[side] = jnp.full((1, n_rec), -1, jnp.int32)
            obs[side] = jnp.zeros((shots, steps, n_rec), F32)

    refl[0] = jnp.zeros((2, LANES), F32)
    refl[rounds + 1] = jnp.zeros((2, LANES), F32)

    first = first_tile[0]
    rotation = lax.rem(first, n_box)
    first_round = lax.div(first, n_box) + (p < rotation).astype(jnp.int32)
    lead = lax.rem(p - first + 3 + 64 * n_box, n_box)
    source_round = lax.div(first - 3 + lead - p + 64 * n_box, n_box) - 64

    load_refl.wait()
    tile_out[:, 0] = refl[pl.ds(source_round + 1, n_box)]
    tile_out[:, 1] = refl[pl.ds(source_round + 2, n_box)]
    tile_in[p] = tile_out[p]

    pl.semaphore_wait(barrier, n_box - 1 + n_shot - 1)

    def box_exchange(staged, landing, place, sem):
        def send(k, carry):
            target_device = lax.rem(p + k, n_box)
            pltpu.make_async_remote_copy(
                src_ref=staged.at[target_device],
                dst_ref=landing.at[place],
                send_sem=box_send.at[sem],
                recv_sem=box_recv.at[sem],
                device_id={"box": target_device},
                device_id_type=MESH,
            ).start()
            return carry

        lax.fori_loop(1, n_box, send, 0)

    def box_sent(staged, sem):
        wait_bytes(staged.at[pl.ds(0, n_box - 1)], box_send.at[sem])

    def box_arrived(landing, sem):
        wait_bytes(landing.at[pl.ds(0, n_box - 1)], box_recv.at[sem])

    left_edge, right_edge = pl.ds(0, HALO), pl.ds(columns - HALO, HALO)
    left_halo, right_halo = pl.ds(0, HALO), pl.ds(HALO + columns, HALO)

    def halo_pieces(edge, halo, side):
        yield 0, [
            (field.at[0, :, edge, half[h]], raw_u.at[f, h, :, halo])
            for f, field in enumerate((u_prev, u_now))
            for h in range(2)
        ]
        yield 1, [(velocity.at[0, edge, half[h]], raw_v.at[h, halo]) for h in range(2)]
        shift = HALO // 2 if side == 0 else 0
        near = pl.ds(edge.start + shift, HALO // 2)
        there = pl.ds(halo.start + shift, HALO // 2)
        yield 2, [
            (field.at[0, :, near, half[h]], raw_q.at[f, h, :, there])
            for f, field in enumerate((adj_after, adj_last))
            for h in range(2)
        ]
        yield 3, [
            (field.at[0, :, edge, half[0]], raw_b.at[f, :, halo])
            for f, field in enumerate((born_prev, born_now))
        ]
        yield 4, [(receivers, rec.at[side])]
        yield 5, [(observed.at[0], obs.at[side])]

    def halo_refs(group, edge_side):
        halo = (left_halo, right_halo)[edge_side]
        side = (0, 2)[edge_side]
        return (
            raw_u.at[:, :, :, halo],
            raw_v.at[:, halo],
            raw_q.at[:, :, :, pl.ds(halo.start + (HALO // 2 if side == 0 else 0), HALO // 2)],
            raw_b.at[:, :, halo],
            rec.at[side],
            obs.at[side],
        )[group]

    def send_halo(direction, groups):
        edge, halo, side = (
            (left_edge, right_halo, 2),
            (right_edge, left_halo, 0),
        )[direction]
        neighbour = (p - 1, p + 1)[direction]
        for group, pieces in halo_pieces(edge, halo, side):
            if group not in groups:
                continue
            for src, dst in pieces:
                pltpu.make_async_remote_copy(
                    src_ref=src,
                    dst_ref=dst,
                    send_sem=halo_send.at[direction, group],
                    recv_sem=halo_recv.at[direction, group],
                    device_id={"box": neighbour},
                    device_id_type=MESH,
                ).start()

    def send_halos(groups):
        @pl.when(p > 0)
        def _():
            send_halo(0, groups)

        @pl.when(p < last)
        def _():
            send_halo(1, groups)

    send_halos((0, 1))
    box_exchange(tile_out, tile_in, p, 0)
    start_out[...] = jnp.full((1, LANES), first_round, jnp.int32)
    start_in[g] = start_out[...]
    send_halos((2, 3, 4, 5))

    blank = jnp.zeros((shots, LANES), F32)
    for pad in (0, ext + 1):
        for level in range(2):
            wave_b[level, pad] = blank
        for level in range(steps):
            adj_m[level, pad] = blank
    for c in (0, 1, ext - 2, ext - 1):
        image[c] = blank
    for back in (back_i,):
        for place in (0, spare + n_box):
            back[pl.ds(place, spare)] = jnp.zeros((spare,) + back.shape[1:], F32)

    def halo_arrived(group):
        @pl.when(p < last)
        def _():
            wait_bytes(halo_refs(group, 1), halo_recv.at[0, group])

        @pl.when(p > 0)
        def _():
            wait_bytes(halo_refs(group, 0), halo_recv.at[1, group])

    def halo_sent(group):
        @pl.when(p > 0)
        def _():
            wait_bytes(halo_refs(group, 1), halo_send.at[0, group])

        @pl.when(p < last)
        def _():
            wait_bytes(halo_refs(group, 0), halo_send.at[1, group])

    lane = lax.broadcasted_iota(jnp.int32, (shots, LANES), 1)
    at_top = lane == 0
    at_bottom = lane == LANES - 1
    shot_row = lax.broadcasted_iota(jnp.int32, (shots, LANES), 0)
    first_cell = (p * columns - HALO) * depth

    def by_columns(raw, working, start, count):
        def move(c, carry):
            working[start + c + 1] = column_of(raw, start + c)
            return carry

        lax.fori_loop(0, count, move, 0, unroll=min(count, 16))

    def widen(start, count):
        for h in range(2):

            def spread(c, carry):
                speed[h, start + c] = jnp.broadcast_to(
                    raw_v[h, pl.ds(start + c, 1), :], (shots, LANES)
                )
                return carry

            lax.fori_loop(0, count, spread, 0, unroll=min(count, 16))

    for copy in load_s:
        copy.wait()
    source_cell = jnp.zeros((shots, LANES), jnp.int32)
    pulses = [jnp.zeros((shots, LANES), F32) for _ in range(steps)]
    for s in range(shots):
        source_cell = jnp.where(shot_row == s, sources_smem[0, s], source_cell)
        for t in range(steps):
            pulses[t] = jnp.where(shot_row == s, wavelet_smem[0, t, s], pulses[t])
    source_cell = source_cell - first_cell - lane

    def blocks(body, start, stop, unroll):
        count = -(-(stop - start) // BLOCK)

        def step(i, carry):
            body(jnp.minimum(start + i * BLOCK, stop - BLOCK), i)
            return carry

        lax.fori_loop(0, count, step, 0, unroll=unroll if count % unroll == 0 else 1)

    def turn(x, by):
        return pltpu.roll(x, by, axis=2)

    def around(wave, c):
        wide = wave[pl.ds(c, BLOCK + 2)]
        return wide[1 : BLOCK + 1], wide[:BLOCK] + wide[2:]

    def lap_both(wave, level, c):
        pairs = [around(wave.at[level, h], c) for h in range(2)]
        n = [pair[0] for pair in pairs]
        down = [turn(n[h], 1) for h in range(2)]
        up = [turn(n[h], LANES - 1) for h in range(2)]
        shallow = [jnp.where(at_top, 0.0, down[0]), jnp.where(at_top, down[0], down[1])]
        deep = [jnp.where(at_bottom, up[1], up[0]), jnp.where(at_bottom, 0.0, up[1])]
        laps = [pairs[h][1] + (shallow[h] + deep[h]) - 4.0 * n[h] for h in range(2)]
        return n, laps

    def lap_top(wave, level, c, closed):
        n, sides = around(wave.at[level], c)
        shallow = jnp.where(at_top, 0.0, turn(n, 1))
        deep = turn(n, LANES - 1)
        if closed:
            deep = jnp.where(at_bottom, 0.0, deep)
        return n, sides + (shallow + deep) - 4.0 * n

    def store_rows(slab, kind, i, block):
        for r in range(BLOCK):
            row = jnp.sum(block[r], axis=0, keepdims=True)
            j = i * (BLOCK // 2) + r // 2
            slab[j, kind, pl.ds(r % 2, 1), :] = row
            slab[j + n_box, kind, pl.ds(r % 2, 1), :] = row

    turned = lax.rem(n_box - rotation, n_box)

    def to_owners(slab, staged, back, place, sem):
        staged[...] = slab[pl.ds(turned, n_box)]
        back[place + p] = staged[p]
        box_exchange(staged, back, place + p, sem)

    def from_boxes(back, aligned, sem):
        box_arrived(back, sem)
        aligned[...] = back[pl.ds(spare - first_round, rounds)]

    def shot_exchange(src_of, landing, sem):
        def send(k, carry):
            s = lax.rem(g + k, n_shot)
            pltpu.make_async_remote_copy(
                src_ref=src_of(s),
                dst_ref=landing,
                send_sem=shot_send.at[sem],
                recv_sem=shot_recv.at[sem],
                device_id={"shot": s},
                device_id_type=MESH,
            ).start()
            return carry

        lax.fori_loop(1, n_shot, send, 0)

    filled = pl.ds(spare, n_box)

    def to_all(back, gathered, sem):
        shot_exchange(lambda s: back, gathered.at[g, filled], sem)
        gathered[g, filled] = back[...]

    shot_exchange(lambda s: start_out, start_in.at[g], 4)
    mine = pl.ds(g * share, share)
    others = pl.ds(0, (n_shot - 1) * share)
    cell_step = lax.broadcasted_iota(jnp.int32, (BLOCK, shots, LANES), 0) * depth

    def advance(t, c):
        n, laps = lap_both(wave_u, t + 1, c)
        for h in range(2):
            offset = (source_cell - (c * depth + h * LANES))[None]
            a = speed[h, pl.ds(c, BLOCK)] * laps[h] + jnp.where(
                offset == cell_step, pulses[t][None], 0.0
            )
            accel[t, h, pl.ds(c, BLOCK)] = a
            if t < steps - 1:
                wave_u[t + 2, h, pl.ds(c + 1, BLOCK)] = (
                    (n[h] + n[h]) - wave_u[t, h, pl.ds(c + 1, BLOCK)]
                ) + a

    for copy in load_u + load_v:
        copy.wait()
    widen(HALO, columns)
    for h in range(2):
        for level in range(2):
            by_columns(raw_u.at[level, h], wave_u.at[level, h], HALO, columns)
    for t in range(steps):
        blocks(lambda c, i: advance(t, c), HALO + 1 + t, HALO + columns - 1 - t, 2)
    halo_arrived(0)
    halo_arrived(1)
    for start in (0, HALO + columns):
        widen(start, HALO)
        for h in range(2):
            for level in range(2):
                by_columns(raw_u.at[level, h], wave_u.at[level, h], start, HALO)
    for t in range(steps):
        advance(t, 1 + t)
        advance(t, HALO + columns - 1 - t)

    def brighten(c, i):
        for h in range(2):
            a = [accel[t, h, pl.ds(c, BLOCK)] for t in range(steps)]
            store_rows(slab_i, h, i, sum(x * x for x in a))

    blocks(brighten, HALO, HALO + columns, 2)
    to_owners(slab_i, stage_i, back_i, spare, 1)

    for copy in load_q:
        copy.wait()
    halo_arrived(2)
    for h in range(2):
        for level in range(2):
            by_columns(raw_q.at[level, h], wave_q.at[level, h], 0, ext)

    def retreat(k, c):
        n, laps = lap_both(wave_q, k + 1, c)
        for h in range(2):
            wave_q[k + 2, h, pl.ds(c + 1, BLOCK)] = (
                (n[h] + n[h]) - wave_q[k, h, pl.ds(c + 1, BLOCK)]
            ) + speed[h, pl.ds(c, BLOCK)] * laps[h]

    for k in range(steps):
        blocks(lambda c, i: retreat(k, c), HALO - 3 + k, HALO + columns + 3 - k, 3)

    def correlate(c, i):
        products = [
            sum(
                wave_q[steps + 1 - t, h, pl.ds(c + 1, BLOCK)] * accel[t, h, pl.ds(c, BLOCK)]
                for t in range(steps)
            )
            for h in range(2)
        ]
        store_rows(slab_d, 0, i, products[1])
        grad_part[pl.ds(i * BLOCK, BLOCK)] = products[0]

    blocks(correlate, HALO, HALO + columns, 2)
    to_owners(slab_d, stage_d, back_d, 0, 2)

    for copy in load_r + load_b:
        copy.wait()
    halo_arrived(4)
    halo_arrived(5)
    halo_arrived(3)
    by_columns(raw_b.at[0], wave_b.at[0], 0, ext)
    by_columns(raw_b.at[1], wave_b.at[1], 0, ext)
    beside = HALO // 2
    heard = (
        [(0, n_rec - beside + r) for r in range(beside)]
        + [(1, r) for r in range(n_rec)]
        + [(2, r) for r in range(beside)]
    )
    for side in range(3):
        for t in range(steps):
            by_step[side, t] = obs[side, :, t, :]
    cells = [jnp.broadcast_to(rec[side], (shots, n_rec)) for side in range(3)]
    data = [[by_step[side, t] for t in range(steps)] for side in range(3)]
    for slot, (side, r) in enumerate(heard):
        cell = jnp.broadcast_to(cells[side][:, r : r + 1], (shots, LANES)) - first_cell - lane
        for t in range(steps):
            target[t, slot] = jnp.broadcast_to(data[side][t][:, r : r + 1], (shots, LANES))
        for w in range(2):
            c = 2 * slot + w
            mask[c] = jnp.where(cell == c * depth, 1.0, 0.0)

    box_arrived(tile_in, 0)
    for j in range(n_box + 6):
        owner = lax.rem(rotation + j - 3 + n_box, n_box)
        tile = tile_in[owner, j // n_box]
        for w in range(2):
            image[HALO - 6 + 2 * j + w] = jnp.broadcast_to(tile[w : w + 1], (shots, LANES))

    def scatter_wave(t, c):
        n, lap = lap_top(wave_b, t + 1, c, False)
        b = (
            ((n + n) - wave_b[t, pl.ds(c + 1, BLOCK)])
            + speed[0, pl.ds(c, BLOCK)] * lap
            + image[pl.ds(c, BLOCK)] * accel[t, 0, pl.ds(c, BLOCK)]
        )
        if t < steps - 1:
            wave_b[t + 2, pl.ds(c + 1, BLOCK)] = b
        recorded = target[t, pl.ds(c // 2, BLOCK // 2)]
        recorded = jnp.broadcast_to(
            recorded[:, None], (BLOCK // 2, 2, shots, LANES)
        ).reshape(BLOCK, shots, LANES)
        adj_m[t, pl.ds(c + 1, BLOCK)] = mask[pl.ds(c, BLOCK)] * (b - recorded)

    for t in range(steps):
        inset = 0 if t < 2 else HALO // 2
        count = (ext - 2 * inset) // BLOCK
        for i in range(count):
            scatter_wave(t, inset + i * BLOCK)

    from_boxes(back_i, aligned_i, 1)
    reduce_i[g] = aligned_i[mine]
    shot_exchange(lambda s: aligned_i.at[pl.ds(s * share, share)], reduce_i.at[g], 0)

    def misfit_wave(t):
        return adj_m.at[t] if t == steps - 1 else adj_r.at[t]

    def residual(t, c):
        n, sides = around(misfit_wave(t + 1), c)
        shallow = jnp.where(at_top, 0.0, turn(n, 1))
        deep = jnp.where(at_bottom, 0.0, turn(n, LANES - 1))
        lap = sides + (shallow + deep) - 4.0 * n
        q = (n + n) + speed[0, pl.ds(c, BLOCK)] * lap + adj_m[t, pl.ds(c + 1, BLOCK)]
        if t + 2 < steps:
            q = q - misfit_wave(t + 2)[pl.ds(c + 1, BLOCK)]
        adj_r[t, pl.ds(c + 1, BLOCK)] = q

    for t in reversed(range(steps - 1)):
        start, stop = HALO - t, HALO + columns + t
        count = -(-(stop - start) // BLOCK)
        for i in range(count):
            residual(t, min(start + i * BLOCK, stop - BLOCK))

    def correlate_late(c, i):
        total = grad_part[pl.ds(i * BLOCK, BLOCK)] + sum(
            misfit_wave(t)[pl.ds(c + 1, BLOCK)] * accel[t, 0, pl.ds(c, BLOCK)]
            for t in range(steps)
        )
        store_rows(slab_s, 0, i, total)

    for i in range(columns // BLOCK):
        correlate_late(HALO + i * BLOCK, i)
    to_owners(slab_s, stage_s, back_s, 0, 3)

    box_arrived(back_d, 2)
    to_all(back_d, gather_d, 1)
    wait_bytes(start_in.at[pl.ds(0, n_shot - 1)], shot_recv.at[4])
    load_starts = pltpu.make_async_copy(start_in, start_smem, load_sem.at[19])
    load_starts.start()
    for gathered in (gather_d, gather_s):
        for place in (0, spare + n_box):
            for s in range(n_shot):
                gathered[s, pl.ds(place, spare)] = jnp.zeros((spare, 1, 2, LANES), F32)
    load_starts.wait()

    wait_bytes(reduce_i.at[pl.ds(0, n_shot - 1)], shot_recv.at[0])
    light = reduce_i[0]
    for s in range(1, n_shot):
        light = light + reduce_i[s]
    scale[mine] = jnp.sqrt(light + damping)
    shot_exchange(lambda s: scale.at[mine], scale.at[mine], 2)

    box_arrived(back_s, 3)
    to_all(back_s, gather_s, 3)

    def total_of(gathered, sem):
        wait_bytes(gathered.at[pl.ds(0, n_shot - 1), filled], shot_recv.at[sem])
        return sum(
            gathered[s, pl.ds(spare - start_smem[s, 0, 0], rounds), 0] for s in range(n_shot)
        )

    deep_total = total_of(gather_d, 1)
    wait_bytes(scale.at[others], shot_recv.at[2])
    out[:, 0, :, half[1]] = deep_total / scale[:, 1]
    out[:, 0, :, half[0]] = total_of(gather_s, 3) / scale[:, 0]

    for group in range(6):
        halo_sent(group)
    box_sent(tile_out, 0)
    box_sent(stage_i, 1)
    box_sent(stage_d, 2)
    box_sent(stage_s, 3)
    wait_bytes(aligned_i.at[others], shot_send.at[0])
    wait_bytes(gather_d.at[pl.ds(0, n_shot - 1), filled], shot_send.at[1])
    wait_bytes(scale.at[others], shot_send.at[2])
    wait_bytes(gather_s.at[pl.ds(0, n_shot - 1), filled], shot_send.at[3])
    wait_bytes(start_in.at[pl.ds(0, n_shot - 1)], shot_send.at[4])


def on_device(
    n_box,
    n_shot,
    u_prev,
    u_now,
    born_prev,
    born_now,
    adj_after,
    adj_last,
    velocity,
    wavelet,
    sources,
    receivers,
    observed,
    first_tile,
    reflectivity,
):
    shots, columns, depth = u_now.shape[1:]
    steps = wavelet.shape[2]
    n_rec = receivers.shape[1]
    rounds = reflectivity.shape[0]
    ext = columns + 2 * HALO
    spare = rounds - n_box
    share = rounds // n_shot

    def vmem(*dims):
        return pltpu.VMEM(dims, F32)

    pitch = ext + HALO
    plane = (shots, LANES)
    tile = (2, LANES)
    scratch = [
        pltpu.SMEM(sources.shape, jnp.int32),
        pltpu.SMEM((1, steps, shots), F32),
        vmem(2, 2, shots, pitch, LANES),
        vmem(2, 2, shots, pitch, LANES),
        vmem(2, shots, pitch, LANES),
        vmem(2, ext, LANES),
        pltpu.VMEM((3, 1, n_rec), jnp.int32),
        vmem(3, shots, steps, n_rec),
        vmem(rounds + 2, *tile),
        vmem(steps + 1, 2, ext + 2, *plane),
        vmem(steps, 2, ext, *plane),
        vmem(steps + 1, ext + 2, *plane),
        vmem(steps + 2, 2, ext + 2, *plane),
        vmem(columns, *plane),
        vmem(steps, ext + 2, *plane),
        vmem(2, ext, *plane),
        vmem(ext, *plane),
        vmem(ext, *plane),
        vmem(steps, ext // 2, *plane),
        vmem(3, steps, shots, n_rec),
        vmem(steps - 1, ext + 2, *plane),
        vmem(n_box, 2, *tile),
        vmem(n_box, 2, *tile),
        vmem(2 * n_box, 2, *tile),
        vmem(2 * n_box, 1, *tile),
        vmem(2 * n_box, 1, *tile),
        vmem(n_box, 2, *tile),
        vmem(n_box, 1, *tile),
        vmem(n_box, 1, *tile),
        vmem(n_box + 2 * spare, 2, *tile),
        vmem(n_box, 1, *tile),
        vmem(n_box, 1, *tile),
        vmem(rounds, 2, *tile),
        vmem(n_shot, share, 2, *tile),
        vmem(n_shot, n_box + 2 * spare, 1, *tile),
        vmem(n_shot, n_box + 2 * spare, 1, *tile),
        vmem(rounds, 2, *tile),
        pltpu.VMEM((1, LANES), jnp.int32),
        pltpu.VMEM((n_shot, 1, LANES), jnp.int32),
        pltpu.SMEM((n_shot, 1, LANES), jnp.int32),
        pltpu.SemaphoreType.DMA((20,)),
        pltpu.SemaphoreType.DMA((2, 6)),
        pltpu.SemaphoreType.DMA((2, 6)),
        pltpu.SemaphoreType.DMA((4,)),
        pltpu.SemaphoreType.DMA((4,)),
        pltpu.SemaphoreType.DMA((5,)),
        pltpu.SemaphoreType.DMA((5,)),
    ]
    hbm = pl.BlockSpec(memory_space=pltpu.HBM)
    return pl.pallas_call(
        functools.partial(kernel, n_box, n_shot),
        out_shape=jax.ShapeDtypeStruct(reflectivity.shape, F32),
        in_specs=[pl.BlockSpec(memory_space=pltpu.SMEM)] + [hbm] * 12,
        out_specs=pl.BlockSpec(memory_space=pltpu.VMEM),
        scratch_shapes=scratch,
        compiler_params=pltpu.CompilerParams(
            collective_id=0, has_side_effects=True, vmem_limit_bytes=60 * 1024 * 1024
        ),
    )(
        first_tile,
        sources,
        jnp.transpose(wavelet, (0, 2, 1)),
        u_prev,
        u_now,
        born_prev,
        born_now,
        adj_after,
        adj_last,
        velocity,
        receivers,
        observed,
        reflectivity,
    )


def solution(mesh):
    return jax.shard_map(
        functools.partial(on_device, mesh.shape["box"], mesh.shape["shot"]),
        mesh=mesh,
        in_specs=(
            P("shot", None, "box", None),
            P("shot", None, "box", None),
            P("shot", None, "box", None),
            P("shot", None, "box", None),
            P("shot", None, "box", None),
            P("shot", None, "box", None),
            P("shot", "box", None),
            P("shot", None, None),
            P("shot", None),
            P("shot", "box"),
            P("shot", None, None, "box"),
            P("shot"),
            P(None, "box", None, None),
        ),
        out_specs=P(None, "box", None, None),
        check_vma=False,
    )
```

```python
import functools

import jax
import jax.numpy as jnp
from jax import lax
from jax.experimental import pallas as pl
from jax.experimental.pallas import tpu as pltpu
from jax.sharding import PartitionSpec as P

damping = 1.0
LANES = 128
HALO = 8
BLOCK = 8
F32 = jnp.float32
MESH = pl.DeviceIdType.MESH


def wait_bytes(ref, sem):
    pltpu.make_async_copy(ref, ref, sem).wait()


def column_of(raw, c):
    shots, ext, lanes = raw.shape
    return raw.reshape(shots * ext, lanes)[pl.ds(c, shots, stride=ext), :]


def kernel(
    n_box,
    n_shot,
    first_tile,
    sources,
    wavelet,
    u_prev,
    u_now,
    born_prev,
    born_now,
    adj_after,
    adj_last,
    velocity,
    receivers,
    observed,
    reflectivity,
    out,
    sources_smem,
    wavelet_smem,
    raw_u,
    raw_q,
    raw_b,
    raw_v,
    rec,
    obs,
    refl,
    wave_u,
    accel,
    wave_b,
    wave_q,
    grad_part,
    adj_m,
    speed,
    image,
    mask,
    target,
    by_step,
    adj_r,
    tile_out,
    tile_in,
    slab_i,
    slab_d,
    slab_s,
    stage_i,
    stage_d,
    stage_s,
    back_i,
    back_d,
    back_s,
    aligned_i,
    reduce_i,
    gather_d,
    gather_s,
    scale,
    start_out,
    start_in,
    start_smem,
    load_sem,
    halo_send,
    halo_recv,
    box_send,
    box_recv,
    shot_send,
    shot_recv,
):
    shots, columns, depth = u_now.shape[1:]
    steps = wavelet_smem.shape[1]
    n_rec = receivers.shape[1]
    rounds = reflectivity.shape[0]
    ext = columns + 2 * HALO
    spare = rounds - n_box
    share = rounds // n_shot
    g = lax.axis_index("shot")
    p = lax.axis_index("box")
    last = n_box - 1

    barrier = pltpu.get_barrier_semaphore()

    def greet_box(k, carry):
        pl.semaphore_signal(
            barrier, inc=1, device_id={"box": lax.rem(p + k, n_box)}, device_id_type=MESH
        )
        return carry

    def greet_shot(k, carry):
        pl.semaphore_signal(
            barrier, inc=1, device_id={"shot": lax.rem(g + k, n_shot)}, device_id_type=MESH
        )
        return carry

    lax.fori_loop(1, n_box, greet_box, 0, unroll=n_box - 1)
    lax.fori_loop(1, n_shot, greet_shot, 0, unroll=n_shot - 1)

    loads = []

    def load(src, dst):
        copy = pltpu.make_async_copy(src, dst, load_sem.at[len(loads)])
        copy.start()
        loads.append(copy)
        return copy

    half = [pl.ds(0, LANES), pl.ds(LANES, LANES)]
    own = pl.ds(HALO, columns)
    load_refl = load(reflectivity.at[:, 0, :, half[0]], refl.at[pl.ds(1, rounds)])
    load_v = [load(velocity.at[0, :, half[h]], raw_v.at[h, own]) for h in range(2)]
    load_u = [
        load(field.at[0, :, :, half[h]], raw_u.at[f, h, :, own])
        for f, field in enumerate((u_prev, u_now))
        for h in range(2)
    ]
    load_s = [load(sources, sources_smem), load(wavelet, wavelet_smem)]
    load_r = [load(receivers, rec.at[1]), load(observed.at[0], obs.at[1])]
    load_q = [
        load(field.at[0, :, :, half[h]], raw_q.at[f, h, :, own])
        for f, field in enumerate((adj_after, adj_last))
        for h in range(2)
    ]
    load_b = [
        load(field.at[0, :, :, half[0]], raw_b.at[f, :, own])
        for f, field in enumerate((born_prev, born_now))
    ]

    for edge, place, side in ((0, 0, 0), (last, HALO + columns, 2)):

        @pl.when(p == edge)
        def _():
            strip = pl.ds(place, HALO)
            raw_v[:, strip] = jnp.zeros((2, HALO, LANES), F32)
            raw_b[:, :, strip] = jnp.zeros((2, shots, HALO, LANES), F32)
            for f in range(2):
                raw_u[f, :, :, strip] = jnp.zeros((2, shots, HALO, LANES), F32)
                raw_q[f, :, :, strip] = jnp.zeros((2, shots, HALO, LANES), F32)
            rec[side] = jnp.full((1, n_rec), -1, jnp.int32)
            obs[side] = jnp.zeros((shots, steps, n_rec), F32)

    refl[0] = jnp.zeros((2, LANES), F32)
    refl[rounds + 1] = jnp.zeros((2, LANES), F32)

    first = first_tile[0]
    rotation = lax.rem(first, n_box)
    first_round = lax.div(first, n_box) + (p < rotation).astype(jnp.int32)
    lead = lax.rem(p - first + 3 + 64 * n_box, n_box)
    source_round = lax.div(first - 3 + lead - p + 64 * n_box, n_box) - 64

    load_refl.wait()
    tile_out[:, 0] = refl[pl.ds(source_round + 1, n_box)]
    tile_out[:, 1] = refl[pl.ds(source_round + 2, n_box)]
    tile_in[p] = tile_out[p]

    pl.semaphore_wait(barrier, n_box - 1 + n_shot - 1)

    def box_exchange(staged, landing, place, sem):
        def send(k, carry):
            target_device = lax.rem(p + k, n_box)
            pltpu.make_async_remote_copy(
                src_ref=staged.at[target_device],
                dst_ref=landing.at[place],
                send_sem=box_send.at[sem],
                recv_sem=box_recv.at[sem],
                device_id={"box": target_device},
                device_id_type=MESH,
            ).start()
            return carry

        lax.fori_loop(1, n_box, send, 0, unroll=n_box - 1)

    def box_sent(staged, sem):
        wait_bytes(staged.at[pl.ds(0, n_box - 1)], box_send.at[sem])

    def box_arrived(landing, sem):
        wait_bytes(landing.at[pl.ds(0, n_box - 1)], box_recv.at[sem])

    left_edge, right_edge = pl.ds(0, HALO), pl.ds(columns - HALO, HALO)
    left_halo, right_halo = pl.ds(0, HALO), pl.ds(HALO + columns, HALO)

    def halo_pieces(edge, halo, side):
        yield 0, [
            (field.at[0, :, edge, half[h]], raw_u.at[f, h, :, halo])
            for f, field in enumerate((u_prev, u_now))
            for h in range(2)
        ]
        yield 1, [(velocity.at[0, edge, half[h]], raw_v.at[h, halo]) for h in range(2)]
        shift = HALO // 2 if side == 0 else 0
        near = pl.ds(edge.start + shift, HALO // 2)
        there = pl.ds(halo.start + shift, HALO // 2)
        yield 2, [
            (field.at[0, :, near, half[h]], raw_q.at[f, h, :, there])
            for f, field in enumerate((adj_after, adj_last))
            for h in range(2)
        ]
        yield 3, [
            (field.at[0, :, edge, half[0]], raw_b.at[f, :, halo])
            for f, field in enumerate((born_prev, born_now))
        ]
        yield 4, [(receivers, rec.at[side])]
        yield 5, [(observed.at[0], obs.at[side])]

    def halo_refs(group, edge_side):
        halo = (left_halo, right_halo)[edge_side]
        side = (0, 2)[edge_side]
        return (
            raw_u.at[:, :, :, halo],
            raw_v.at[:, halo],
            raw_q.at[:, :, :, pl.ds(halo.start + (HALO // 2 if side == 0 else 0), HALO // 2)],
            raw_b.at[:, :, halo],
            rec.at[side],
            obs.at[side],
        )[group]

    def send_halo(direction, groups):
        edge, halo, side = (
            (left_edge, right_halo, 2),
            (right_edge, left_halo, 0),
        )[direction]
        neighbour = (p - 1, p + 1)[direction]
        for group, pieces in halo_pieces(edge, halo, side):
            if group not in groups:
                continue
            for src, dst in pieces:
                pltpu.make_async_remote_copy(
                    src_ref=src,
                    dst_ref=dst,
                    send_sem=halo_send.at[direction, group],
                    recv_sem=halo_recv.at[direction, group],
                    device_id={"box": neighbour},
                    device_id_type=MESH,
                ).start()

    def send_halos(groups):
        @pl.when(p > 0)
        def _():
            send_halo(0, groups)

        @pl.when(p < last)
        def _():
            send_halo(1, groups)

    send_halos((0, 1))
    box_exchange(tile_out, tile_in, p, 0)
    start_out[...] = jnp.full((1, LANES), first_round, jnp.int32)
    start_in[g] = start_out[...]
    send_halos((2, 3, 4, 5))

    blank = jnp.zeros((shots, LANES), F32)
    for pad in (0, ext + 1):
        for level in range(2):
            wave_b[level, pad] = blank
        for level in range(steps):
            adj_m[level, pad] = blank
    for c in (0, 1, ext - 2, ext - 1):
        image[c] = blank
    for back in (back_i,):
        for place in (0, spare + n_box):
            back[pl.ds(place, spare)] = jnp.zeros((spare,) + back.shape[1:], F32)

    def halo_arrived(group):
        @pl.when(p < last)
        def _():
            wait_bytes(halo_refs(group, 1), halo_recv.at[0, group])

        @pl.when(p > 0)
        def _():
            wait_bytes(halo_refs(group, 0), halo_recv.at[1, group])

    def halo_sent(group):
        @pl.when(p > 0)
        def _():
            wait_bytes(halo_refs(group, 1), halo_send.at[0, group])

        @pl.when(p < last)
        def _():
            wait_bytes(halo_refs(group, 0), halo_send.at[1, group])

    lane = lax.broadcasted_iota(jnp.int32, (shots, LANES), 1)
    at_top = lane == 0
    at_bottom = lane == LANES - 1
    shot_row = lax.broadcasted_iota(jnp.int32, (shots, LANES), 0)
    first_cell = (p * columns - HALO) * depth

    def by_columns(raw, working, start, count):
        def move(c, carry):
            working[start + c + 1] = column_of(raw, start + c)
            return carry

        lax.fori_loop(0, count, move, 0, unroll=min(count, 16))

    def widen(start, count):
        for h in range(2):

            def spread(c, carry):
                speed[h, start + c] = jnp.broadcast_to(
                    raw_v[h, pl.ds(start + c, 1), :], (shots, LANES)
                )
                return carry

            lax.fori_loop(0, count, spread, 0, unroll=min(count, 16))

    for copy in load_s:
        copy.wait()
    source_cell = jnp.zeros((shots, LANES), jnp.int32)
    pulses = [jnp.zeros((shots, LANES), F32) for _ in range(steps)]
    for s in range(shots):
        source_cell = jnp.where(shot_row == s, sources_smem[0, s], source_cell)
        for t in range(steps):
            pulses[t] = jnp.where(shot_row == s, wavelet_smem[0, t, s], pulses[t])
    source_cell = source_cell - first_cell - lane

    def blocks(body, start, stop, unroll):
        count = -(-(stop - start) // BLOCK)

        def step(i, carry):
            body(jnp.minimum(start + i * BLOCK, stop - BLOCK), i)
            return carry

        lax.fori_loop(0, count, step, 0, unroll=unroll if count % unroll == 0 else 1)

    def turn(x, by):
        return pltpu.roll(x, by, axis=2)

    def around(wave, c):
        wide = wave[pl.ds(c, BLOCK + 2)]
        return wide[1 : BLOCK + 1], wide[:BLOCK] + wide[2:]

    def lap_both(wave, level, c):
        pairs = [around(wave.at[level, h], c) for h in range(2)]
        n = [pair[0] for pair in pairs]
        down = [turn(n[h], 1) for h in range(2)]
        up = [turn(n[h], LANES - 1) for h in range(2)]
        shallow = [jnp.where(at_top, 0.0, down[0]), jnp.where(at_top, down[0], down[1])]
        deep = [jnp.where(at_bottom, up[1], up[0]), jnp.where(at_bottom, 0.0, up[1])]
        laps = [pairs[h][1] + (shallow[h] + deep[h]) - 4.0 * n[h] for h in range(2)]
        return n, laps

    def lap_top(wave, level, c, closed):
        n, sides = around(wave.at[level], c)
        shallow = jnp.where(at_top, 0.0, turn(n, 1))
        deep = turn(n, LANES - 1)
        if closed:
            deep = jnp.where(at_bottom, 0.0, deep)
        return n, sides + (shallow + deep) - 4.0 * n

    def store_rows(slab, kind, i, block):
        for r in range(BLOCK):
            row = jnp.sum(block[r], axis=0, keepdims=True)
            j = i * (BLOCK // 2) + r // 2
            slab[j, kind, pl.ds(r % 2, 1), :] = row
            slab[j + n_box, kind, pl.ds(r % 2, 1), :] = row

    turned = lax.rem(n_box - rotation, n_box)

    def to_owners(slab, staged, back, place, sem):
        staged[...] = slab[pl.ds(turned, n_box)]
        back[place + p] = staged[p]
        box_exchange(staged, back, place + p, sem)

    def from_boxes(back, aligned, sem):
        box_arrived(back, sem)
        aligned[...] = back[pl.ds(spare - first_round, rounds)]

    def shot_exchange(src_of, landing, sem):
        def send(k, carry):
            s = lax.rem(g + k, n_shot)
            pltpu.make_async_remote_copy(
                src_ref=src_of(s),
                dst_ref=landing,
                send_sem=shot_send.at[sem],
                recv_sem=shot_recv.at[sem],
                device_id={"shot": s},
                device_id_type=MESH,
            ).start()
            return carry

        lax.fori_loop(1, n_shot, send, 0, unroll=n_shot - 1)

    filled = pl.ds(spare, n_box)

    def to_all(back, gathered, sem):
        shot_exchange(lambda s: back, gathered.at[g, filled], sem)
        gathered[g, filled] = back[...]

    shot_exchange(lambda s: start_out, start_in.at[g], 4)
    mine = pl.ds(g * share, share)
    others = pl.ds(0, (n_shot - 1) * share)
    cell_step = lax.broadcasted_iota(jnp.int32, (BLOCK, shots, LANES), 0) * depth

    def advance(t, c):
        n, laps = lap_both(wave_u, t + 1, c)
        for h in range(2):
            offset = (source_cell - (c * depth + h * LANES))[None]
            a = speed[h, pl.ds(c, BLOCK)] * laps[h] + jnp.where(
                offset == cell_step, pulses[t][None], 0.0
            )
            accel[t, h, pl.ds(c, BLOCK)] = a
            if t < steps - 1:
                wave_u[t + 2, h, pl.ds(c + 1, BLOCK)] = (
                    (n[h] + n[h]) - wave_u[t, h, pl.ds(c + 1, BLOCK)]
                ) + a

    for copy in load_u + load_v:
        copy.wait()
    widen(HALO, columns)
    for h in range(2):
        for level in range(2):
            by_columns(raw_u.at[level, h], wave_u.at[level, h], HALO, columns)
    for t in range(steps):
        blocks(lambda c, i: advance(t, c), HALO + 1 + t, HALO + columns - 1 - t, 8 if t < 3 else 7)
    halo_arrived(0)
    halo_arrived(1)
    for start in (0, HALO + columns):
        widen(start, HALO)
        for h in range(2):
            for level in range(2):
                by_columns(raw_u.at[level, h], wave_u.at[level, h], start, HALO)
    for t in range(steps):
        advance(t, 1 + t)
        advance(t, HALO + columns - 1 - t)

    def brighten(c, i):
        for h in range(2):
            a = [accel[t, h, pl.ds(c, BLOCK)] for t in range(steps)]
            store_rows(slab_i, h, i, sum(x * x for x in a))

    blocks(brighten, HALO, HALO + columns, 2)
    to_owners(slab_i, stage_i, back_i, spare, 1)

    for copy in load_q:
        copy.wait()
    halo_arrived(2)
    for h in range(2):
        for level in range(2):
            by_columns(raw_q.at[level, h], wave_q.at[level, h], 0, ext)

    def retreat(k, c):
        n, laps = lap_both(wave_q, k + 1, c)
        for h in range(2):
            wave_q[k + 2, h, pl.ds(c + 1, BLOCK)] = (
                (n[h] + n[h]) - wave_q[k, h, pl.ds(c + 1, BLOCK)]
            ) + speed[h, pl.ds(c, BLOCK)] * laps[h]

    for k in range(steps):
        blocks(lambda c, i: retreat(k, c), HALO - 3 + k, HALO + columns + 3 - k, 9 if k < 3 else 8)

    def correlate(c, i):
        products = [
            sum(
                wave_q[steps + 1 - t, h, pl.ds(c + 1, BLOCK)] * accel[t, h, pl.ds(c, BLOCK)]
                for t in range(steps)
            )
            for h in range(2)
        ]
        store_rows(slab_d, 0, i, products[1])
        grad_part[pl.ds(i * BLOCK, BLOCK)] = products[0]

    blocks(correlate, HALO, HALO + columns, 2)
    to_owners(slab_d, stage_d, back_d, 0, 2)

    for copy in load_r + load_b:
        copy.wait()
    halo_arrived(4)
    halo_arrived(5)
    halo_arrived(3)
    by_columns(raw_b.at[0], wave_b.at[0], 0, ext)
    by_columns(raw_b.at[1], wave_b.at[1], 0, ext)
    beside = HALO // 2
    heard = (
        [(0, n_rec - beside + r) for r in range(beside)]
        + [(1, r) for r in range(n_rec)]
        + [(2, r) for r in range(beside)]
    )
    for side in range(3):
        for t in range(steps):
            by_step[side, t] = obs[side, :, t, :]
    cells = [jnp.broadcast_to(rec[side], (shots, n_rec)) for side in range(3)]
    data = [[by_step[side, t] for t in range(steps)] for side in range(3)]
    for slot, (side, r) in enumerate(heard):
        cell = jnp.broadcast_to(cells[side][:, r : r + 1], (shots, LANES)) - first_cell - lane
        for t in range(steps):
            target[t, slot] = jnp.broadcast_to(data[side][t][:, r : r + 1], (shots, LANES))
        for w in range(2):
            c = 2 * slot + w
            mask[c] = jnp.where(cell == c * depth, 1.0, 0.0)

    box_arrived(tile_in, 0)
    for j in range(n_box + 6):
        owner = lax.rem(rotation + j - 3 + n_box, n_box)
        tile = tile_in[owner, j // n_box]
        for w in range(2):
            image[HALO - 6 + 2 * j + w] = jnp.broadcast_to(tile[w : w + 1], (shots, LANES))

    def scatter_wave(t, c):
        n, lap = lap_top(wave_b, t + 1, c, False)
        b = (
            ((n + n) - wave_b[t, pl.ds(c + 1, BLOCK)])
            + speed[0, pl.ds(c, BLOCK)] * lap
            + image[pl.ds(c, BLOCK)] * accel[t, 0, pl.ds(c, BLOCK)]
        )
        if t < steps - 1:
            wave_b[t + 2, pl.ds(c + 1, BLOCK)] = b
        recorded = target[t, pl.ds(c // 2, BLOCK // 2)]
        recorded = jnp.broadcast_to(
            recorded[:, None], (BLOCK // 2, 2, shots, LANES)
        ).reshape(BLOCK, shots, LANES)
        adj_m[t, pl.ds(c + 1, BLOCK)] = mask[pl.ds(c, BLOCK)] * (b - recorded)

    for t in range(steps):
        inset = 0 if t < 2 else HALO // 2
        count = (ext - 2 * inset) // BLOCK
        for i in range(count):
            scatter_wave(t, inset + i * BLOCK)

    from_boxes(back_i, aligned_i, 1)
    reduce_i[g] = aligned_i[mine]
    shot_exchange(lambda s: aligned_i.at[pl.ds(s * share, share)], reduce_i.at[g], 0)

    def misfit_wave(t):
        return adj_m.at[t] if t == steps - 1 else adj_r.at[t]

    def residual(t, c):
        n, sides = around(misfit_wave(t + 1), c)
        shallow = jnp.where(at_top, 0.0, turn(n, 1))
        deep = jnp.where(at_bottom, 0.0, turn(n, LANES - 1))
        lap = sides + (shallow + deep) - 4.0 * n
        q = (n + n) + speed[0, pl.ds(c, BLOCK)] * lap + adj_m[t, pl.ds(c + 1, BLOCK)]
        if t + 2 < steps:
            q = q - misfit_wave(t + 2)[pl.ds(c + 1, BLOCK)]
        adj_r[t, pl.ds(c + 1, BLOCK)] = q

    for t in reversed(range(steps - 1)):
        start, stop = HALO - t, HALO + columns + t
        count = -(-(stop - start) // BLOCK)
        for i in range(count):
            residual(t, min(start + i * BLOCK, stop - BLOCK))

    def correlate_late(c, i):
        total = grad_part[pl.ds(i * BLOCK, BLOCK)] + sum(
            misfit_wave(t)[pl.ds(c + 1, BLOCK)] * accel[t, 0, pl.ds(c, BLOCK)]
            for t in range(steps)
        )
        store_rows(slab_s, 0, i, total)

    for i in range(columns // BLOCK):
        correlate_late(HALO + i * BLOCK, i)
    to_owners(slab_s, stage_s, back_s, 0, 3)

    box_arrived(back_d, 2)
    to_all(back_d, gather_d, 1)
    wait_bytes(start_in.at[pl.ds(0, n_shot - 1)], shot_recv.at[4])
    load_starts = pltpu.make_async_copy(start_in, start_smem, load_sem.at[19])
    load_starts.start()
    for gathered in (gather_d, gather_s):
        for place in (0, spare + n_box):
            for s in range(n_shot):
                gathered[s, pl.ds(place, spare)] = jnp.zeros((spare, 1, 2, LANES), F32)
    load_starts.wait()

    wait_bytes(reduce_i.at[pl.ds(0, n_shot - 1)], shot_recv.at[0])
    light = reduce_i[0]
    for s in range(1, n_shot):
        light = light + reduce_i[s]
    scale[mine] = jnp.sqrt(light + damping)
    shot_exchange(lambda s: scale.at[mine], scale.at[mine], 2)

    box_arrived(back_s, 3)
    to_all(back_s, gather_s, 3)

    def total_of(gathered, sem):
        wait_bytes(gathered.at[pl.ds(0, n_shot - 1), filled], shot_recv.at[sem])
        return sum(
            gathered[s, pl.ds(spare - start_smem[s, 0, 0], rounds), 0] for s in range(n_shot)
        )

    deep_total = total_of(gather_d, 1)
    wait_bytes(scale.at[others], shot_recv.at[2])
    out[:, 0, :, half[1]] = deep_total / scale[:, 1]
    out[:, 0, :, half[0]] = total_of(gather_s, 3) / scale[:, 0]

    for group in range(6):
        halo_sent(group)
    box_sent(tile_out, 0)
    box_sent(stage_i, 1)
    box_sent(stage_d, 2)
    box_sent(stage_s, 3)
    wait_bytes(aligned_i.at[others], shot_send.at[0])
    wait_bytes(gather_d.at[pl.ds(0, n_shot - 1), filled], shot_send.at[1])
    wait_bytes(scale.at[others], shot_send.at[2])
    wait_bytes(gather_s.at[pl.ds(0, n_shot - 1), filled], shot_send.at[3])
    wait_bytes(start_in.at[pl.ds(0, n_shot - 1)], shot_send.at[4])


def on_device(
    n_box,
    n_shot,
    u_prev,
    u_now,
    born_prev,
    born_now,
    adj_after,
    adj_last,
    velocity,
    wavelet,
    sources,
    receivers,
    observed,
    first_tile,
    reflectivity,
):
    shots, columns, depth = u_now.shape[1:]
    steps = wavelet.shape[2]
    n_rec = receivers.shape[1]
    rounds = reflectivity.shape[0]
    ext = columns + 2 * HALO
    spare = rounds - n_box
    share = rounds // n_shot

    def vmem(*dims):
        return pltpu.VMEM(dims, F32)

    pitch = ext + HALO
    plane = (shots, LANES)
    tile = (2, LANES)
    scratch = [
        pltpu.SMEM(sources.shape, jnp.int32),
        pltpu.SMEM((1, steps, shots), F32),
        vmem(2, 2, shots, pitch, LANES),
        vmem(2, 2, shots, pitch, LANES),
        vmem(2, shots, pitch, LANES),
        vmem(2, ext, LANES),
        pltpu.VMEM((3, 1, n_rec), jnp.int32),
        vmem(3, shots, steps, n_rec),
        vmem(rounds + 2, *tile),
        vmem(steps + 1, 2, ext + 2, *plane),
        vmem(steps, 2, ext, *plane),
        vmem(steps + 1, ext + 2, *plane),
        vmem(steps + 2, 2, ext + 2, *plane),
        vmem(columns, *plane),
        vmem(steps, ext + 2, *plane),
        vmem(2, ext, *plane),
        vmem(ext, *plane),
        vmem(ext, *plane),
        vmem(steps, ext // 2, *plane),
        vmem(3, steps, shots, n_rec),
        vmem(steps - 1, ext + 2, *plane),
        vmem(n_box, 2, *tile),
        vmem(n_box, 2, *tile),
        vmem(2 * n_box, 2, *tile),
        vmem(2 * n_box, 1, *tile),
        vmem(2 * n_box, 1, *tile),
        vmem(n_box, 2, *tile),
        vmem(n_box, 1, *tile),
        vmem(n_box, 1, *tile),
        vmem(n_box + 2 * spare, 2, *tile),
        vmem(n_box, 1, *tile),
        vmem(n_box, 1, *tile),
        vmem(rounds, 2, *tile),
        vmem(n_shot, share, 2, *tile),
        vmem(n_shot, n_box + 2 * spare, 1, *tile),
        vmem(n_shot, n_box + 2 * spare, 1, *tile),
        vmem(rounds, 2, *tile),
        pltpu.VMEM((1, LANES), jnp.int32),
        pltpu.VMEM((n_shot, 1, LANES), jnp.int32),
        pltpu.SMEM((n_shot, 1, LANES), jnp.int32),
        pltpu.SemaphoreType.DMA((20,)),
        pltpu.SemaphoreType.DMA((2, 6)),
        pltpu.SemaphoreType.DMA((2, 6)),
        pltpu.SemaphoreType.DMA((4,)),
        pltpu.SemaphoreType.DMA((4,)),
        pltpu.SemaphoreType.DMA((5,)),
        pltpu.SemaphoreType.DMA((5,)),
    ]
    hbm = pl.BlockSpec(memory_space=pltpu.HBM)
    return pl.pallas_call(
        functools.partial(kernel, n_box, n_shot),
        out_shape=jax.ShapeDtypeStruct(reflectivity.shape, F32),
        in_specs=[pl.BlockSpec(memory_space=pltpu.SMEM)] + [hbm] * 12,
        out_specs=pl.BlockSpec(memory_space=pltpu.VMEM),
        scratch_shapes=scratch,
        compiler_params=pltpu.CompilerParams(
            collective_id=0, has_side_effects=True, vmem_limit_bytes=60 * 1024 * 1024
        ),
    )(
        first_tile,
        sources,
        jnp.transpose(wavelet, (0, 2, 1)),
        u_prev,
        u_now,
        born_prev,
        born_now,
        adj_after,
        adj_last,
        velocity,
        receivers,
        observed,
        reflectivity,
    )


def solution(mesh):
    return jax.shard_map(
        functools.partial(on_device, mesh.shape["box"], mesh.shape["shot"]),
        mesh=mesh,
        in_specs=(
            P("shot", None, "box", None),
            P("shot", None, "box", None),
            P("shot", None, "box", None),
            P("shot", None, "box", None),
            P("shot", None, "box", None),
            P("shot", None, "box", None),
            P("shot", "box", None),
            P("shot", None, None),
            P("shot", None),
            P("shot", "box"),
            P("shot", None, None, "box"),
            P("shot"),
            P(None, "box", None, None),
        ),
        out_specs=P(None, "box", None, None),
        check_vma=False,
    )
```

```python
import functools

import jax
import jax.numpy as jnp
from jax import lax
from jax.experimental import pallas as pl
from jax.experimental.pallas import tpu as pltpu
from jax.sharding import PartitionSpec as P

damping = 1.0
LANES = 128
HALO = 8
BLOCK = 8
F32 = jnp.float32
MESH = pl.DeviceIdType.MESH


def wait_bytes(ref, sem):
    pltpu.make_async_copy(ref, ref, sem).wait()


def column_of(raw, c):
    shots, ext, lanes = raw.shape
    return raw.reshape(shots * ext, lanes)[pl.ds(c, shots, stride=ext), :]


def kernel(
    n_box,
    n_shot,
    first_tile,
    sources,
    wavelet,
    u_prev,
    u_now,
    born_prev,
    born_now,
    adj_after,
    adj_last,
    velocity,
    receivers,
    observed,
    reflectivity,
    out,
    sources_smem,
    wavelet_smem,
    raw_u,
    raw_q,
    raw_b,
    raw_v,
    rec,
    obs,
    refl,
    wave_u,
    accel,
    wave_b,
    wave_q,
    grad_part,
    adj_m,
    speed,
    image,
    mask,
    target,
    by_step,
    adj_r,
    tile_out,
    tile_in,
    slab_i,
    slab_d,
    slab_s,
    stage_i,
    stage_d,
    stage_s,
    back_i,
    back_d,
    back_s,
    aligned_i,
    reduce_i,
    gather_d,
    gather_s,
    scale,
    start_out,
    start_in,
    start_smem,
    load_sem,
    halo_send,
    halo_recv,
    box_send,
    box_recv,
    shot_send,
    shot_recv,
):
    shots, columns, depth = u_now.shape[1:]
    steps = wavelet_smem.shape[1]
    n_rec = receivers.shape[1]
    rounds = reflectivity.shape[0]
    ext = columns + 2 * HALO
    spare = rounds - n_box
    share = rounds // n_shot
    g = lax.axis_index("shot")
    p = lax.axis_index("box")
    last = n_box - 1

    barrier = pltpu.get_barrier_semaphore()

    def greet_box(k, carry):
        pl.semaphore_signal(
            barrier, inc=1, device_id={"box": lax.rem(p + k, n_box)}, device_id_type=MESH
        )
        return carry

    def greet_shot(k, carry):
        pl.semaphore_signal(
            barrier, inc=1, device_id={"shot": lax.rem(g + k, n_shot)}, device_id_type=MESH
        )
        return carry

    lax.fori_loop(1, n_box, greet_box, 0, unroll=n_box - 1)
    lax.fori_loop(1, n_shot, greet_shot, 0, unroll=n_shot - 1)

    loads = []

    def load(src, dst):
        copy = pltpu.make_async_copy(src, dst, load_sem.at[len(loads)])
        copy.start()
        loads.append(copy)
        return copy

    half = [pl.ds(0, LANES), pl.ds(LANES, LANES)]
    own = pl.ds(HALO, columns)
    load_refl = load(reflectivity.at[:, 0, :, half[0]], refl.at[pl.ds(1, rounds)])
    load_v = [load(velocity.at[0, :, half[h]], raw_v.at[h, own]) for h in range(2)]
    load_u = [
        load(field.at[0, :, :, half[h]], raw_u.at[f, h, :, own])
        for f, field in enumerate((u_prev, u_now))
        for h in range(2)
    ]
    load_s = [load(sources, sources_smem), load(wavelet, wavelet_smem)]
    load_r = [load(receivers, rec.at[1]), load(observed.at[0], obs.at[1])]
    load_q = [
        load(field.at[0, :, :, half[h]], raw_q.at[f, h, :, own])
        for f, field in enumerate((adj_after, adj_last))
        for h in range(2)
    ]
    load_b = [
        load(field.at[0, :, :, half[0]], raw_b.at[f, :, own])
        for f, field in enumerate((born_prev, born_now))
    ]

    for edge, place, side in ((0, 0, 0), (last, HALO + columns, 2)):

        @pl.when(p == edge)
        def _():
            strip = pl.ds(place, HALO)
            raw_v[:, strip] = jnp.zeros((2, HALO, LANES), F32)
            raw_b[:, :, strip] = jnp.zeros((2, shots, HALO, LANES), F32)
            for f in range(2):
                raw_u[f, :, :, strip] = jnp.zeros((2, shots, HALO, LANES), F32)
                raw_q[f, :, :, strip] = jnp.zeros((2, shots, HALO, LANES), F32)
            rec[side] = jnp.full((1, n_rec), -1, jnp.int32)
            obs[side] = jnp.zeros((shots, steps, n_rec), F32)

    refl[0] = jnp.zeros((2, LANES), F32)
    refl[rounds + 1] = jnp.zeros((2, LANES), F32)

    first = first_tile[0]
    rotation = lax.rem(first, n_box)
    first_round = lax.div(first, n_box) + (p < rotation).astype(jnp.int32)
    lead = lax.rem(p - first + 3 + 64 * n_box, n_box)
    source_round = lax.div(first - 3 + lead - p + 64 * n_box, n_box) - 64

    load_refl.wait()
    tile_out[:, 0] = refl[pl.ds(source_round + 1, n_box)]
    tile_out[:, 1] = refl[pl.ds(source_round + 2, n_box)]
    tile_in[p] = tile_out[p]

    pl.semaphore_wait(barrier, n_box - 1 + n_shot - 1)

    def box_exchange(staged, landing, place, sem):
        def send(k, carry):
            target_device = lax.rem(p + k, n_box)
            pltpu.make_async_remote_copy(
                src_ref=staged.at[target_device],
                dst_ref=landing.at[place],
                send_sem=box_send.at[sem],
                recv_sem=box_recv.at[sem],
                device_id={"box": target_device},
                device_id_type=MESH,
            ).start()
            return carry

        lax.fori_loop(1, n_box, send, 0, unroll=n_box - 1)

    def box_sent(staged, sem):
        wait_bytes(staged.at[pl.ds(0, n_box - 1)], box_send.at[sem])

    def box_arrived(landing, sem):
        wait_bytes(landing.at[pl.ds(0, n_box - 1)], box_recv.at[sem])

    left_edge, right_edge = pl.ds(0, HALO), pl.ds(columns - HALO, HALO)
    left_halo, right_halo = pl.ds(0, HALO), pl.ds(HALO + columns, HALO)

    def halo_pieces(edge, halo, side):
        yield 0, [
            (field.at[0, :, edge, half[h]], raw_u.at[f, h, :, halo])
            for f, field in enumerate((u_prev, u_now))
            for h in range(2)
        ]
        yield 1, [(velocity.at[0, edge, half[h]], raw_v.at[h, halo]) for h in range(2)]
        shift = HALO // 2 if side == 0 else 0
        near = pl.ds(edge.start + shift, HALO // 2)
        there = pl.ds(halo.start + shift, HALO // 2)
        yield 2, [
            (field.at[0, :, near, half[h]], raw_q.at[f, h, :, there])
            for f, field in enumerate((adj_after, adj_last))
            for h in range(2)
        ]
        yield 3, [
            (field.at[0, :, edge, half[0]], raw_b.at[f, :, halo])
            for f, field in enumerate((born_prev, born_now))
        ]
        yield 4, [(receivers, rec.at[side])]
        yield 5, [(observed.at[0], obs.at[side])]

    def halo_refs(group, edge_side):
        halo = (left_halo, right_halo)[edge_side]
        side = (0, 2)[edge_side]
        return (
            raw_u.at[:, :, :, halo],
            raw_v.at[:, halo],
            raw_q.at[:, :, :, pl.ds(halo.start + (HALO // 2 if side == 0 else 0), HALO // 2)],
            raw_b.at[:, :, halo],
            rec.at[side],
            obs.at[side],
        )[group]

    def send_halo(direction, groups):
        edge, halo, side = (
            (left_edge, right_halo, 2),
            (right_edge, left_halo, 0),
        )[direction]
        neighbour = (p - 1, p + 1)[direction]
        for group, pieces in halo_pieces(edge, halo, side):
            if group not in groups:
                continue
            for src, dst in pieces:
                pltpu.make_async_remote_copy(
                    src_ref=src,
                    dst_ref=dst,
                    send_sem=halo_send.at[direction, group],
                    recv_sem=halo_recv.at[direction, group],
                    device_id={"box": neighbour},
                    device_id_type=MESH,
                ).start()

    def send_halos(groups):
        @pl.when(p > 0)
        def _():
            send_halo(0, groups)

        @pl.when(p < last)
        def _():
            send_halo(1, groups)

    send_halos((0, 1))
    box_exchange(tile_out, tile_in, p, 0)
    start_out[...] = jnp.full((1, LANES), first_round, jnp.int32)
    start_in[g] = start_out[...]
    send_halos((2, 3, 4, 5))

    blank = jnp.zeros((shots, LANES), F32)
    for pad in (0, ext + 1):
        for level in range(2):
            wave_b[level, pad] = blank
        for level in range(steps):
            adj_m[level, pad] = blank
    for c in (0, 1, ext - 2, ext - 1):
        image[c] = blank
    for back in (back_i,):
        for place in (0, spare + n_box):
            back[pl.ds(place, spare)] = jnp.zeros((spare,) + back.shape[1:], F32)

    def halo_arrived(group):
        @pl.when(p < last)
        def _():
            wait_bytes(halo_refs(group, 1), halo_recv.at[0, group])

        @pl.when(p > 0)
        def _():
            wait_bytes(halo_refs(group, 0), halo_recv.at[1, group])

    def halo_sent(group):
        @pl.when(p > 0)
        def _():
            wait_bytes(halo_refs(group, 1), halo_send.at[0, group])

        @pl.when(p < last)
        def _():
            wait_bytes(halo_refs(group, 0), halo_send.at[1, group])

    lane = lax.broadcasted_iota(jnp.int32, (shots, LANES), 1)
    at_top = lane == 0
    at_bottom = lane == LANES - 1
    shot_row = lax.broadcasted_iota(jnp.int32, (shots, LANES), 0)
    first_cell = (p * columns - HALO) * depth

    def by_columns(raw, working, start, count):
        def move(c, carry):
            working[start + c + 1] = column_of(raw, start + c)
            return carry

        lax.fori_loop(0, count, move, 0, unroll=count)

    def widen(start, count):
        for h in range(2):

            def spread(c, carry):
                speed[h, start + c] = jnp.broadcast_to(
                    raw_v[h, pl.ds(start + c, 1), :], (shots, LANES)
                )
                return carry

            lax.fori_loop(0, count, spread, 0, unroll=count)

    for copy in load_s:
        copy.wait()
    source_cell = jnp.zeros((shots, LANES), jnp.int32)
    pulses = [jnp.zeros((shots, LANES), F32) for _ in range(steps)]
    for s in range(shots):
        source_cell = jnp.where(shot_row == s, sources_smem[0, s], source_cell)
        for t in range(steps):
            pulses[t] = jnp.where(shot_row == s, wavelet_smem[0, t, s], pulses[t])
    source_cell = source_cell - first_cell - lane

    def blocks(body, start, stop, unroll):
        count = -(-(stop - start) // BLOCK)

        def step(i, carry):
            body(jnp.minimum(start + i * BLOCK, stop - BLOCK), i)
            return carry

        lax.fori_loop(0, count, step, 0, unroll=unroll if count % unroll == 0 else 1)

    def turn(x, by):
        return pltpu.roll(x, by, axis=2)

    def around(wave, c):
        wide = wave[pl.ds(c, BLOCK + 2)]
        return wide[1 : BLOCK + 1], wide[:BLOCK] + wide[2:]

    def lap_both(wave, level, c):
        pairs = [around(wave.at[level, h], c) for h in range(2)]
        n = [pair[0] for pair in pairs]
        down = [turn(n[h], 1) for h in range(2)]
        up = [turn(n[h], LANES - 1) for h in range(2)]
        shallow = [jnp.where(at_top, 0.0, down[0]), jnp.where(at_top, down[0], down[1])]
        deep = [jnp.where(at_bottom, up[1], up[0]), jnp.where(at_bottom, 0.0, up[1])]
        laps = [pairs[h][1] + (shallow[h] + deep[h]) - 4.0 * n[h] for h in range(2)]
        return n, laps

    def lap_top(wave, level, c, closed):
        n, sides = around(wave.at[level], c)
        shallow = jnp.where(at_top, 0.0, turn(n, 1))
        deep = turn(n, LANES - 1)
        if closed:
            deep = jnp.where(at_bottom, 0.0, deep)
        return n, sides + (shallow + deep) - 4.0 * n

    def store_rows(slab, kind, i, block):
        for r in range(BLOCK):
            row = jnp.sum(block[r], axis=0, keepdims=True)
            j = i * (BLOCK // 2) + r // 2
            slab[j, kind, pl.ds(r % 2, 1), :] = row
            slab[j + n_box, kind, pl.ds(r % 2, 1), :] = row

    turned = lax.rem(n_box - rotation, n_box)

    def to_owners(slab, staged, back, place, sem):
        staged[...] = slab[pl.ds(turned, n_box)]
        back[place + p] = staged[p]
        box_exchange(staged, back, place + p, sem)

    def from_boxes(back, aligned, sem):
        box_arrived(back, sem)
        aligned[...] = back[pl.ds(spare - first_round, rounds)]

    def shot_exchange(src_of, landing, sem):
        def send(k, carry):
            s = lax.rem(g + k, n_shot)
            pltpu.make_async_remote_copy(
                src_ref=src_of(s),
                dst_ref=landing,
                send_sem=shot_send.at[sem],
                recv_sem=shot_recv.at[sem],
                device_id={"shot": s},
                device_id_type=MESH,
            ).start()
            return carry

        lax.fori_loop(1, n_shot, send, 0, unroll=n_shot - 1)

    filled = pl.ds(spare, n_box)

    def to_all(back, gathered, sem):
        shot_exchange(lambda s: back, gathered.at[g, filled], sem)
        gathered[g, filled] = back[...]

    shot_exchange(lambda s: start_out, start_in.at[g], 4)
    mine = pl.ds(g * share, share)
    others = pl.ds(0, (n_shot - 1) * share)
    cell_step = lax.broadcasted_iota(jnp.int32, (BLOCK, shots, LANES), 0) * depth

    def advance(t, c):
        n, laps = lap_both(wave_u, t + 1, c)
        for h in range(2):
            offset = (source_cell - (c * depth + h * LANES))[None]
            a = speed[h, pl.ds(c, BLOCK)] * laps[h] + jnp.where(
                offset == cell_step, pulses[t][None], 0.0
            )
            accel[t, h, pl.ds(c, BLOCK)] = a
            if t < steps - 1:
                wave_u[t + 2, h, pl.ds(c + 1, BLOCK)] = (
                    (n[h] + n[h]) - wave_u[t, h, pl.ds(c + 1, BLOCK)]
                ) + a

    for copy in load_u + load_v:
        copy.wait()
    widen(HALO, columns)
    for h in range(2):
        for level in range(2):
            by_columns(raw_u.at[level, h], wave_u.at[level, h], HALO, columns)
    for t in range(steps):
        blocks(lambda c, i: advance(t, c), HALO + 1 + t, HALO + columns - 1 - t, 8 if t < 3 else 7)
    halo_arrived(0)
    halo_arrived(1)
    for start in (0, HALO + columns):
        widen(start, HALO)
        for h in range(2):
            for level in range(2):
                by_columns(raw_u.at[level, h], wave_u.at[level, h], start, HALO)
    for t in range(steps):
        advance(t, 1 + t)
        advance(t, HALO + columns - 1 - t)

    def brighten(c, i):
        for h in range(2):
            a = [accel[t, h, pl.ds(c, BLOCK)] for t in range(steps)]
            store_rows(slab_i, h, i, sum(x * x for x in a))

    blocks(brighten, HALO, HALO + columns, 8)
    to_owners(slab_i, stage_i, back_i, spare, 1)

    for copy in load_q:
        copy.wait()
    halo_arrived(2)
    for h in range(2):
        for level in range(2):
            by_columns(raw_q.at[level, h], wave_q.at[level, h], 0, ext)

    def retreat(k, c):
        n, laps = lap_both(wave_q, k + 1, c)
        for h in range(2):
            wave_q[k + 2, h, pl.ds(c + 1, BLOCK)] = (
                (n[h] + n[h]) - wave_q[k, h, pl.ds(c + 1, BLOCK)]
            ) + speed[h, pl.ds(c, BLOCK)] * laps[h]

    for k in range(steps):
        blocks(lambda c, i: retreat(k, c), HALO - 3 + k, HALO + columns + 3 - k, 9 if k < 3 else 8)

    def correlate(c, i):
        products = [
            sum(
                wave_q[steps + 1 - t, h, pl.ds(c + 1, BLOCK)] * accel[t, h, pl.ds(c, BLOCK)]
                for t in range(steps)
            )
            for h in range(2)
        ]
        store_rows(slab_d, 0, i, products[1])
        grad_part[pl.ds(i * BLOCK, BLOCK)] = products[0]

    blocks(correlate, HALO, HALO + columns, 8)
    to_owners(slab_d, stage_d, back_d, 0, 2)

    for copy in load_r + load_b:
        copy.wait()
    halo_arrived(4)
    halo_arrived(5)
    halo_arrived(3)
    by_columns(raw_b.at[0], wave_b.at[0], 0, ext)
    by_columns(raw_b.at[1], wave_b.at[1], 0, ext)
    beside = HALO // 2
    heard = (
        [(0, n_rec - beside + r) for r in range(beside)]
        + [(1, r) for r in range(n_rec)]
        + [(2, r) for r in range(beside)]
    )
    for side in range(3):
        for t in range(steps):
            by_step[side, t] = obs[side, :, t, :]
    cells = [jnp.broadcast_to(rec[side], (shots, n_rec)) for side in range(3)]
    data = [[by_step[side, t] for t in range(steps)] for side in range(3)]
    for slot, (side, r) in enumerate(heard):
        cell = jnp.broadcast_to(cells[side][:, r : r + 1], (shots, LANES)) - first_cell - lane
        for t in range(steps):
            target[t, slot] = jnp.broadcast_to(data[side][t][:, r : r + 1], (shots, LANES))
        for w in range(2):
            c = 2 * slot + w
            mask[c] = jnp.where(cell == c * depth, 1.0, 0.0)

    box_arrived(tile_in, 0)
    for j in range(n_box + 6):
        owner = lax.rem(rotation + j - 3 + n_box, n_box)
        tile = tile_in[owner, j // n_box]
        for w in range(2):
            image[HALO - 6 + 2 * j + w] = jnp.broadcast_to(tile[w : w + 1], (shots, LANES))

    def scatter_wave(t, c):
        n, lap = lap_top(wave_b, t + 1, c, False)
        b = (
            ((n + n) - wave_b[t, pl.ds(c + 1, BLOCK)])
            + speed[0, pl.ds(c, BLOCK)] * lap
            + image[pl.ds(c, BLOCK)] * accel[t, 0, pl.ds(c, BLOCK)]
        )
        if t < steps - 1:
            wave_b[t + 2, pl.ds(c + 1, BLOCK)] = b
        recorded = target[t, pl.ds(c // 2, BLOCK // 2)]
        recorded = jnp.broadcast_to(
            recorded[:, None], (BLOCK // 2, 2, shots, LANES)
        ).reshape(BLOCK, shots, LANES)
        adj_m[t, pl.ds(c + 1, BLOCK)] = mask[pl.ds(c, BLOCK)] * (b - recorded)

    for t in range(steps):
        inset = 0 if t < 2 else HALO // 2
        count = (ext - 2 * inset) // BLOCK
        for i in range(count):
            scatter_wave(t, inset + i * BLOCK)

    from_boxes(back_i, aligned_i, 1)
    reduce_i[g] = aligned_i[mine]
    shot_exchange(lambda s: aligned_i.at[pl.ds(s * share, share)], reduce_i.at[g], 0)

    def misfit_wave(t):
        return adj_m.at[t] if t == steps - 1 else adj_r.at[t]

    def residual(t, c):
        n, sides = around(misfit_wave(t + 1), c)
        shallow = jnp.where(at_top, 0.0, turn(n, 1))
        deep = jnp.where(at_bottom, 0.0, turn(n, LANES - 1))
        lap = sides + (shallow + deep) - 4.0 * n
        q = (n + n) + speed[0, pl.ds(c, BLOCK)] * lap + adj_m[t, pl.ds(c + 1, BLOCK)]
        if t + 2 < steps:
            q = q - misfit_wave(t + 2)[pl.ds(c + 1, BLOCK)]
        adj_r[t, pl.ds(c + 1, BLOCK)] = q

    for t in reversed(range(steps - 1)):
        start, stop = HALO - t, HALO + columns + t
        count = -(-(stop - start) // BLOCK)
        for i in range(count):
            residual(t, min(start + i * BLOCK, stop - BLOCK))

    def correlate_late(c, i):
        total = grad_part[pl.ds(i * BLOCK, BLOCK)] + sum(
            misfit_wave(t)[pl.ds(c + 1, BLOCK)] * accel[t, 0, pl.ds(c, BLOCK)]
            for t in range(steps)
        )
        store_rows(slab_s, 0, i, total)

    for i in range(columns // BLOCK):
        correlate_late(HALO + i * BLOCK, i)
    to_owners(slab_s, stage_s, back_s, 0, 3)

    box_arrived(back_d, 2)
    to_all(back_d, gather_d, 1)
    wait_bytes(start_in.at[pl.ds(0, n_shot - 1)], shot_recv.at[4])
    load_starts = pltpu.make_async_copy(start_in, start_smem, load_sem.at[19])
    load_starts.start()
    for gathered in (gather_d, gather_s):
        for place in (0, spare + n_box):
            for s in range(n_shot):
                gathered[s, pl.ds(place, spare)] = jnp.zeros((spare, 1, 2, LANES), F32)
    load_starts.wait()

    wait_bytes(reduce_i.at[pl.ds(0, n_shot - 1)], shot_recv.at[0])
    light = reduce_i[0]
    for s in range(1, n_shot):
        light = light + reduce_i[s]
    scale[mine] = jnp.sqrt(light + damping)
    shot_exchange(lambda s: scale.at[mine], scale.at[mine], 2)

    box_arrived(back_s, 3)
    to_all(back_s, gather_s, 3)

    def total_of(gathered, sem):
        wait_bytes(gathered.at[pl.ds(0, n_shot - 1), filled], shot_recv.at[sem])
        return sum(
            gathered[s, pl.ds(spare - start_smem[s, 0, 0], rounds), 0] for s in range(n_shot)
        )

    deep_total = total_of(gather_d, 1)
    wait_bytes(scale.at[others], shot_recv.at[2])
    out[:, 0, :, half[1]] = deep_total / scale[:, 1]
    out[:, 0, :, half[0]] = total_of(gather_s, 3) / scale[:, 0]

    for group in range(6):
        halo_sent(group)
    box_sent(tile_out, 0)
    box_sent(stage_i, 1)
    box_sent(stage_d, 2)
    box_sent(stage_s, 3)
    wait_bytes(aligned_i.at[others], shot_send.at[0])
    wait_bytes(gather_d.at[pl.ds(0, n_shot - 1), filled], shot_send.at[1])
    wait_bytes(scale.at[others], shot_send.at[2])
    wait_bytes(gather_s.at[pl.ds(0, n_shot - 1), filled], shot_send.at[3])
    wait_bytes(start_in.at[pl.ds(0, n_shot - 1)], shot_send.at[4])


def on_device(
    n_box,
    n_shot,
    u_prev,
    u_now,
    born_prev,
    born_now,
    adj_after,
    adj_last,
    velocity,
    wavelet,
    sources,
    receivers,
    observed,
    first_tile,
    reflectivity,
):
    shots, columns, depth = u_now.shape[1:]
    steps = wavelet.shape[2]
    n_rec = receivers.shape[1]
    rounds = reflectivity.shape[0]
    ext = columns + 2 * HALO
    spare = rounds - n_box
    share = rounds // n_shot

    def vmem(*dims):
        return pltpu.VMEM(dims, F32)

    pitch = ext + HALO
    plane = (shots, LANES)
    tile = (2, LANES)
    scratch = [
        pltpu.SMEM(sources.shape, jnp.int32),
        pltpu.SMEM((1, steps, shots), F32),
        vmem(2, 2, shots, pitch, LANES),
        vmem(2, 2, shots, pitch, LANES),
        vmem(2, shots, pitch, LANES),
        vmem(2, ext, LANES),
        pltpu.VMEM((3, 1, n_rec), jnp.int32),
        vmem(3, shots, steps, n_rec),
        vmem(rounds + 2, *tile),
        vmem(steps + 1, 2, ext + 2, *plane),
        vmem(steps, 2, ext, *plane),
        vmem(steps + 1, ext + 2, *plane),
        vmem(steps + 2, 2, ext + 2, *plane),
        vmem(columns, *plane),
        vmem(steps, ext + 2, *plane),
        vmem(2, ext, *plane),
        vmem(ext, *plane),
        vmem(ext, *plane),
        vmem(steps, ext // 2, *plane),
        vmem(3, steps, shots, n_rec),
        vmem(steps - 1, ext + 2, *plane),
        vmem(n_box, 2, *tile),
        vmem(n_box, 2, *tile),
        vmem(2 * n_box, 2, *tile),
        vmem(2 * n_box, 1, *tile),
        vmem(2 * n_box, 1, *tile),
        vmem(n_box, 2, *tile),
        vmem(n_box, 1, *tile),
        vmem(n_box, 1, *tile),
        vmem(n_box + 2 * spare, 2, *tile),
        vmem(n_box, 1, *tile),
        vmem(n_box, 1, *tile),
        vmem(rounds, 2, *tile),
        vmem(n_shot, share, 2, *tile),
        vmem(n_shot, n_box + 2 * spare, 1, *tile),
        vmem(n_shot, n_box + 2 * spare, 1, *tile),
        vmem(rounds, 2, *tile),
        pltpu.VMEM((1, LANES), jnp.int32),
        pltpu.VMEM((n_shot, 1, LANES), jnp.int32),
        pltpu.SMEM((n_shot, 1, LANES), jnp.int32),
        pltpu.SemaphoreType.DMA((20,)),
        pltpu.SemaphoreType.DMA((2, 6)),
        pltpu.SemaphoreType.DMA((2, 6)),
        pltpu.SemaphoreType.DMA((4,)),
        pltpu.SemaphoreType.DMA((4,)),
        pltpu.SemaphoreType.DMA((5,)),
        pltpu.SemaphoreType.DMA((5,)),
    ]
    hbm = pl.BlockSpec(memory_space=pltpu.HBM)
    return pl.pallas_call(
        functools.partial(kernel, n_box, n_shot),
        out_shape=jax.ShapeDtypeStruct(reflectivity.shape, F32),
        in_specs=[pl.BlockSpec(memory_space=pltpu.SMEM)] + [hbm] * 12,
        out_specs=pl.BlockSpec(memory_space=pltpu.VMEM),
        scratch_shapes=scratch,
        compiler_params=pltpu.CompilerParams(
            collective_id=0, has_side_effects=True, vmem_limit_bytes=60 * 1024 * 1024
        ),
    )(
        first_tile,
        sources,
        jnp.transpose(wavelet, (0, 2, 1)),
        u_prev,
        u_now,
        born_prev,
        born_now,
        adj_after,
        adj_last,
        velocity,
        receivers,
        observed,
        reflectivity,
    )


def solution(mesh):
    return jax.shard_map(
        functools.partial(on_device, mesh.shape["box"], mesh.shape["shot"]),
        mesh=mesh,
        in_specs=(
            P("shot", None, "box", None),
            P("shot", None, "box", None),
            P("shot", None, "box", None),
            P("shot", None, "box", None),
            P("shot", None, "box", None),
            P("shot", None, "box", None),
            P("shot", "box", None),
            P("shot", None, None),
            P("shot", None),
            P("shot", "box"),
            P("shot", None, None, "box"),
            P("shot"),
            P(None, "box", None, None),
        ),
        out_specs=P(None, "box", None, None),
        check_vma=False,
    )
```
